128 devices in a mesh: dp: 16 (over y, x), seq: 8 (over z, core).
Axes of the slice: x: 4, y: 4, z: 4, core: 2. Of those that a mesh axis runs over, the one named last changes fastest.
Arguments:
- feats: bfloat16 [65536, 1024], P(('dp', 'seq')), may hold values from -6 to 6
- gain: float32 [1024], replicated, may hold values from 0.1 to 1.9
- w_qkv: bfloat16 [1024, 3072], replicated, as said below
- w_out: bfloat16 [1024, 1024], replicated, may hold values from -3 to 3
- block_cols: int32 [16, 32, 8], P('dp'), may hold values from 0 to 31, as said below
- block_counts: int32 [16, 32], P('dp'), may hold values from 1 to 8, 128 in all within a row
- cotan: bfloat16 [65536, 1024], P(('dp', 'seq')), may hold values from -0.3984375 to 0.3984375
Outputs:
- result: bfloat16 [65536, 1024], P(('dp', 'seq'))
- grad_feats: bfloat16 [65536, 1024], P(('dp', 'seq'))
- grad_qkv: bfloat16 [1024, 3072], P('seq')
- grad_out: bfloat16 [1024, 1024], P('seq')
The draws below stay inside these ranges and needn't reach their ends.
Inputs may be any that keep to these rules, and one draw needn't show every extreme that they name: `block_cols`: for every batch and row block r, the 8 listed column blocks are distinct and the first is r itself. `block_counts`: each batch's counts sum to 128. `w_qkv`: entries lie within 70 / sqrt(1024) in magnitude.
All inputs are finite; a program needn't handle non-finite values.
Results may differ from the reference program's by a relative error of at most 0.014.
Values may be sent and summed in bfloat16 or wider, within the bound.
A program may use at most 128 MiB of HBM per device.

```python
import math
import jax
import jax.numpy as jnp
import numpy as np
from jax import lax

D = 1024
H = 16
HD = 64
BLK = 128
MAXB = 8
NODES = 4096
NB = 32
LIVE = 128
GROUPS = 16
TOTAL = 65536


def draw_block_cols(key, part):
    noise = jax.random.randint(key, (GROUPS, NB, NB), 0, 4 * NB)
    rows_at = jnp.arange(NB, dtype=jnp.int32)[:, None]
    cols_at = jnp.arange(NB, dtype=jnp.int32)[None, :]
    apart = jnp.abs(rows_at - cols_at)
    apart = jnp.minimum(apart, NB - apart)
    ranked = (noise - 3 * apart + jnp.where(apart == 0, 100 * NB, 0)) * NB + cols_at
    picked = lax.top_k(ranked, MAXB)[1]
    return picked.astype(jnp.int32)


def draw_w_qkv(key, part):
    base_scale = D ** (-0.5)
    return (jax.random.truncated_normal(key, -6.0, 6.0, (D, 3 * D), jnp.float32) * base_scale).astype(jnp.bfloat16)


def level_of(rng, shape, cuts, low, top_value):
    def one(axis_at, shards_of):
        heights = jax.random.uniform(jax.random.fold_in(jax.random.fold_in(rng, 6), axis_at), (shards_of,), jnp.float32, low / len(cuts), top_value / len(cuts))
        return jnp.repeat(jnp.exp(heights), shape[axis_at] // shards_of).reshape((-1,) + (1,) * (len(shape) - axis_at - 1))

    factor_of = one(*cuts[0])
    for cut in cuts[1:]:
        factor_of = factor_of * one(*cut)
    return factor_of


def profile(count, total, most, lean):
    loads = [(1 << 20) // math.isqrt(grade ** lean) + 1 for grade in range(2, count + 1)]
    rest, given = total - most - (count - 1), [1] * (count - 1)
    while rest > 0:
        candidates = [i for i in range(count - 1) if given[i] < most]
        pool, budget = sum([loads[i] for i in candidates]), rest
        for i in candidates:
            extra = min(most - given[i], max(1, budget * loads[i] // pool), rest)
            given[i] = given[i] + extra
            rest = rest - extra
    return np.array([most] + given)


def ragged(rng, number_of, total, bound, lean):
    if number_of == 2:
        one = jax.random.randint(rng, (), max(1, total - bound), min(bound, total - 1) + 1)
        return jnp.stack([one, total - one])
    lengths = jnp.asarray(profile(number_of, total, bound, lean), jnp.int32)
    twos = (number_of - 1) // 2
    giver, taker = lengths[1:1 + 2 * twos:2], lengths[2:2 + 2 * twos:2]
    margin = jnp.minimum(giver - 1, bound - taker)
    moved = jax.random.randint(jax.random.fold_in(rng, 1), (twos,), 0, 1 << 20) % (margin + 1)
    lengths = lengths.at[1:1 + 2 * twos:2].set(giver - moved).at[2:2 + 2 * twos:2].set(taker + moved)
    return lengths[jax.random.permutation(jax.random.fold_in(rng, 2), number_of)]


def scatter_about(key, shape, scale, limit, split=(), kind=jnp.bfloat16):
    entries = jax.random.normal(key, shape, jnp.float32) * scale
    if len(split) > 0:
        entries = level_of(key, shape, split, -0.22, 0.18) * entries
    return jnp.clip(entries, min=-limit, max=limit).astype(kind)


def setup_inputs(seed: int = 0) -> dict:
    streams_of = jax.random.split(jax.random.key(seed), 8)
    feats = scatter_about(streams_of[0], (TOTAL, D), 1.0, 6.0, ((0, 128),))
    gain = jnp.clip(1.0 + 0.18 * jax.random.normal(streams_of[1], (D,), jnp.float32), 0.1, 1.9)
    w_qkv = draw_w_qkv(jax.random.fold_in(streams_of[7], 71), 0)
    w_out = scatter_about(streams_of[3], (D, D), 4 ** -0.5, 3.0)
    block_cols = draw_block_cols(jax.random.fold_in(streams_of[7], 71), 0)
    block_counts = jax.vmap(lambda own: ragged(own, NB, LIVE, MAXB, 2))(jax.random.split(streams_of[5], GROUPS)).reshape((GROUPS, NB)).astype(jnp.int32)
    cotan = scatter_about(streams_of[6], (TOTAL, D), 0.0625, 0.3984375, ((0, 128),))
    return {"feats": feats, "gain": gain, "w_qkv": w_qkv, "w_out": w_out, "block_cols": block_cols, "block_counts": block_counts, "cotan": cotan}


EPSILON = 1e-05

def layer_norm(feats, gain):
    values_f = feats.astype(jnp.float32)
    centred = values_f - lax.optimization_barrier(jnp.mean(values_f, axis=1, keepdims=True))
    inverse = lax.rsqrt(lax.optimization_barrier(jnp.mean(centred * centred, axis=1, keepdims=True)) + EPSILON)
    scaled = centred * inverse
    return (scaled, inverse, (scaled * gain[None, :]).astype(jnp.bfloat16))

def live_slots(counts):
    return jnp.arange(MAXB, dtype=jnp.int32)[None, :] < counts[:, None]

def forward_blocks(query_heads, key_heads, value_heads, col_blocks, counts, head_count):
    per_step = 4
    block_total = query_heads.shape[0] // BLK
    steps_count = block_total // per_step
    query_b = query_heads.reshape(steps_count, per_step, BLK, head_count, HD)
    key_b = key_heads.reshape(block_total, BLK, head_count, HD)
    value_b = value_heads.reshape(block_total, BLK, head_count, HD)
    col_steps = col_blocks.reshape(steps_count, per_step, MAXB)
    count_steps = counts.reshape(steps_count, per_step)
    score_scale = HD ** (-0.5)

    def block_step(inputs):
        query_g, col_g, count_g = inputs
        key_g = key_b[col_g]
        value_g = value_b[col_g]
        scores = jnp.einsum('gqhd,gskhd->ghqsk', query_g.astype(jnp.float32), key_g.astype(jnp.float32)) * score_scale
        live_mask = live_slots(count_g)[:, None, None, :, None]
        row_max = lax.optimization_barrier(jnp.max(jnp.where(live_mask, scores, -jnp.inf), axis=(3, 4), keepdims=True))
        row_total = lax.optimization_barrier(jnp.sum(jnp.where(live_mask, jnp.exp(scores - row_max), 0.0), axis=(3, 4), keepdims=True))
        log_total = row_max + jnp.log(row_total)
        probabilities = jnp.where(live_mask, jnp.exp(scores - log_total), 0.0).astype(jnp.bfloat16)
        attended = jnp.einsum('ghqsk,gskhd->gqhd', probabilities.astype(jnp.float32), value_g.astype(jnp.float32))
        return (attended.astype(jnp.bfloat16), log_total[:, :, :, 0, 0])
    attended, log_total = lax.map(block_step, (query_b, col_steps, count_steps))
    return (attended.reshape(query_heads.shape), log_total)

def backward_blocks(query_heads, key_heads, value_heads, attended_heads, grad_heads, log_total, col_blocks, counts, head_count):
    per_step = 4
    block_total = query_heads.shape[0] // BLK
    steps_count = block_total // per_step
    query_b = query_heads.reshape(steps_count, per_step, BLK, head_count, HD)
    grad_b = grad_heads.reshape(steps_count, per_step, BLK, head_count, HD)
    attended_b = attended_heads.reshape(steps_count, per_step, BLK, head_count, HD)
    key_b = key_heads.reshape(block_total, BLK, head_count, HD)
    value_b = value_heads.reshape(block_total, BLK, head_count, HD)
    col_steps = col_blocks.reshape(steps_count, per_step, MAXB)
    count_steps = counts.reshape(steps_count, per_step)
    delta_all = lax.optimization_barrier(jnp.sum(attended_b.astype(jnp.float32) * grad_b.astype(jnp.float32), axis=4))
    block_range = jnp.arange(block_total, dtype=jnp.int32)
    score_scale = HD ** (-0.5)

    def block_step(carry, inputs):
        key_sum, value_sum = carry
        query_g, grad_g, delta_g, log_g, col_g, count_g = inputs
        key_g = key_b[col_g].astype(jnp.float32)
        value_g = value_b[col_g].astype(jnp.float32)
        query_f = query_g.astype(jnp.float32)
        grad_f = grad_g.astype(jnp.float32)
        scores = jnp.einsum('gqhd,gskhd->ghqsk', query_f, key_g) * score_scale
        live_mask = live_slots(count_g)[:, None, None, :, None]
        probabilities = jnp.where(live_mask, jnp.exp(scores - log_g[:, :, :, None, None]), 0.0).astype(jnp.bfloat16)
        prob_f = probabilities.astype(jnp.float32)
        prob_grad = jnp.einsum('gqhd,gskhd->ghqsk', grad_f, value_g)
        delta_t = jnp.transpose(delta_g, (0, 2, 1))[:, :, :, None, None]
        score_grad = (prob_f * (prob_grad - delta_t) * score_scale).astype(jnp.bfloat16).astype(jnp.float32)
        query_grad = jnp.einsum('ghqsk,gskhd->gqhd', score_grad, key_g).astype(jnp.bfloat16)
        key_pairs = jnp.einsum('ghqsk,gqhd->gskhd', score_grad, query_f)
        value_pairs = jnp.einsum('ghqsk,gqhd->gskhd', prob_f, grad_f)
        selector = (col_g[:, :, None] == block_range[None, None, :]).astype(jnp.float32)
        key_sum = key_sum + jnp.einsum('gsc,gskhd->ckhd', selector, key_pairs, precision=lax.Precision.HIGHEST)
        value_sum = value_sum + jnp.einsum('gsc,gskhd->ckhd', selector, value_pairs, precision=lax.Precision.HIGHEST)
        return ((key_sum, value_sum), query_grad)
    zeros_f = jnp.zeros((block_total, BLK, head_count, HD), jnp.float32)
    (key_sum, value_sum), query_grad = lax.scan(block_step, (zeros_f, zeros_f), (query_b, grad_b, delta_all, log_total, col_steps, count_steps))
    shape = query_heads.shape
    return (query_grad.reshape(shape), key_sum.reshape(shape).astype(jnp.bfloat16), value_sum.reshape(shape).astype(jnp.bfloat16))

def one_group(feats, cotan, col_blocks, counts, gain, w_qkv, w_out):
    scaled, inverse, normed = layer_norm(feats, gain)
    mixed_proj = jnp.dot(normed, w_qkv, preferred_element_type=jnp.float32).astype(jnp.bfloat16)
    query_rows = mixed_proj[:, :D]
    key_rows = mixed_proj[:, D:2 * D]
    value_rows = mixed_proj[:, 2 * D:]
    attended, log_total = forward_blocks(query_rows, key_rows, value_rows, col_blocks, counts, H)
    result = (feats.astype(jnp.float32) + jnp.dot(attended, w_out, preferred_element_type=jnp.float32)).astype(jnp.bfloat16)
    grad_att = lax.dot_general(cotan, w_out, (((1,), (1,)), ((), ())), preferred_element_type=jnp.float32).astype(jnp.bfloat16)
    query_grad, key_grad, value_grad = backward_blocks(query_rows, key_rows, value_rows, attended, grad_att, log_total, col_blocks, counts, H)
    grad_mixed = jnp.concatenate([query_grad, key_grad, value_grad], axis=1)
    grad_normed = lax.dot_general(grad_mixed, w_qkv, (((1,), (1,)), ((), ())), preferred_element_type=jnp.float32)
    gained = grad_normed * gain[None, :]
    mean_one = lax.optimization_barrier(jnp.mean(gained, axis=1, keepdims=True))
    mean_two = lax.optimization_barrier(jnp.mean(gained * scaled, axis=1, keepdims=True))
    grad_feats = (cotan.astype(jnp.float32) + inverse * (gained - mean_one - scaled * mean_two)).astype(jnp.bfloat16)
    term_qkv = lax.dot_general(normed, grad_mixed, (((0,), (0,)), ((), ())), preferred_element_type=jnp.float32)
    term_out = lax.dot_general(attended, cotan, (((0,), (0,)), ((), ())), preferred_element_type=jnp.float32)
    return (result, grad_feats, term_qkv, term_out)

def reference(feats, gain, w_qkv, w_out, block_cols, block_counts, cotan):
    feats_g = feats.reshape(GROUPS, NODES, D)
    cotan_g = cotan.reshape(GROUPS, NODES, D)

    def group_step(carry, inputs):
        qkv_sum, out_sum = carry
        result, grad_feats, term_qkv, term_out = one_group(inputs[0], inputs[1], inputs[2], inputs[3], gain, w_qkv, w_out)
        return ((qkv_sum + term_qkv, out_sum + term_out), (result, grad_feats))
    start_qkv = jnp.zeros((D, 3 * D), jnp.float32)
    start_out = jnp.zeros((D, D), jnp.float32)
    (qkv_sum, out_sum), (results, grads) = lax.scan(group_step, (start_qkv, start_out), (feats_g, cotan_g, block_cols, block_counts))
    return (results.reshape(TOTAL, D), grads.reshape(TOTAL, D), qkv_sum.astype(jnp.bfloat16), out_sum.astype(jnp.bfloat16))
```

```python
import functools

import jax
import jax.numpy as jnp
from jax import lax
from jax.experimental import pallas as pl
from jax.experimental.pallas import tpu as pltpu
from jax.sharding import PartitionSpec as P

HD = 64
BLK = 128
MAXB = 8
SCALE = HD ** (-0.5)
NEG = -1e30

EPSILON = 1e-05


def layer_norm(feats, gain):
    values_f = feats.astype(jnp.float32)
    centred = values_f - jnp.mean(values_f, axis=1, keepdims=True)
    inverse = lax.rsqrt(jnp.mean(centred * centred, axis=1, keepdims=True) + EPSILON)
    scaled = centred * inverse
    return (scaled, inverse, (scaled * gain[None, :]).astype(jnp.bfloat16))


def contract_rows(left_cols, right_cols):
    return lax.dot_general(
        left_cols, right_cols, (((0,), (0,)), ((), ())), preferred_element_type=jnp.float32
    )


def head_masks(width):
    lane = lax.broadcasted_iota(jnp.int32, (1, width), 1)
    return [(lane >= h * HD) & (lane < (h + 1) * HD) for h in range(width // HD)]


def stack_heads(x, masks):
    return jnp.concatenate([jnp.where(m, x, jnp.zeros_like(x)) for m in masks], axis=0)


def unstack_heads(y, masks):
    out = y[0:BLK]
    for h in range(1, len(masks)):
        out = jnp.where(masks[h], y[h * BLK : (h + 1) * BLK], out)
    return out


def nt_dot(a, b):
    return lax.dot_general(a, b, (((1,), (1,)), ((), ())), preferred_element_type=jnp.float32)


def tn_dot(a, b):
    return lax.dot_general(a, b, (((0,), (0,)), ((), ())), preferred_element_type=jnp.float32)


def attn_fwd_kernel(cols_ref, counts_ref, q_ref, k_ref, v_ref, o_ref, lse_ref):
    width = q_ref.shape[1]
    nblk = q_ref.shape[0] // BLK
    masks = head_masks(width)
    rows = len(masks) * BLK

    def row_body(r, carry):
        row0 = pl.multiple_of(r * BLK, BLK)
        cnt = counts_ref[r]
        q2 = stack_heads(q_ref[pl.ds(row0, BLK), :], masks)

        def scores(s):
            col0 = pl.multiple_of(cols_ref[r * MAXB + s] * BLK, BLK)
            return nt_dot(q2, k_ref[pl.ds(col0, BLK), :]) * SCALE, col0

        def first(s, mc):
            m, l = mc
            sc, _ = scores(s)
            m_new = jnp.maximum(m, jnp.max(sc, axis=1, keepdims=True))
            l = l * jnp.exp(m - m_new) + jnp.sum(jnp.exp(sc - m_new), axis=1, keepdims=True)
            return m_new, l

        m, l = lax.fori_loop(
            0,
            cnt,
            first,
            (jnp.full((rows, 1), NEG, jnp.float32), jnp.zeros((rows, 1), jnp.float32)),
        )
        lse = m + jnp.log(l)

        def second(s, acc):
            sc, col0 = scores(s)
            p = jnp.exp(sc - lse).astype(jnp.bfloat16)
            return acc + jnp.dot(p, v_ref[pl.ds(col0, BLK), :], preferred_element_type=jnp.float32)

        acc = lax.fori_loop(0, cnt, second, jnp.zeros((rows, width), jnp.float32))
        o_ref[pl.ds(row0, BLK), :] = unstack_heads(acc, masks).astype(o_ref.dtype)
        lse_ref[pl.ds(pl.multiple_of(r * rows, rows), rows), :] = jnp.broadcast_to(
            lse, (rows, lse_ref.shape[1])
        )
        return carry

    lax.fori_loop(0, nblk, row_body, 0)


def attn_bwd_kernel(
    cols_ref, counts_ref, q_ref, k_ref, v_ref, o_ref, do_ref, lse_ref, dq_ref, dk_ref, dv_ref, dk_acc, dv_acc
):
    width = q_ref.shape[1]
    nblk = q_ref.shape[0] // BLK
    masks = head_masks(width)
    rows = len(masks) * BLK
    dk_acc[...] = jnp.zeros_like(dk_acc)
    dv_acc[...] = jnp.zeros_like(dv_acc)

    def row_body(r, carry):
        row0 = pl.multiple_of(r * BLK, BLK)
        cnt = counts_ref[r]
        q2 = stack_heads(q_ref[pl.ds(row0, BLK), :], masks)
        do_blk = do_ref[pl.ds(row0, BLK), :]
        do2 = stack_heads(do_blk, masks)
        prod = o_ref[pl.ds(row0, BLK), :].astype(jnp.float32) * do_blk.astype(jnp.float32)
        delta = jnp.concatenate(
            [jnp.sum(jnp.where(m, prod, 0.0), axis=1, keepdims=True) for m in masks], axis=0
        )
        lse = lse_ref[pl.ds(pl.multiple_of(r * rows, rows), rows), :]

        def step(s, dq):
            col0 = pl.multiple_of(cols_ref[r * MAXB + s] * BLK, BLK)
            kb = k_ref[pl.ds(col0, BLK), :]
            vb = v_ref[pl.ds(col0, BLK), :]
            sc = nt_dot(q2, kb) * SCALE
            p = jnp.exp(sc - lse).astype(jnp.bfloat16)
            dp = nt_dot(do2, vb)
            ds = (p.astype(jnp.float32) * (dp - delta) * SCALE).astype(jnp.bfloat16)
            dk_acc[pl.ds(col0, BLK), :] += tn_dot(ds, q2)
            dv_acc[pl.ds(col0, BLK), :] += tn_dot(p, do2)
            return dq + jnp.dot(ds, kb, preferred_element_type=jnp.float32)

        dq = lax.fori_loop(0, cnt, step, jnp.zeros((rows, width), jnp.float32))
        dq_ref[pl.ds(row0, BLK), :] = unstack_heads(dq, masks).astype(dq_ref.dtype)
        return carry

    lax.fori_loop(0, nblk, row_body, 0)
    dk_ref[...] = dk_acc[...].astype(dk_ref.dtype)
    dv_ref[...] = dv_acc[...].astype(dv_ref.dtype)


def smem_spec():
    return pl.BlockSpec(memory_space=pltpu.SMEM)


def vmem_spec():
    return pl.BlockSpec(memory_space=pltpu.VMEM)


VMEM_LIMIT = 48 * 1024 * 1024


def attention_forward(q, k, v, cols, counts):
    n, width = q.shape
    rows = (width // HD) * BLK
    return pl.pallas_call(
        attn_fwd_kernel,
        out_shape=(
            jax.ShapeDtypeStruct((n, width), jnp.bfloat16),
            jax.ShapeDtypeStruct(((n // BLK) * rows, 128), jnp.float32),
        ),
        in_specs=[smem_spec(), smem_spec(), vmem_spec(), vmem_spec(), vmem_spec()],
        out_specs=(vmem_spec(), vmem_spec()),
        compiler_params=pltpu.CompilerParams(vmem_limit_bytes=VMEM_LIMIT),
    )(cols, counts, q, k, v)


def attention_backward(q, k, v, o, do, lse, cols, counts):
    n, width = q.shape
    return pl.pallas_call(
        attn_bwd_kernel,
        out_shape=tuple(jax.ShapeDtypeStruct((n, width), jnp.bfloat16) for _ in range(3)),
        in_specs=[smem_spec(), smem_spec()] + [vmem_spec()] * 6,
        out_specs=(vmem_spec(), vmem_spec(), vmem_spec()),
        scratch_shapes=[pltpu.VMEM((n, width), jnp.float32), pltpu.VMEM((n, width), jnp.float32)],
        compiler_params=pltpu.CompilerParams(vmem_limit_bytes=VMEM_LIMIT),
    )(cols, counts, q, k, v, o, do, lse)


def body(feats, gain, w_qkv, w_out, block_cols, block_counts, cotan):
    model_width = feats.shape[1]
    qkv_width = 3 * model_width
    scaled, inverse, normed = layer_norm(feats, gain)
    mixed_proj = jnp.dot(normed, w_qkv, preferred_element_type=jnp.float32).astype(jnp.bfloat16)
    query_rows = mixed_proj[:, :model_width]
    key_rows = mixed_proj[:, model_width : 2 * model_width]
    value_rows = mixed_proj[:, 2 * model_width :]
    query_heads, key_heads, value_heads = (
        lax.all_to_all(query_rows, "seq", split_axis=1, concat_axis=0, tiled=True),
        lax.all_to_all(key_rows, "seq", split_axis=1, concat_axis=0, tiled=True),
        lax.all_to_all(value_rows, "seq", split_axis=1, concat_axis=0, tiled=True),
    )
    cols = block_cols[0].reshape(-1)
    counts = block_counts[0]
    attended_heads, lse = attention_forward(query_heads, key_heads, value_heads, cols, counts)
    attended = lax.all_to_all(attended_heads, "seq", split_axis=0, concat_axis=1, tiled=True)
    result = (
        feats.astype(jnp.float32) + jnp.dot(attended, w_out, preferred_element_type=jnp.float32)
    ).astype(jnp.bfloat16)
    grad_att = lax.dot_general(
        cotan, w_out, (((1,), (1,)), ((), ())), preferred_element_type=jnp.float32
    ).astype(jnp.bfloat16)
    grad_heads = lax.all_to_all(grad_att, "seq", split_axis=1, concat_axis=0, tiled=True)
    query_grad, key_grad, value_grad = attention_backward(
        query_heads, key_heads, value_heads, attended_heads, grad_heads, lse, cols, counts
    )
    query_back, key_back, value_back = (
        lax.all_to_all(query_grad, "seq", split_axis=0, concat_axis=1, tiled=True),
        lax.all_to_all(key_grad, "seq", split_axis=0, concat_axis=1, tiled=True),
        lax.all_to_all(value_grad, "seq", split_axis=0, concat_axis=1, tiled=True),
    )
    grad_mixed = jnp.concatenate([query_back, key_back, value_back], axis=1)
    grad_normed = lax.dot_general(
        grad_mixed, w_qkv, (((1,), (1,)), ((), ())), preferred_element_type=jnp.float32
    )
    gained = grad_normed * gain[None, :]
    mean_one = jnp.mean(gained, axis=1, keepdims=True)
    mean_two = jnp.mean(gained * scaled, axis=1, keepdims=True)
    grad_feats = (
        cotan.astype(jnp.float32) + inverse * (gained - mean_one - scaled * mean_two)
    ).astype(jnp.bfloat16)
    terms = jnp.concatenate(
        [contract_rows(normed, grad_mixed), contract_rows(attended, cotan)], axis=1
    )
    own_rows = lax.psum(lax.psum_scatter(terms, "seq", scatter_dimension=0, tiled=True), "dp")
    grad_qkv = own_rows[:, :qkv_width].astype(jnp.bfloat16)
    grad_out = own_rows[:, qkv_width:].astype(jnp.bfloat16)
    return (result, grad_feats, grad_qkv, grad_out)


def solution(mesh):
    in_specs = (
        P(("dp", "seq"), None),
        P(),
        P(),
        P(),
        P("dp", None, None),
        P("dp", None),
        P(("dp", "seq"), None),
    )
    out_specs = (P(("dp", "seq"), None), P(("dp", "seq"), None), P("seq", None), P("seq", None))
    return jax.shard_map(body, mesh=mesh, in_specs=in_specs, out_specs=out_specs, check_vma=False)
```

```python
import functools

import jax
import jax.numpy as jnp
from jax import lax
from jax.experimental import pallas as pl
from jax.experimental.pallas import tpu as pltpu
from jax.sharding import PartitionSpec as P

HD = 64
BLK = 128
MAXB = 8
SCALE = HD ** (-0.5)
NEG = -1e30

EPSILON = 1e-05


def layer_norm(feats, gain):
    values_f = feats.astype(jnp.float32)
    centred = values_f - jnp.mean(values_f, axis=1, keepdims=True)
    inverse = lax.rsqrt(jnp.mean(centred * centred, axis=1, keepdims=True) + EPSILON)
    scaled = centred * inverse
    return (scaled, inverse, (scaled * gain[None, :]).astype(jnp.bfloat16))


def contract_rows(left_cols, right_cols):
    return lax.dot_general(
        left_cols, right_cols, (((0,), (0,)), ((), ())), preferred_element_type=jnp.float32
    )


def head_masks(width):
    lane = lax.broadcasted_iota(jnp.int32, (1, width), 1)
    return [(lane >= h * HD) & (lane < (h + 1) * HD) for h in range(width // HD)]


def stack_heads(x, masks):
    return jnp.concatenate([jnp.where(m, x, jnp.zeros_like(x)) for m in masks], axis=0)


def unstack_heads(y, masks):
    out = y[0:BLK]
    for h in range(1, len(masks)):
        out = jnp.where(masks[h], y[h * BLK : (h + 1) * BLK], out)
    return out


def nt_dot(a, b):
    return lax.dot_general(a, b, (((1,), (1,)), ((), ())), preferred_element_type=jnp.float32)


def tn_dot(a, b):
    return lax.dot_general(a, b, (((0,), (0,)), ((), ())), preferred_element_type=jnp.float32)


def gather_blocks(ref, cols_ref, r):
    return jnp.concatenate(
        [
            ref[pl.ds(pl.multiple_of(cols_ref[r * MAXB + s] * BLK, BLK), BLK), :]
            for s in range(MAXB)
        ],
        axis=0,
    )


def live_lanes(cnt):
    return lax.broadcasted_iota(jnp.int32, (1, MAXB * BLK), 1) < cnt * BLK


def attn_fwd_kernel(cols_ref, counts_ref, q_ref, k_ref, v_ref, o_ref, lse_ref):
    width = q_ref.shape[1]
    nblk = q_ref.shape[0] // BLK
    masks = head_masks(width)
    rows = len(masks) * BLK

    def row_body(r, carry):
        row0 = pl.multiple_of(r * BLK, BLK)
        live = live_lanes(counts_ref[r])
        q2 = stack_heads(q_ref[pl.ds(row0, BLK), :], masks)
        sc = jnp.where(live, nt_dot(q2, gather_blocks(k_ref, cols_ref, r)) * SCALE, NEG)
        m = jnp.max(sc, axis=1, keepdims=True)
        e = jnp.where(live, jnp.exp(sc - m), 0.0)
        l = jnp.sum(e, axis=1, keepdims=True)
        p = (e * (1.0 / l)).astype(jnp.bfloat16)
        acc = jnp.dot(p, gather_blocks(v_ref, cols_ref, r), preferred_element_type=jnp.float32)
        o_ref[pl.ds(row0, BLK), :] = unstack_heads(acc, masks).astype(o_ref.dtype)
        lse_ref[pl.ds(pl.multiple_of(r * rows, rows), rows), :] = jnp.broadcast_to(
            m + jnp.log(l), (rows, lse_ref.shape[1])
        )
        return carry

    lax.fori_loop(0, nblk, row_body, 0)


def attn_bwd_kernel(
    cols_ref, counts_ref, q_ref, k_ref, v_ref, o_ref, do_ref, lse_ref, dq_ref, dk_ref, dv_ref, dk_acc, dv_acc
):
    width = q_ref.shape[1]
    nblk = q_ref.shape[0] // BLK
    masks = head_masks(width)
    rows = len(masks) * BLK
    dk_acc[...] = jnp.zeros_like(dk_acc)
    dv_acc[...] = jnp.zeros_like(dv_acc)

    def row_body(r, carry):
        row0 = pl.multiple_of(r * BLK, BLK)
        cnt = counts_ref[r]
        live = live_lanes(cnt)
        q2 = stack_heads(q_ref[pl.ds(row0, BLK), :], masks)
        do_blk = do_ref[pl.ds(row0, BLK), :]
        do2 = stack_heads(do_blk, masks)
        prod = o_ref[pl.ds(row0, BLK), :].astype(jnp.float32) * do_blk.astype(jnp.float32)
        delta = jnp.concatenate(
            [jnp.sum(jnp.where(m, prod, 0.0), axis=1, keepdims=True) for m in masks], axis=0
        )
        lse = lse_ref[pl.ds(pl.multiple_of(r * rows, rows), rows), :][:, 0:1]
        kc = gather_blocks(k_ref, cols_ref, r)
        vc = gather_blocks(v_ref, cols_ref, r)
        sc = nt_dot(q2, kc) * SCALE
        p = jnp.where(live, jnp.exp(sc - lse), 0.0).astype(jnp.bfloat16)
        dp = nt_dot(do2, vc)
        ds = (p.astype(jnp.float32) * (dp - delta) * SCALE).astype(jnp.bfloat16)
        dq = jnp.dot(ds, kc, preferred_element_type=jnp.float32)
        dq_ref[pl.ds(row0, BLK), :] = unstack_heads(dq, masks).astype(dq_ref.dtype)
        dkc = tn_dot(ds, q2)
        dvc = tn_dot(p, do2)
        for s in range(MAXB):

            @pl.when(s < cnt)
            def _():
                col0 = pl.multiple_of(cols_ref[r * MAXB + s] * BLK, BLK)
                dk_acc[pl.ds(col0, BLK), :] += dkc[s * BLK : (s + 1) * BLK]
                dv_acc[pl.ds(col0, BLK), :] += dvc[s * BLK : (s + 1) * BLK]

        return carry

    lax.fori_loop(0, nblk, row_body, 0)
    dk_ref[...] = dk_acc[...].astype(dk_ref.dtype)
    dv_ref[...] = dv_acc[...].astype(dv_ref.dtype)


def smem_spec():
    return pl.BlockSpec(memory_space=pltpu.SMEM)


def vmem_spec():
    return pl.BlockSpec(memory_space=pltpu.VMEM)


VMEM_LIMIT = 48 * 1024 * 1024


def attention_forward(q, k, v, cols, counts):
    n, width = q.shape
    rows = (width // HD) * BLK
    return pl.pallas_call(
        attn_fwd_kernel,
        out_shape=(
            jax.ShapeDtypeStruct((n, width), jnp.bfloat16),
            jax.ShapeDtypeStruct(((n // BLK) * rows, 128), jnp.float32),
        ),
        in_specs=[smem_spec(), smem_spec(), vmem_spec(), vmem_spec(), vmem_spec()],
        out_specs=(vmem_spec(), vmem_spec()),
        compiler_params=pltpu.CompilerParams(vmem_limit_bytes=VMEM_LIMIT),
    )(cols, counts, q, k, v)


def attention_backward(q, k, v, o, do, lse, cols, counts):
    n, width = q.shape
    return pl.pallas_call(
        attn_bwd_kernel,
        out_shape=tuple(jax.ShapeDtypeStruct((n, width), jnp.bfloat16) for _ in range(3)),
        in_specs=[smem_spec(), smem_spec()] + [vmem_spec()] * 6,
        out_specs=(vmem_spec(), vmem_spec(), vmem_spec()),
        scratch_shapes=[pltpu.VMEM((n, width), jnp.float32), pltpu.VMEM((n, width), jnp.float32)],
        compiler_params=pltpu.CompilerParams(vmem_limit_bytes=VMEM_LIMIT),
    )(cols, counts, q, k, v, o, do, lse)


def body(feats, gain, w_qkv, w_out, block_cols, block_counts, cotan):
    model_width = feats.shape[1]
    qkv_width = 3 * model_width
    scaled, inverse, normed = layer_norm(feats, gain)
    mixed_proj = jnp.dot(normed, w_qkv, preferred_element_type=jnp.float32).astype(jnp.bfloat16)
    query_rows = mixed_proj[:, :model_width]
    key_rows = mixed_proj[:, model_width : 2 * model_width]
    value_rows = mixed_proj[:, 2 * model_width :]
    query_heads, key_heads, value_heads = (
        lax.all_to_all(query_rows, "seq", split_axis=1, concat_axis=0, tiled=True),
        lax.all_to_all(key_rows, "seq", split_axis=1, concat_axis=0, tiled=True),
        lax.all_to_all(value_rows, "seq", split_axis=1, concat_axis=0, tiled=True),
    )
    cols = block_cols[0].reshape(-1)
    counts = block_counts[0]
    attended_heads, lse = attention_forward(query_heads, key_heads, value_heads, cols, counts)
    attended = lax.all_to_all(attended_heads, "seq", split_axis=0, concat_axis=1, tiled=True)
    result = (
        feats.astype(jnp.float32) + jnp.dot(attended, w_out, preferred_element_type=jnp.float32)
    ).astype(jnp.bfloat16)
    grad_att = lax.dot_general(
        cotan, w_out, (((1,), (1,)), ((), ())), preferred_element_type=jnp.float32
    ).astype(jnp.bfloat16)
    grad_heads = lax.all_to_all(grad_att, "seq", split_axis=1, concat_axis=0, tiled=True)
    query_grad, key_grad, value_grad = attention_backward(
        query_heads, key_heads, value_heads, attended_heads, grad_heads, lse, cols, counts
    )
    query_back, key_back, value_back = (
        lax.all_to_all(query_grad, "seq", split_axis=0, concat_axis=1, tiled=True),
        lax.all_to_all(key_grad, "seq", split_axis=0, concat_axis=1, tiled=True),
        lax.all_to_all(value_grad, "seq", split_axis=0, concat_axis=1, tiled=True),
    )
    grad_mixed = jnp.concatenate([query_back, key_back, value_back], axis=1)
    grad_normed = lax.dot_general(
        grad_mixed, w_qkv, (((1,), (1,)), ((), ())), preferred_element_type=jnp.float32
    )
    gained = grad_normed * gain[None, :]
    mean_one = jnp.mean(gained, axis=1, keepdims=True)
    mean_two = jnp.mean(gained * scaled, axis=1, keepdims=True)
    grad_feats = (
        cotan.astype(jnp.float32) + inverse * (gained - mean_one - scaled * mean_two)
    ).astype(jnp.bfloat16)
    terms = jnp.concatenate(
        [contract_rows(normed, grad_mixed), contract_rows(attended, cotan)], axis=1
    )
    piece = lax.psum_scatter(terms, ("seq", "dp"), scatter_dimension=0, tiled=True)
    own_rows = lax.all_gather(piece.astype(jnp.bfloat16), "dp", axis=0, tiled=True)
    grad_qkv = own_rows[:, :qkv_width]
    grad_out = own_rows[:, qkv_width:]
    return (result, grad_feats, grad_qkv, grad_out)


def solution(mesh):
    in_specs = (
        P(("dp", "seq"), None),
        P(),
        P(),
        P(),
        P("dp", None, None),
        P("dp", None),
        P(("dp", "seq"), None),
    )
    out_specs = (P(("dp", "seq"), None), P(("dp", "seq"), None), P("seq", None), P("seq", None))
    return jax.shard_map(body, mesh=mesh, in_specs=in_specs, out_specs=out_specs, check_vma=False)
```

```python
import functools

import jax
import jax.numpy as jnp
from jax import lax
from jax.experimental import pallas as pl
from jax.experimental.pallas import tpu as pltpu
from jax.sharding import PartitionSpec as P

HD = 64
BLK = 128
MAXB = 8
SCALE = HD ** (-0.5)
NEG = -1e30

EPSILON = 1e-05


def layer_norm(feats, gain):
    values_f = feats.astype(jnp.float32)
    centred = values_f - jnp.mean(values_f, axis=1, keepdims=True)
    inverse = lax.rsqrt(jnp.mean(centred * centred, axis=1, keepdims=True) + EPSILON)
    scaled = centred * inverse
    return (scaled, inverse, (scaled * gain[None, :]).astype(jnp.bfloat16))


def contract_rows(left_cols, right_cols):
    return lax.dot_general(
        left_cols, right_cols, (((0,), (0,)), ((), ())), preferred_element_type=jnp.float32
    )


def head_masks(width):
    lane = lax.broadcasted_iota(jnp.int32, (1, width), 1)
    return [(lane >= h * HD) & (lane < (h + 1) * HD) for h in range(width // HD)]


def stack_heads(x, masks):
    return jnp.concatenate([jnp.where(m, x, jnp.zeros_like(x)) for m in masks], axis=0)


def unstack_heads(y, masks):
    out = y[0:BLK]
    for h in range(1, len(masks)):
        out = jnp.where(masks[h], y[h * BLK : (h + 1) * BLK], out)
    return out


def nt_dot(a, b):
    return lax.dot_general(a, b, (((1,), (1,)), ((), ())), preferred_element_type=jnp.float32)


def tn_dot(a, b):
    return lax.dot_general(a, b, (((0,), (0,)), ((), ())), preferred_element_type=jnp.float32)


def gather_blocks(ref, cols_ref, r):
    return jnp.concatenate(
        [
            ref[pl.ds(pl.multiple_of(cols_ref[r * MAXB + s] * BLK, BLK), BLK), :]
            for s in range(MAXB)
        ],
        axis=0,
    )


def live_lanes(cnt):
    return lax.broadcasted_iota(jnp.int32, (1, MAXB * BLK), 1) < cnt * BLK


def attn_fwd_kernel(cols_ref, counts_ref, q_ref, k_ref, v_ref, o_ref, lse_ref):
    width = q_ref.shape[1]
    nblk = q_ref.shape[0] // BLK
    masks = head_masks(width)
    rows = len(masks) * BLK

    def row_body(r, carry):
        row0 = pl.multiple_of(r * BLK, BLK)
        live = live_lanes(counts_ref[r])
        q2 = stack_heads(q_ref[pl.ds(row0, BLK), :], masks)
        sc = jnp.where(live, nt_dot(q2, gather_blocks(k_ref, cols_ref, r)) * SCALE, NEG)
        m = jnp.max(sc, axis=1, keepdims=True)
        e = jnp.where(live, jnp.exp(sc - m), 0.0)
        l = jnp.sum(e, axis=1, keepdims=True)
        p = (e * (1.0 / l)).astype(jnp.bfloat16)
        acc = jnp.dot(p, gather_blocks(v_ref, cols_ref, r), preferred_element_type=jnp.float32)
        o_ref[pl.ds(row0, BLK), :] = unstack_heads(acc, masks).astype(o_ref.dtype)
        lse_ref[pl.ds(pl.multiple_of(r * rows, rows), rows), :] = jnp.broadcast_to(
            m + jnp.log(l), (rows, lse_ref.shape[1])
        )
        return carry

    lax.fori_loop(0, nblk, row_body, 0)


def attn_bwd_kernel(
    cols_ref, counts_ref, q_ref, k_ref, v_ref, o_ref, do_ref, lse_ref, dq_ref, dk_ref, dv_ref, dk_acc, dv_acc
):
    width = q_ref.shape[1]
    nblk = q_ref.shape[0] // BLK
    masks = head_masks(width)
    rows = len(masks) * BLK
    dk_acc[...] = jnp.zeros_like(dk_acc)
    dv_acc[...] = jnp.zeros_like(dv_acc)

    def row_body(r, carry):
        row0 = pl.multiple_of(r * BLK, BLK)
        cnt = counts_ref[r]
        live = live_lanes(cnt)
        q2 = stack_heads(q_ref[pl.ds(row0, BLK), :], masks)
        do_blk = do_ref[pl.ds(row0, BLK), :]
        do2 = stack_heads(do_blk, masks)
        prod = o_ref[pl.ds(row0, BLK), :].astype(jnp.float32) * do_blk.astype(jnp.float32)
        delta = jnp.concatenate(
            [jnp.sum(jnp.where(m, prod, 0.0), axis=1, keepdims=True) for m in masks], axis=0
        )
        lse = lse_ref[pl.ds(pl.multiple_of(r * rows, rows), rows), :][:, 0:1]
        kc = gather_blocks(k_ref, cols_ref, r)
        vc = gather_blocks(v_ref, cols_ref, r)
        sc = nt_dot(q2, kc) * SCALE
        p = jnp.where(live, jnp.exp(sc - lse), 0.0).astype(jnp.bfloat16)
        dp = nt_dot(do2, vc)
        ds = (p.astype(jnp.float32) * (dp - delta) * SCALE).astype(jnp.bfloat16)
        dq = jnp.dot(ds, kc, preferred_element_type=jnp.float32)
        dq_ref[pl.ds(row0, BLK), :] = unstack_heads(dq, masks).astype(dq_ref.dtype)
        dkc = tn_dot(ds, q2)
        dvc = tn_dot(p, do2)
        for s in range(MAXB):

            @pl.when(s < cnt)
            def _():
                col0 = pl.multiple_of(cols_ref[r * MAXB + s] * BLK, BLK)
                dk_acc[pl.ds(col0, BLK), :] += dkc[s * BLK : (s + 1) * BLK]
                dv_acc[pl.ds(col0, BLK), :] += dvc[s * BLK : (s + 1) * BLK]

        return carry

    lax.fori_loop(0, nblk, row_body, 0)
    dk_ref[...] = dk_acc[...].astype(dk_ref.dtype)
    dv_ref[...] = dv_acc[...].astype(dv_ref.dtype)


def smem_spec():
    return pl.BlockSpec(memory_space=pltpu.SMEM)


def vmem_spec():
    return pl.BlockSpec(memory_space=pltpu.VMEM)


VMEM_LIMIT = 48 * 1024 * 1024


def attention_forward(q, k, v, cols, counts):
    n, width = q.shape
    rows = (width // HD) * BLK
    return pl.pallas_call(
        attn_fwd_kernel,
        out_shape=(
            jax.ShapeDtypeStruct((n, width), jnp.bfloat16),
            jax.ShapeDtypeStruct(((n // BLK) * rows, 128), jnp.float32),
        ),
        in_specs=[smem_spec(), smem_spec(), vmem_spec(), vmem_spec(), vmem_spec()],
        out_specs=(vmem_spec(), vmem_spec()),
        compiler_params=pltpu.CompilerParams(vmem_limit_bytes=VMEM_LIMIT),
    )(cols, counts, q, k, v)


def attention_backward(q, k, v, o, do, lse, cols, counts):
    n, width = q.shape
    return pl.pallas_call(
        attn_bwd_kernel,
        out_shape=tuple(jax.ShapeDtypeStruct((n, width), jnp.bfloat16) for _ in range(3)),
        in_specs=[smem_spec(), smem_spec()] + [vmem_spec()] * 6,
        out_specs=(vmem_spec(), vmem_spec(), vmem_spec()),
        scratch_shapes=[pltpu.VMEM((n, width), jnp.float32), pltpu.VMEM((n, width), jnp.float32)],
        compiler_params=pltpu.CompilerParams(vmem_limit_bytes=VMEM_LIMIT),
    )(cols, counts, q, k, v, o, do, lse)


def body(feats, gain, w_qkv, w_out, block_cols, block_counts, cotan):
    model_width = feats.shape[1]
    qkv_width = 3 * model_width
    scaled, inverse, normed = layer_norm(feats, gain)
    mixed_proj = jnp.dot(normed, w_qkv, preferred_element_type=jnp.float32).astype(jnp.bfloat16)
    query_rows = mixed_proj[:, :model_width]
    key_rows = mixed_proj[:, model_width : 2 * model_width]
    value_rows = mixed_proj[:, 2 * model_width :]
    query_heads, key_heads, value_heads = (
        lax.all_to_all(query_rows, "seq", split_axis=1, concat_axis=0, tiled=True),
        lax.all_to_all(key_rows, "seq", split_axis=1, concat_axis=0, tiled=True),
        lax.all_to_all(value_rows, "seq", split_axis=1, concat_axis=0, tiled=True),
    )
    cols = block_cols[0].reshape(-1)
    counts = block_counts[0]
    attended_heads, lse = attention_forward(query_heads, key_heads, value_heads, cols, counts)
    attended = lax.all_to_all(attended_heads, "seq", split_axis=0, concat_axis=1, tiled=True)
    result = (
        feats.astype(jnp.float32) + jnp.dot(attended, w_out, preferred_element_type=jnp.float32)
    ).astype(jnp.bfloat16)
    grad_att = lax.dot_general(
        cotan, w_out, (((1,), (1,)), ((), ())), preferred_element_type=jnp.float32
    ).astype(jnp.bfloat16)
    grad_heads = lax.all_to_all(grad_att, "seq", split_axis=1, concat_axis=0, tiled=True)
    query_grad, key_grad, value_grad = attention_backward(
        query_heads, key_heads, value_heads, attended_heads, grad_heads, lse, cols, counts
    )
    query_back, key_back, value_back = (
        lax.all_to_all(query_grad, "seq", split_axis=0, concat_axis=1, tiled=True),
        lax.all_to_all(key_grad, "seq", split_axis=0, concat_axis=1, tiled=True),
        lax.all_to_all(value_grad, "seq", split_axis=0, concat_axis=1, tiled=True),
    )
    grad_mixed = jnp.concatenate([query_back, key_back, value_back], axis=1)
    grad_normed = lax.dot_general(
        grad_mixed, w_qkv, (((1,), (1,)), ((), ())), preferred_element_type=jnp.float32
    )
    gained = grad_normed * gain[None, :]
    mean_one = jnp.mean(gained, axis=1, keepdims=True)
    mean_two = jnp.mean(gained * scaled, axis=1, keepdims=True)
    grad_feats = (
        cotan.astype(jnp.float32) + inverse * (gained - mean_one - scaled * mean_two)
    ).astype(jnp.bfloat16)
    terms = jnp.concatenate(
        [contract_rows(normed, grad_mixed), contract_rows(attended, cotan)], axis=1
    )
    summed = lax.psum(terms, ("dp", "seq"))
    shard_rows = model_width // lax.axis_size("seq")
    own_rows = lax.dynamic_slice_in_dim(summed, lax.axis_index("seq") * shard_rows, shard_rows, 0)
    grad_qkv = own_rows[:, :qkv_width].astype(jnp.bfloat16)
    grad_out = own_rows[:, qkv_width:].astype(jnp.bfloat16)
    return (result, grad_feats, grad_qkv, grad_out)


def solution(mesh):
    in_specs = (
        P(("dp", "seq"), None),
        P(),
        P(),
        P(),
        P("dp", None, None),
        P("dp", None),
        P(("dp", "seq"), None),
    )
    out_specs = (P(("dp", "seq"), None), P(("dp", "seq"), None), P("seq", None), P("seq", None))
    return jax.shard_map(body, mesh=mesh, in_specs=in_specs, out_specs=out_specs, check_vma=False)
```

```python
import functools

import jax
import jax.numpy as jnp
from jax import lax
from jax.experimental import pallas as pl
from jax.experimental.pallas import tpu as pltpu
from jax.sharding import PartitionSpec as P

HD = 64
BLK = 128
MAXB = 8
SCALE = HD ** (-0.5)
NEG = -1e30

EPSILON = 1e-05


def layer_norm(feats, gain):
    values_f = feats.astype(jnp.float32)
    centred = values_f - jnp.mean(values_f, axis=1, keepdims=True)
    inverse = lax.rsqrt(jnp.mean(centred * centred, axis=1, keepdims=True) + EPSILON)
    scaled = centred * inverse
    return (scaled, inverse, (scaled * gain[None, :]).astype(jnp.bfloat16))


def contract_rows(left_cols, right_cols):
    return lax.dot_general(
        left_cols, right_cols, (((0,), (0,)), ((), ())), preferred_element_type=jnp.float32
    )


def head_masks(width):
    lane = lax.broadcasted_iota(jnp.int32, (1, width), 1)
    return [(lane >= h * HD) & (lane < (h + 1) * HD) for h in range(width // HD)]


def stack_heads(x, masks):
    return jnp.concatenate([jnp.where(m, x, jnp.zeros_like(x)) for m in masks], axis=0)


def unstack_heads(y, masks):
    out = y[0:BLK]
    for h in range(1, len(masks)):
        out = jnp.where(masks[h], y[h * BLK : (h + 1) * BLK], out)
    return out


def nt_dot(a, b):
    return lax.dot_general(a, b, (((1,), (1,)), ((), ())), preferred_element_type=jnp.float32)


def tn_dot(a, b):
    return lax.dot_general(a, b, (((0,), (0,)), ((), ())), preferred_element_type=jnp.float32)


def gather_blocks(ref, cols_ref, r):
    return jnp.concatenate(
        [
            ref[pl.ds(pl.multiple_of(cols_ref[r * MAXB + s] * BLK, BLK), BLK), :]
            for s in range(MAXB)
        ],
        axis=0,
    )


def live_lanes(cnt):
    return lax.broadcasted_iota(jnp.int32, (1, MAXB * BLK), 1) < cnt * BLK


def attn_fwd_kernel(cols_ref, counts_ref, q_ref, k_ref, v_ref, o_ref, lse_ref):
    width = q_ref.shape[1]
    nblk = q_ref.shape[0] // BLK
    masks = head_masks(width)
    rows = len(masks) * BLK

    def row_body(r, carry):
        row0 = pl.multiple_of(r * BLK, BLK)
        live = live_lanes(counts_ref[r])
        q2 = stack_heads(q_ref[pl.ds(row0, BLK), :], masks)
        sc = jnp.where(live, nt_dot(q2, gather_blocks(k_ref, cols_ref, r)) * SCALE, NEG)
        m = jnp.max(sc, axis=1, keepdims=True)
        e = jnp.where(live, jnp.exp(sc - m), 0.0)
        l = jnp.sum(e, axis=1, keepdims=True)
        p = (e * (1.0 / l)).astype(jnp.bfloat16)
        acc = jnp.dot(p, gather_blocks(v_ref, cols_ref, r), preferred_element_type=jnp.float32)
        o_ref[pl.ds(row0, BLK), :] = unstack_heads(acc, masks).astype(o_ref.dtype)
        lse_ref[pl.ds(pl.multiple_of(r * rows, rows), rows), :] = jnp.broadcast_to(
            m + jnp.log(l), (rows, lse_ref.shape[1])
        )
        return carry

    lax.fori_loop(0, nblk, row_body, 0)


def attn_bwd_kernel(
    cols_ref, counts_ref, q_ref, k_ref, v_ref, o_ref, do_ref, lse_ref, dq_ref, dk_ref, dv_ref, dk_acc, dv_acc
):
    width = q_ref.shape[1]
    nblk = q_ref.shape[0] // BLK
    masks = head_masks(width)
    rows = len(masks) * BLK
    dk_acc[...] = jnp.zeros_like(dk_acc)
    dv_acc[...] = jnp.zeros_like(dv_acc)

    def row_body(r, carry):
        row0 = pl.multiple_of(r * BLK, BLK)
        cnt = counts_ref[r]
        live = live_lanes(cnt)
        q2 = stack_heads(q_ref[pl.ds(row0, BLK), :], masks)
        do_blk = do_ref[pl.ds(row0, BLK), :]
        do2 = stack_heads(do_blk, masks)
        prod = o_ref[pl.ds(row0, BLK), :].astype(jnp.float32) * do_blk.astype(jnp.float32)
        delta = jnp.concatenate(
            [jnp.sum(jnp.where(m, prod, 0.0), axis=1, keepdims=True) for m in masks], axis=0
        )
        lse = lse_ref[pl.ds(pl.multiple_of(r * rows, rows), rows), :][:, 0:1]
        kc = gather_blocks(k_ref, cols_ref, r)
        vc = gather_blocks(v_ref, cols_ref, r)
        sc = nt_dot(q2, kc) * SCALE
        p = jnp.where(live, jnp.exp(sc - lse), 0.0).astype(jnp.bfloat16)
        dp = nt_dot(do2, vc)
        ds = (p.astype(jnp.float32) * (dp - delta) * SCALE).astype(jnp.bfloat16)
        dq = jnp.dot(ds, kc, preferred_element_type=jnp.float32)
        dq_ref[pl.ds(row0, BLK), :] = unstack_heads(dq, masks).astype(dq_ref.dtype)
        dkc = tn_dot(ds, q2)
        dvc = tn_dot(p, do2)
        for s in range(MAXB):

            @pl.when(s < cnt)
            def _():
                col0 = pl.multiple_of(cols_ref[r * MAXB + s] * BLK, BLK)
                dk_acc[pl.ds(col0, BLK), :] += dkc[s * BLK : (s + 1) * BLK]
                dv_acc[pl.ds(col0, BLK), :] += dvc[s * BLK : (s + 1) * BLK]

        return carry

    lax.fori_loop(0, nblk, row_body, 0)
    dk_ref[...] = dk_acc[...].astype(dk_ref.dtype)
    dv_ref[...] = dv_acc[...].astype(dv_ref.dtype)


def smem_spec():
    return pl.BlockSpec(memory_space=pltpu.SMEM)


def vmem_spec():
    return pl.BlockSpec(memory_space=pltpu.VMEM)


VMEM_LIMIT = 48 * 1024 * 1024


def attention_forward(q, k, v, cols, counts):
    n, width = q.shape
    rows = (width // HD) * BLK
    return pl.pallas_call(
        attn_fwd_kernel,
        out_shape=(
            jax.ShapeDtypeStruct((n, width), jnp.bfloat16),
            jax.ShapeDtypeStruct(((n // BLK) * rows, 128), jnp.float32),
        ),
        in_specs=[smem_spec(), smem_spec(), vmem_spec(), vmem_spec(), vmem_spec()],
        out_specs=(vmem_spec(), vmem_spec()),
        compiler_params=pltpu.CompilerParams(vmem_limit_bytes=VMEM_LIMIT),
    )(cols, counts, q, k, v)


def attention_backward(q, k, v, o, do, lse, cols, counts):
    n, width = q.shape
    return pl.pallas_call(
        attn_bwd_kernel,
        out_shape=tuple(jax.ShapeDtypeStruct((n, width), jnp.bfloat16) for _ in range(3)),
        in_specs=[smem_spec(), smem_spec()] + [vmem_spec()] * 6,
        out_specs=(vmem_spec(), vmem_spec(), vmem_spec()),
        scratch_shapes=[pltpu.VMEM((n, width), jnp.float32), pltpu.VMEM((n, width), jnp.float32)],
        compiler_params=pltpu.CompilerParams(vmem_limit_bytes=VMEM_LIMIT),
    )(cols, counts, q, k, v, o, do, lse)


def body(feats, gain, w_qkv, w_out, block_cols, block_counts, cotan):
    model_width = feats.shape[1]
    seq_count = lax.axis_size("seq")
    group_width = model_width // seq_count
    seq_at = lax.axis_index("seq")
    scaled, inverse, normed = layer_norm(feats, gain)
    normed_all = lax.all_gather(normed, "seq", axis=0, tiled=True)
    cotan_all = lax.all_gather(cotan, "seq", axis=0, tiled=True)
    w_heads = jnp.concatenate(
        [
            lax.dynamic_slice_in_dim(w_qkv, j * model_width + seq_at * group_width, group_width, 1)
            for j in range(3)
        ],
        axis=1,
    )
    mixed_heads = jnp.dot(normed_all, w_heads, preferred_element_type=jnp.float32).astype(
        jnp.bfloat16
    )
    query_heads = mixed_heads[:, :group_width]
    key_heads = mixed_heads[:, group_width : 2 * group_width]
    value_heads = mixed_heads[:, 2 * group_width :]
    cols = block_cols[0].reshape(-1)
    counts = block_counts[0]
    attended_heads, lse = attention_forward(query_heads, key_heads, value_heads, cols, counts)
    attended = lax.all_to_all(attended_heads, "seq", split_axis=0, concat_axis=1, tiled=True)
    result = (
        feats.astype(jnp.float32) + jnp.dot(attended, w_out, preferred_element_type=jnp.float32)
    ).astype(jnp.bfloat16)
    w_out_rows = lax.dynamic_slice_in_dim(w_out, seq_at * group_width, group_width, 0)
    grad_heads = lax.dot_general(
        cotan_all, w_out_rows, (((1,), (1,)), ((), ())), preferred_element_type=jnp.float32
    ).astype(jnp.bfloat16)
    query_grad, key_grad, value_grad = attention_backward(
        query_heads, key_heads, value_heads, attended_heads, grad_heads, lse, cols, counts
    )
    query_back, key_back, value_back = (
        lax.all_to_all(query_grad, "seq", split_axis=0, concat_axis=1, tiled=True),
        lax.all_to_all(key_grad, "seq", split_axis=0, concat_axis=1, tiled=True),
        lax.all_to_all(value_grad, "seq", split_axis=0, concat_axis=1, tiled=True),
    )
    grad_mixed = jnp.concatenate([query_back, key_back, value_back], axis=1)
    grad_normed = lax.dot_general(
        grad_mixed, w_qkv, (((1,), (1,)), ((), ())), preferred_element_type=jnp.float32
    )
    gained = grad_normed * gain[None, :]
    mean_one = jnp.mean(gained, axis=1, keepdims=True)
    mean_two = jnp.mean(gained * scaled, axis=1, keepdims=True)
    grad_feats = (
        cotan.astype(jnp.float32) + inverse * (gained - mean_one - scaled * mean_two)
    ).astype(jnp.bfloat16)
    grad_heads_mixed = jnp.concatenate([query_grad, key_grad, value_grad], axis=1)
    term_qkv = lax.psum(contract_rows(normed_all, grad_heads_mixed), "dp")
    term_out = lax.psum(contract_rows(attended_heads, cotan_all), "dp")
    moved = lax.all_to_all(
        term_qkv.astype(jnp.bfloat16), "seq", split_axis=0, concat_axis=1, tiled=True
    )
    rows = moved.shape[0]
    grad_qkv = (
        moved.reshape(rows, seq_count, 3, group_width)
        .transpose(0, 2, 1, 3)
        .reshape(rows, 3 * model_width)
    )
    grad_out = term_out.astype(jnp.bfloat16)
    return (result, grad_feats, grad_qkv, grad_out)


def solution(mesh):
    in_specs = (
        P(("dp", "seq"), None),
        P(),
        P(),
        P(),
        P("dp", None, None),
        P("dp", None),
        P(("dp", "seq"), None),
    )
    out_specs = (P(("dp", "seq"), None), P(("dp", "seq"), None), P("seq", None), P("seq", None))
    return jax.shard_map(body, mesh=mesh, in_specs=in_specs, out_specs=out_specs, check_vma=False)
```

```python
import functools

import jax
import jax.numpy as jnp
from jax import lax
from jax.experimental import pallas as pl
from jax.experimental.pallas import tpu as pltpu
from jax.sharding import PartitionSpec as P

HD = 64
BLK = 128
MAXB = 8
SCALE = HD ** (-0.5)
NEG = -1e30

EPSILON = 1e-05


def layer_norm(feats, gain):
    values_f = feats.astype(jnp.float32)
    centred = values_f - jnp.mean(values_f, axis=1, keepdims=True)
    inverse = lax.rsqrt(jnp.mean(centred * centred, axis=1, keepdims=True) + EPSILON)
    scaled = centred * inverse
    return (scaled, inverse, (scaled * gain[None, :]).astype(jnp.bfloat16))


def contract_rows(left_cols, right_cols):
    return lax.dot_general(
        left_cols, right_cols, (((0,), (0,)), ((), ())), preferred_element_type=jnp.float32
    )


def head_masks(width):
    lane = lax.broadcasted_iota(jnp.int32, (1, width), 1)
    return [(lane >= h * HD) & (lane < (h + 1) * HD) for h in range(width // HD)]


def stack_heads(x, masks):
    return jnp.concatenate([jnp.where(m, x, jnp.zeros_like(x)) for m in masks], axis=0)


def unstack_heads(y, masks):
    out = y[0:BLK]
    for h in range(1, len(masks)):
        out = jnp.where(masks[h], y[h * BLK : (h + 1) * BLK], out)
    return out


def nt_dot(a, b):
    return lax.dot_general(a, b, (((1,), (1,)), ((), ())), preferred_element_type=jnp.float32)


def tn_dot(a, b):
    return lax.dot_general(a, b, (((0,), (0,)), ((), ())), preferred_element_type=jnp.float32)


def gather_blocks(ref, cols_ref, r):
    return jnp.concatenate(
        [
            ref[pl.ds(pl.multiple_of(cols_ref[r * MAXB + s] * BLK, BLK), BLK), :]
            for s in range(MAXB)
        ],
        axis=0,
    )


def live_lanes(cnt):
    return lax.broadcasted_iota(jnp.int32, (1, MAXB * BLK), 1) < cnt * BLK


def attn_fwd_kernel(cols_ref, counts_ref, q_ref, k_ref, v_ref, o_ref, lse_ref):
    width = q_ref.shape[1]
    nblk = q_ref.shape[0] // BLK
    masks = head_masks(width)
    rows = len(masks) * BLK

    def row_body(r, carry):
        row0 = pl.multiple_of(r * BLK, BLK)
        live = live_lanes(counts_ref[r])
        q2 = stack_heads(q_ref[pl.ds(row0, BLK), :], masks)
        sc = jnp.where(live, nt_dot(q2, gather_blocks(k_ref, cols_ref, r)) * SCALE, NEG)
        m = jnp.max(sc, axis=1, keepdims=True)
        e = jnp.where(live, jnp.exp(sc - m), 0.0)
        l = jnp.sum(e, axis=1, keepdims=True)
        p = (e * (1.0 / l)).astype(jnp.bfloat16)
        acc = jnp.dot(p, gather_blocks(v_ref, cols_ref, r), preferred_element_type=jnp.float32)
        o_ref[pl.ds(row0, BLK), :] = unstack_heads(acc, masks).astype(o_ref.dtype)
        lse_ref[pl.ds(pl.multiple_of(r * rows, rows), rows), :] = jnp.broadcast_to(
            m + jnp.log(l), (rows, lse_ref.shape[1])
        )
        return carry

    lax.fori_loop(0, nblk, row_body, 0)


def attn_bwd_kernel(
    cols_ref, counts_ref, q_ref, k_ref, v_ref, o_ref, do_ref, lse_ref, dq_ref, dk_ref, dv_ref, dk_acc, dv_acc
):
    width = q_ref.shape[1]
    nblk = q_ref.shape[0] // BLK
    masks = head_masks(width)
    rows = len(masks) * BLK
    dk_acc[...] = jnp.zeros_like(dk_acc)
    dv_acc[...] = jnp.zeros_like(dv_acc)

    def row_body(r, carry):
        row0 = pl.multiple_of(r * BLK, BLK)
        cnt = counts_ref[r]
        live = live_lanes(cnt)
        q2 = stack_heads(q_ref[pl.ds(row0, BLK), :], masks)
        do_blk = do_ref[pl.ds(row0, BLK), :]
        do2 = stack_heads(do_blk, masks)
        prod = o_ref[pl.ds(row0, BLK), :].astype(jnp.float32) * do_blk.astype(jnp.float32)
        delta = jnp.concatenate(
            [jnp.sum(jnp.where(m, prod, 0.0), axis=1, keepdims=True) for m in masks], axis=0
        )
        lse = lse_ref[pl.ds(pl.multiple_of(r * rows, rows), rows), :][:, 0:1]
        kc = gather_blocks(k_ref, cols_ref, r)
        vc = gather_blocks(v_ref, cols_ref, r)
        sc = nt_dot(q2, kc) * SCALE
        p = jnp.where(live, jnp.exp(sc - lse), 0.0).astype(jnp.bfloat16)
        dp = nt_dot(do2, vc)
        ds = (p.astype(jnp.float32) * (dp - delta) * SCALE).astype(jnp.bfloat16)
        dq = jnp.dot(ds, kc, preferred_element_type=jnp.float32)
        dq_ref[pl.ds(row0, BLK), :] = unstack_heads(dq, masks).astype(dq_ref.dtype)
        dkc = tn_dot(ds, q2)
        dvc = tn_dot(p, do2)
        for s in range(MAXB):

            @pl.when(s < cnt)
            def _():
                col0 = pl.multiple_of(cols_ref[r * MAXB + s] * BLK, BLK)
                dk_acc[pl.ds(col0, BLK), :] += dkc[s * BLK : (s + 1) * BLK]
                dv_acc[pl.ds(col0, BLK), :] += dvc[s * BLK : (s + 1) * BLK]

        return carry

    lax.fori_loop(0, nblk, row_body, 0)
    dk_ref[...] = dk_acc[...].astype(dk_ref.dtype)
    dv_ref[...] = dv_acc[...].astype(dv_ref.dtype)


def smem_spec():
    return pl.BlockSpec(memory_space=pltpu.SMEM)


def vmem_spec():
    return pl.BlockSpec(memory_space=pltpu.VMEM)


VMEM_LIMIT = 48 * 1024 * 1024


def attention_forward(q, k, v, cols, counts):
    n, width = q.shape
    rows = (width // HD) * BLK
    return pl.pallas_call(
        attn_fwd_kernel,
        out_shape=(
            jax.ShapeDtypeStruct((n, width), jnp.bfloat16),
            jax.ShapeDtypeStruct(((n // BLK) * rows, 128), jnp.float32),
        ),
        in_specs=[smem_spec(), smem_spec(), vmem_spec(), vmem_spec(), vmem_spec()],
        out_specs=(vmem_spec(), vmem_spec()),
        compiler_params=pltpu.CompilerParams(vmem_limit_bytes=VMEM_LIMIT),
    )(cols, counts, q, k, v)


def attention_backward(q, k, v, o, do, lse, cols, counts):
    n, width = q.shape
    return pl.pallas_call(
        attn_bwd_kernel,
        out_shape=tuple(jax.ShapeDtypeStruct((n, width), jnp.bfloat16) for _ in range(3)),
        in_specs=[smem_spec(), smem_spec()] + [vmem_spec()] * 6,
        out_specs=(vmem_spec(), vmem_spec(), vmem_spec()),
        scratch_shapes=[pltpu.VMEM((n, width), jnp.float32), pltpu.VMEM((n, width), jnp.float32)],
        compiler_params=pltpu.CompilerParams(vmem_limit_bytes=VMEM_LIMIT),
    )(cols, counts, q, k, v, o, do, lse)


def regroup_columns(moved, seq_count, group_width):
    rows = moved.shape[0]
    return (
        moved.reshape(rows, seq_count, 3, group_width)
        .transpose(0, 2, 1, 3)
        .reshape(rows, 3 * seq_count * group_width)
    )


def sum_over_dp(term, axis):
    piece = lax.psum_scatter(term, "dp", scatter_dimension=axis, tiled=True)
    return lax.all_gather(piece.astype(jnp.bfloat16), "dp", axis=axis, tiled=True)


def body(feats, gain, w_qkv, w_out, block_cols, block_counts, cotan):
    model_width = feats.shape[1]
    seq_count = lax.axis_size("seq")
    group_width = model_width // seq_count
    seq_at = lax.axis_index("seq")
    scaled, inverse, normed = layer_norm(feats, gain)
    normed_all = lax.all_gather(normed, "seq", axis=0, tiled=True)
    cotan_all = lax.all_gather(cotan, "seq", axis=0, tiled=True)
    w_heads = jnp.concatenate(
        [
            lax.dynamic_slice_in_dim(w_qkv, j * model_width + seq_at * group_width, group_width, 1)
            for j in range(3)
        ],
        axis=1,
    )
    mixed_heads = jnp.dot(normed_all, w_heads, preferred_element_type=jnp.float32).astype(
        jnp.bfloat16
    )
    query_heads = mixed_heads[:, :group_width]
    key_heads = mixed_heads[:, group_width : 2 * group_width]
    value_heads = mixed_heads[:, 2 * group_width :]
    cols = block_cols[0].reshape(-1)
    counts = block_counts[0]
    attended_heads, lse = attention_forward(query_heads, key_heads, value_heads, cols, counts)
    attended = lax.all_to_all(attended_heads, "seq", split_axis=0, concat_axis=1, tiled=True)
    result = (
        feats.astype(jnp.float32) + jnp.dot(attended, w_out, preferred_element_type=jnp.float32)
    ).astype(jnp.bfloat16)
    w_out_rows = lax.dynamic_slice_in_dim(w_out, seq_at * group_width, group_width, 0)
    grad_heads = lax.dot_general(
        cotan_all, w_out_rows, (((1,), (1,)), ((), ())), preferred_element_type=jnp.float32
    ).astype(jnp.bfloat16)
    query_grad, key_grad, value_grad = attention_backward(
        query_heads, key_heads, value_heads, attended_heads, grad_heads, lse, cols, counts
    )
    grad_heads_mixed = jnp.concatenate([query_grad, key_grad, value_grad], axis=1)
    grad_mixed = regroup_columns(
        lax.all_to_all(grad_heads_mixed, "seq", split_axis=0, concat_axis=1, tiled=True),
        seq_count,
        group_width,
    )
    grad_normed = lax.dot_general(
        grad_mixed, w_qkv, (((1,), (1,)), ((), ())), preferred_element_type=jnp.float32
    )
    gained = grad_normed * gain[None, :]
    mean_one = jnp.mean(gained, axis=1, keepdims=True)
    mean_two = jnp.mean(gained * scaled, axis=1, keepdims=True)
    grad_feats = (
        cotan.astype(jnp.float32) + inverse * (gained - mean_one - scaled * mean_two)
    ).astype(jnp.bfloat16)
    term_qkv = sum_over_dp(contract_rows(normed_all, grad_heads_mixed), 0)
    term_out = sum_over_dp(contract_rows(attended_heads, cotan_all), 1)
    grad_qkv = regroup_columns(
        lax.all_to_all(term_qkv, "seq", split_axis=0, concat_axis=1, tiled=True),
        seq_count,
        group_width,
    )
    grad_out = term_out
    return (result, grad_feats, grad_qkv, grad_out)


def solution(mesh):
    in_specs = (
        P(("dp", "seq"), None),
        P(),
        P(),
        P(),
        P("dp", None, None),
        P("dp", None),
        P(("dp", "seq"), None),
    )
    out_specs = (P(("dp", "seq"), None), P(("dp", "seq"), None), P("seq", None), P("seq", None))
    return jax.shard_map(body, mesh=mesh, in_specs=in_specs, out_specs=out_specs, check_vma=False)
```

```python
import functools

import jax
import jax.numpy as jnp
from jax import lax
from jax.experimental import pallas as pl
from jax.experimental.pallas import tpu as pltpu
from jax.sharding import PartitionSpec as P

HD = 64
BLK = 128
MAXB = 8
SCALE = HD ** (-0.5)
NEG = -1e30

EPSILON = 1e-05


def layer_norm(feats, gain):
    values_f = feats.astype(jnp.float32)
    centred = values_f - jnp.mean(values_f, axis=1, keepdims=True)
    inverse = lax.rsqrt(jnp.mean(centred * centred, axis=1, keepdims=True) + EPSILON)
    scaled = centred * inverse
    return (scaled, inverse, (scaled * gain[None, :]).astype(jnp.bfloat16))


def contract_rows(left_cols, right_cols):
    return lax.dot_general(
        left_cols, right_cols, (((0,), (0,)), ((), ())), preferred_element_type=jnp.float32
    )


def head_masks(width):
    lane = lax.broadcasted_iota(jnp.int32, (1, width), 1)
    return [(lane >= h * HD) & (lane < (h + 1) * HD) for h in range(width // HD)]


def stack_heads(x, masks):
    return jnp.concatenate([jnp.where(m, x, jnp.zeros_like(x)) for m in masks], axis=0)


def unstack_heads(y, masks):
    out = y[0:BLK]
    for h in range(1, len(masks)):
        out = jnp.where(masks[h], y[h * BLK : (h + 1) * BLK], out)
    return out


def nt_dot(a, b):
    return lax.dot_general(a, b, (((1,), (1,)), ((), ())), preferred_element_type=jnp.float32)


def tn_dot(a, b):
    return lax.dot_general(a, b, (((0,), (0,)), ((), ())), preferred_element_type=jnp.float32)


def gather_blocks(ref, cols_ref, r):
    return jnp.concatenate(
        [
            ref[pl.ds(pl.multiple_of(cols_ref[r * MAXB + s] * BLK, BLK), BLK), :]
            for s in range(MAXB)
        ],
        axis=0,
    )


def live_lanes(cnt):
    return lax.broadcasted_iota(jnp.int32, (1, MAXB * BLK), 1) < cnt * BLK


def attn_fwd_kernel(cols_ref, counts_ref, q_ref, k_ref, v_ref, o_ref, lse_ref):
    width = q_ref.shape[1]
    nblk = q_ref.shape[0] // BLK
    masks = head_masks(width)
    rows = len(masks) * BLK

    def row_body(r, carry):
        row0 = pl.multiple_of(r * BLK, BLK)
        live = live_lanes(counts_ref[r])
        q2 = stack_heads(q_ref[pl.ds(row0, BLK), :], masks)
        sc = jnp.where(live, nt_dot(q2, gather_blocks(k_ref, cols_ref, r)) * SCALE, NEG)
        m = jnp.max(sc, axis=1, keepdims=True)
        e = jnp.where(live, jnp.exp(sc - m), 0.0)
        l = jnp.sum(e, axis=1, keepdims=True)
        p = (e * (1.0 / l)).astype(jnp.bfloat16)
        acc = jnp.dot(p, gather_blocks(v_ref, cols_ref, r), preferred_element_type=jnp.float32)
        o_ref[pl.ds(row0, BLK), :] = unstack_heads(acc, masks).astype(o_ref.dtype)
        lse_ref[pl.ds(pl.multiple_of(r * rows, rows), rows), :] = jnp.broadcast_to(
            m + jnp.log(l), (rows, lse_ref.shape[1])
        )
        return carry

    lax.fori_loop(0, nblk, row_body, 0)


def attn_bwd_kernel(
    cols_ref, counts_ref, q_ref, k_ref, v_ref, o_ref, do_ref, lse_ref, dq_ref, dk_ref, dv_ref, dk_acc, dv_acc
):
    width = q_ref.shape[1]
    nblk = q_ref.shape[0] // BLK
    masks = head_masks(width)
    rows = len(masks) * BLK
    dk_acc[...] = jnp.zeros_like(dk_acc)
    dv_acc[...] = jnp.zeros_like(dv_acc)

    def row_body(r, carry):
        row0 = pl.multiple_of(r * BLK, BLK)
        cnt = counts_ref[r]
        live = live_lanes(cnt)
        q2 = stack_heads(q_ref[pl.ds(row0, BLK), :], masks)
        do_blk = do_ref[pl.ds(row0, BLK), :]
        do2 = stack_heads(do_blk, masks)
        prod = o_ref[pl.ds(row0, BLK), :].astype(jnp.float32) * do_blk.astype(jnp.float32)
        delta = jnp.concatenate(
            [jnp.sum(jnp.where(m, prod, 0.0), axis=1, keepdims=True) for m in masks], axis=0
        )
        lse = lse_ref[pl.ds(pl.multiple_of(r * rows, rows), rows), :][:, 0:1]
        kc = gather_blocks(k_ref, cols_ref, r)
        vc = gather_blocks(v_ref, cols_ref, r)
        sc = nt_dot(q2, kc) * SCALE
        p = jnp.where(live, jnp.exp(sc - lse), 0.0).astype(jnp.bfloat16)
        dp = nt_dot(do2, vc)
        ds = (p.astype(jnp.float32) * (dp - delta) * SCALE).astype(jnp.bfloat16)
        dq = jnp.dot(ds, kc, preferred_element_type=jnp.float32)
        dq_ref[pl.ds(row0, BLK), :] = unstack_heads(dq, masks).astype(dq_ref.dtype)
        dkc = tn_dot(ds, q2)
        dvc = tn_dot(p, do2)
        for s in range(MAXB):

            @pl.when(s < cnt)
            def _():
                col0 = pl.multiple_of(cols_ref[r * MAXB + s] * BLK, BLK)
                dk_acc[pl.ds(col0, BLK), :] += dkc[s * BLK : (s + 1) * BLK]
                dv_acc[pl.ds(col0, BLK), :] += dvc[s * BLK : (s + 1) * BLK]

        return carry

    lax.fori_loop(0, nblk, row_body, 0)
    dk_ref[...] = dk_acc[...].astype(dk_ref.dtype)
    dv_ref[...] = dv_acc[...].astype(dv_ref.dtype)


def smem_spec():
    return pl.BlockSpec(memory_space=pltpu.SMEM)


def vmem_spec():
    return pl.BlockSpec(memory_space=pltpu.VMEM)


VMEM_LIMIT = 48 * 1024 * 1024


def attention_forward(q, k, v, cols, counts):
    n, width = q.shape
    rows = (width // HD) * BLK
    return pl.pallas_call(
        attn_fwd_kernel,
        out_shape=(
            jax.ShapeDtypeStruct((n, width), jnp.bfloat16),
            jax.ShapeDtypeStruct(((n // BLK) * rows, 128), jnp.float32),
        ),
        in_specs=[smem_spec(), smem_spec(), vmem_spec(), vmem_spec(), vmem_spec()],
        out_specs=(vmem_spec(), vmem_spec()),
        compiler_params=pltpu.CompilerParams(vmem_limit_bytes=VMEM_LIMIT),
    )(cols, counts, q, k, v)


def attention_backward(q, k, v, o, do, lse, cols, counts):
    n, width = q.shape
    return pl.pallas_call(
        attn_bwd_kernel,
        out_shape=tuple(jax.ShapeDtypeStruct((n, width), jnp.bfloat16) for _ in range(3)),
        in_specs=[smem_spec(), smem_spec()] + [vmem_spec()] * 6,
        out_specs=(vmem_spec(), vmem_spec(), vmem_spec()),
        scratch_shapes=[pltpu.VMEM((n, width), jnp.float32), pltpu.VMEM((n, width), jnp.float32)],
        compiler_params=pltpu.CompilerParams(vmem_limit_bytes=VMEM_LIMIT),
    )(cols, counts, q, k, v, o, do, lse)


def regroup_columns(moved, seq_count, group_width):
    rows = moved.shape[0]
    return (
        moved.reshape(rows, seq_count, 3, group_width)
        .transpose(0, 2, 1, 3)
        .reshape(rows, 3 * seq_count * group_width)
    )


MESH = pl.DeviceIdType.MESH


def dp_sum_kernel(n, x_ref, o_ref, recv, gath, send1, recv1, send2, recv2):
    me = lax.axis_index("dp")
    barrier = pltpu.get_barrier_semaphore()
    for k in range(1, n):
        pl.semaphore_signal(
            barrier, inc=1, device_id={"dp": lax.rem(me + k, n)}, device_id_type=MESH
        )
    pl.semaphore_wait(barrier, n - 1)

    def exchange(src_of, dst, send, arrive):
        started = []
        for k in range(1, n):
            peer = lax.rem(me + k, n)
            copy = pltpu.make_async_remote_copy(
                src_ref=src_of(peer),
                dst_ref=dst.at[me],
                send_sem=send.at[peer],
                recv_sem=arrive.at[me],
                device_id={"dp": peer},
                device_id_type=MESH,
            )
            copy.start()
            started.append(copy)
        for k in range(1, n):
            source = lax.rem(me + n - k, n)
            pltpu.make_async_remote_copy(
                src_ref=src_of(source),
                dst_ref=dst.at[source],
                send_sem=send.at[source],
                recv_sem=arrive.at[source],
                device_id={"dp": source},
                device_id_type=MESH,
            ).wait_recv()
        for copy in started:
            copy.wait_send()

    exchange(lambda peer: x_ref.at[peer], recv, send1, recv1)
    total = x_ref[me]
    for k in range(1, n):
        total = total + recv[lax.rem(me + k, n)]
    gath[me] = total.astype(gath.dtype)
    exchange(lambda peer: gath.at[me], gath, send2, recv2)
    o_ref[...] = gath[...]


def sum_over_dp(term):
    n = lax.axis_size("dp")
    rows, cols = term.shape
    chunked = term.reshape(n, rows // n, cols)
    out = pl.pallas_call(
        functools.partial(dp_sum_kernel, n),
        out_shape=jax.ShapeDtypeStruct(chunked.shape, jnp.bfloat16),
        in_specs=[vmem_spec()],
        out_specs=vmem_spec(),
        scratch_shapes=[
            pltpu.VMEM(chunked.shape, jnp.float32),
            pltpu.VMEM(chunked.shape, jnp.bfloat16),
            pltpu.SemaphoreType.DMA((n,)),
            pltpu.SemaphoreType.DMA((n,)),
            pltpu.SemaphoreType.DMA((n,)),
            pltpu.SemaphoreType.DMA((n,)),
        ],
        compiler_params=pltpu.CompilerParams(
            collective_id=0, has_side_effects=True, vmem_limit_bytes=VMEM_LIMIT
        ),
    )(chunked)
    return out.reshape(rows, cols)


def body(feats, gain, w_qkv, w_out, block_cols, block_counts, cotan):
    model_width = feats.shape[1]
    seq_count = lax.axis_size("seq")
    group_width = model_width // seq_count
    seq_at = lax.axis_index("seq")
    scaled, inverse, normed = layer_norm(feats, gain)
    normed_all = lax.all_gather(normed, "seq", axis=0, tiled=True)
    cotan_all = lax.all_gather(cotan, "seq", axis=0, tiled=True)
    w_heads = jnp.concatenate(
        [
            lax.dynamic_slice_in_dim(w_qkv, j * model_width + seq_at * group_width, group_width, 1)
            for j in range(3)
        ],
        axis=1,
    )
    mixed_heads = jnp.dot(normed_all, w_heads, preferred_element_type=jnp.float32).astype(
        jnp.bfloat16
    )
    query_heads = mixed_heads[:, :group_width]
    key_heads = mixed_heads[:, group_width : 2 * group_width]
    value_heads = mixed_heads[:, 2 * group_width :]
    cols = block_cols[0].reshape(-1)
    counts = block_counts[0]
    attended_heads, lse = attention_forward(query_heads, key_heads, value_heads, cols, counts)
    attended = lax.all_to_all(attended_heads, "seq", split_axis=0, concat_axis=1, tiled=True)
    result = (
        feats.astype(jnp.float32) + jnp.dot(attended, w_out, preferred_element_type=jnp.float32)
    ).astype(jnp.bfloat16)
    w_out_rows = lax.dynamic_slice_in_dim(w_out, seq_at * group_width, group_width, 0)
    grad_heads = lax.dot_general(
        cotan_all, w_out_rows, (((1,), (1,)), ((), ())), preferred_element_type=jnp.float32
    ).astype(jnp.bfloat16)
    query_grad, key_grad, value_grad = attention_backward(
        query_heads, key_heads, value_heads, attended_heads, grad_heads, lse, cols, counts
    )
    grad_heads_mixed = jnp.concatenate([query_grad, key_grad, value_grad], axis=1)
    grad_mixed = regroup_columns(
        lax.all_to_all(grad_heads_mixed, "seq", split_axis=0, concat_axis=1, tiled=True),
        seq_count,
        group_width,
    )
    grad_normed = lax.dot_general(
        grad_mixed, w_qkv, (((1,), (1,)), ((), ())), preferred_element_type=jnp.float32
    )
    gained = grad_normed * gain[None, :]
    mean_one = jnp.mean(gained, axis=1, keepdims=True)
    mean_two = jnp.mean(gained * scaled, axis=1, keepdims=True)
    grad_feats = (
        cotan.astype(jnp.float32) + inverse * (gained - mean_one - scaled * mean_two)
    ).astype(jnp.bfloat16)
    term_qkv = contract_rows(normed_all, grad_heads_mixed)
    term_out = contract_rows(attended_heads, cotan_all)
    qkv_cols = term_qkv.shape[1]
    summed = sum_over_dp(
        jnp.concatenate([term_qkv, term_out.reshape(term_qkv.shape[0], -1)], axis=1)
    )
    term_qkv = summed[:, :qkv_cols]
    term_out = summed[:, qkv_cols:].reshape(term_out.shape)
    grad_qkv = regroup_columns(
        lax.all_to_all(term_qkv, "seq", split_axis=0, concat_axis=1, tiled=True),
        seq_count,
        group_width,
    )
    grad_out = term_out
    return (result, grad_feats, grad_qkv, grad_out)


def solution(mesh):
    in_specs = (
        P(("dp", "seq"), None),
        P(),
        P(),
        P(),
        P("dp", None, None),
        P("dp", None),
        P(("dp", "seq"), None),
    )
    out_specs = (P(("dp", "seq"), None), P(("dp", "seq"), None), P("seq", None), P("seq", None))
    return jax.shard_map(body, mesh=mesh, in_specs=in_specs, out_specs=out_specs, check_vma=False)
```

```python
import functools

import jax
import jax.numpy as jnp
from jax import lax
from jax.experimental import pallas as pl
from jax.experimental.pallas import tpu as pltpu
from jax.sharding import PartitionSpec as P

HD = 64
BLK = 128
MAXB = 8
SCALE = HD ** (-0.5)
NEG = -1e30

EPSILON = 1e-05


def layer_norm(feats, gain):
    values_f = feats.astype(jnp.float32)
    centred = values_f - jnp.mean(values_f, axis=1, keepdims=True)
    inverse = lax.rsqrt(jnp.mean(centred * centred, axis=1, keepdims=True) + EPSILON)
    scaled = centred * inverse
    return (scaled, inverse, (scaled * gain[None, :]).astype(jnp.bfloat16))


def contract_rows(left_cols, right_cols):
    return lax.dot_general(
        left_cols, right_cols, (((0,), (0,)), ((), ())), preferred_element_type=jnp.float32
    )


def head_masks(width):
    lane = lax.broadcasted_iota(jnp.int32, (1, width), 1)
    return [(lane >= h * HD) & (lane < (h + 1) * HD) for h in range(width // HD)]


def stack_heads(x, masks):
    return jnp.concatenate([jnp.where(m, x, jnp.zeros_like(x)) for m in masks], axis=0)


def unstack_heads(y, masks):
    out = y[0:BLK]
    for h in range(1, len(masks)):
        out = jnp.where(masks[h], y[h * BLK : (h + 1) * BLK], out)
    return out


def nt_dot(a, b):
    return lax.dot_general(a, b, (((1,), (1,)), ((), ())), preferred_element_type=jnp.float32)


def tn_dot(a, b):
    return lax.dot_general(a, b, (((0,), (0,)), ((), ())), preferred_element_type=jnp.float32)


def gather_blocks(ref, cols_ref, r):
    return jnp.concatenate(
        [
            ref[pl.ds(pl.multiple_of(cols_ref[r * MAXB + s] * BLK, BLK), BLK), :]
            for s in range(MAXB)
        ],
        axis=0,
    )


def live_lanes(cnt):
    return lax.broadcasted_iota(jnp.int32, (1, MAXB * BLK), 1) < cnt * BLK


def attn_fwd_kernel(cols_ref, counts_ref, q_ref, k_ref, v_ref, o_ref, lse_ref):
    width = q_ref.shape[1]
    nblk = q_ref.shape[0] // BLK
    masks = head_masks(width)
    rows = len(masks) * BLK

    def row_body(r, carry):
        row0 = pl.multiple_of(r * BLK, BLK)
        live = live_lanes(counts_ref[r])
        q2 = stack_heads(q_ref[pl.ds(row0, BLK), :], masks)
        sc = jnp.where(live, nt_dot(q2, gather_blocks(k_ref, cols_ref, r)) * SCALE, NEG)
        m = jnp.max(sc, axis=1, keepdims=True)
        e = jnp.where(live, jnp.exp(sc - m), 0.0)
        l = jnp.sum(e, axis=1, keepdims=True)
        p = (e * (1.0 / l)).astype(jnp.bfloat16)
        acc = jnp.dot(p, gather_blocks(v_ref, cols_ref, r), preferred_element_type=jnp.float32)
        o_ref[pl.ds(row0, BLK), :] = unstack_heads(acc, masks).astype(o_ref.dtype)
        lse_ref[pl.ds(pl.multiple_of(r * rows, rows), rows), :] = jnp.broadcast_to(
            m + jnp.log(l), (rows, lse_ref.shape[1])
        )
        return carry

    lax.fori_loop(0, nblk, row_body, 0)


def attn_bwd_kernel(
    cols_ref, counts_ref, q_ref, k_ref, v_ref, o_ref, do_ref, lse_ref, dq_ref, dk_ref, dv_ref, dk_acc, dv_acc
):
    width = q_ref.shape[1]
    nblk = q_ref.shape[0] // BLK
    masks = head_masks(width)
    rows = len(masks) * BLK
    dk_acc[...] = jnp.zeros_like(dk_acc)
    dv_acc[...] = jnp.zeros_like(dv_acc)

    def row_body(r, carry):
        row0 = pl.multiple_of(r * BLK, BLK)
        cnt = counts_ref[r]
        live = live_lanes(cnt)
        q2 = stack_heads(q_ref[pl.ds(row0, BLK), :], masks)
        do_blk = do_ref[pl.ds(row0, BLK), :]
        do2 = stack_heads(do_blk, masks)
        prod = o_ref[pl.ds(row0, BLK), :].astype(jnp.float32) * do_blk.astype(jnp.float32)
        delta = jnp.concatenate(
            [jnp.sum(jnp.where(m, prod, 0.0), axis=1, keepdims=True) for m in masks], axis=0
        )
        lse = lse_ref[pl.ds(pl.multiple_of(r * rows, rows), rows), :][:, 0:1]
        kc = gather_blocks(k_ref, cols_ref, r)
        vc = gather_blocks(v_ref, cols_ref, r)
        sc = nt_dot(q2, kc) * SCALE
        p = jnp.where(live, jnp.exp(sc - lse), 0.0).astype(jnp.bfloat16)
        dp = nt_dot(do2, vc)
        ds = (p.astype(jnp.float32) * (dp - delta) * SCALE).astype(jnp.bfloat16)
        dq = jnp.dot(ds, kc, preferred_element_type=jnp.float32)
        dq_ref[pl.ds(row0, BLK), :] = unstack_heads(dq, masks).astype(dq_ref.dtype)
        dkc = tn_dot(ds, q2)
        dvc = tn_dot(p, do2)
        for s in range(MAXB):

            @pl.when(s < cnt)
            def _():
                col0 = pl.multiple_of(cols_ref[r * MAXB + s] * BLK, BLK)
                dk_acc[pl.ds(col0, BLK), :] += dkc[s * BLK : (s + 1) * BLK]
                dv_acc[pl.ds(col0, BLK), :] += dvc[s * BLK : (s + 1) * BLK]

        return carry

    lax.fori_loop(0, nblk, row_body, 0)
    dk_ref[...] = dk_acc[...].astype(dk_ref.dtype)
    dv_ref[...] = dv_acc[...].astype(dv_ref.dtype)


def smem_spec():
    return pl.BlockSpec(memory_space=pltpu.SMEM)


def vmem_spec():
    return pl.BlockSpec(memory_space=pltpu.VMEM)


VMEM_LIMIT = 48 * 1024 * 1024


def attention_forward(q, k, v, cols, counts):
    n, width = q.shape
    rows = (width // HD) * BLK
    return pl.pallas_call(
        attn_fwd_kernel,
        out_shape=(
            jax.ShapeDtypeStruct((n, width), jnp.bfloat16),
            jax.ShapeDtypeStruct(((n // BLK) * rows, 128), jnp.float32),
        ),
        in_specs=[smem_spec(), smem_spec(), vmem_spec(), vmem_spec(), vmem_spec()],
        out_specs=(vmem_spec(), vmem_spec()),
        compiler_params=pltpu.CompilerParams(vmem_limit_bytes=VMEM_LIMIT),
    )(cols, counts, q, k, v)


def attention_backward(q, k, v, o, do, lse, cols, counts):
    n, width = q.shape
    return pl.pallas_call(
        attn_bwd_kernel,
        out_shape=tuple(jax.ShapeDtypeStruct((n, width), jnp.bfloat16) for _ in range(3)),
        in_specs=[smem_spec(), smem_spec()] + [vmem_spec()] * 6,
        out_specs=(vmem_spec(), vmem_spec(), vmem_spec()),
        scratch_shapes=[pltpu.VMEM((n, width), jnp.float32), pltpu.VMEM((n, width), jnp.float32)],
        compiler_params=pltpu.CompilerParams(vmem_limit_bytes=VMEM_LIMIT),
    )(cols, counts, q, k, v, o, do, lse)


def regroup_columns(moved, seq_count, group_width):
    rows = moved.shape[0]
    return (
        moved.reshape(rows, seq_count, 3, group_width)
        .transpose(0, 2, 1, 3)
        .reshape(rows, 3 * seq_count * group_width)
    )


MESH = pl.DeviceIdType.MESH


def exchange_kernel(n, m, x_ref, g_ref, o_ref, moved_ref, recv, gath, landed, sems):
    me = lax.axis_index("dp")
    here = lax.axis_index("seq")
    barrier = pltpu.get_barrier_semaphore()
    for k in range(1, n):
        pl.semaphore_signal(
            barrier, inc=1, device_id={"dp": lax.rem(me + k, n)}, device_id_type=MESH
        )
    for k in range(1, m):
        pl.semaphore_signal(
            barrier, inc=1, device_id={"seq": lax.rem(here + k, m)}, device_id_type=MESH
        )
    pl.semaphore_wait(barrier, n - 1 + m - 1)

    def start_all(src_of, dst, send, arrive, axis, at, size):
        started = []
        for k in range(1, size):
            peer = lax.rem(at + k, size)
            copy = pltpu.make_async_remote_copy(
                src_ref=src_of(peer),
                dst_ref=dst.at[at],
                send_sem=send.at[peer],
                recv_sem=arrive.at[at],
                device_id={axis: peer},
                device_id_type=MESH,
            )
            copy.start()
            started.append(copy)
        return started

    def finish_all(started, src_of, dst, send, arrive, axis, at, size):
        for k in range(1, size):
            source = lax.rem(at + size - k, size)
            pltpu.make_async_remote_copy(
                src_ref=src_of(source),
                dst_ref=dst.at[source],
                send_sem=send.at[source],
                recv_sem=arrive.at[source],
                device_id={axis: source},
                device_id_type=MESH,
            ).wait_recv()
        for copy in started:
            copy.wait_send()

    a2a = (lambda peer: g_ref.at[peer], landed, sems.at[4], sems.at[5], "seq", here, m)
    a2a_started = start_all(*a2a)
    rs = (lambda peer: x_ref.at[peer], recv, sems.at[0], sems.at[1], "dp", me, n)
    finish_all(start_all(*rs), *rs)
    total = x_ref[me]
    for k in range(1, n):
        total = total + recv[lax.rem(me + k, n)]
    gath[me] = total.astype(gath.dtype)
    ag = (lambda peer: gath.at[me], gath, sems.at[2], sems.at[3], "dp", me, n)
    finish_all(start_all(*ag), *ag)
    o_ref[...] = gath[...]
    landed[here] = g_ref[here]
    finish_all(a2a_started, *a2a)
    moved_ref[...] = landed[...]


def sum_and_exchange(term, grads):
    n = lax.axis_size("dp")
    m = lax.axis_size("seq")
    rows, cols = term.shape
    chunked = term.reshape(n, rows // n, cols)
    pieces = grads.reshape(m, grads.shape[0] // m, grads.shape[1])
    out, moved = pl.pallas_call(
        functools.partial(exchange_kernel, n, m),
        out_shape=(
            jax.ShapeDtypeStruct(chunked.shape, jnp.bfloat16),
            jax.ShapeDtypeStruct(pieces.shape, pieces.dtype),
        ),
        in_specs=[vmem_spec(), vmem_spec()],
        out_specs=(vmem_spec(), vmem_spec()),
        scratch_shapes=[
            pltpu.VMEM(chunked.shape, jnp.float32),
            pltpu.VMEM(chunked.shape, jnp.bfloat16),
            pltpu.VMEM(pieces.shape, pieces.dtype),
            pltpu.SemaphoreType.DMA((6, max(n, m))),
        ],
        compiler_params=pltpu.CompilerParams(
            collective_id=0, has_side_effects=True, vmem_limit_bytes=VMEM_LIMIT
        ),
    )(chunked, pieces)
    return out.reshape(rows, cols), jnp.concatenate(list(moved), axis=1)


def body(feats, gain, w_qkv, w_out, block_cols, block_counts, cotan):
    model_width = feats.shape[1]
    seq_count = lax.axis_size("seq")
    group_width = model_width // seq_count
    seq_at = lax.axis_index("seq")
    scaled, inverse, normed = layer_norm(feats, gain)
    normed_all = lax.all_gather(normed, "seq", axis=0, tiled=True)
    cotan_all = lax.all_gather(cotan, "seq", axis=0, tiled=True)
    w_heads = jnp.concatenate(
        [
            lax.dynamic_slice_in_dim(w_qkv, j * model_width + seq_at * group_width, group_width, 1)
            for j in range(3)
        ],
        axis=1,
    )
    mixed_heads = jnp.dot(normed_all, w_heads, preferred_element_type=jnp.float32).astype(
        jnp.bfloat16
    )
    query_heads = mixed_heads[:, :group_width]
    key_heads = mixed_heads[:, group_width : 2 * group_width]
    value_heads = mixed_heads[:, 2 * group_width :]
    cols = block_cols[0].reshape(-1)
    counts = block_counts[0]
    attended_heads, lse = attention_forward(query_heads, key_heads, value_heads, cols, counts)
    attended = lax.all_to_all(attended_heads, "seq", split_axis=0, concat_axis=1, tiled=True)
    result = (
        feats.astype(jnp.float32) + jnp.dot(attended, w_out, preferred_element_type=jnp.float32)
    ).astype(jnp.bfloat16)
    w_out_rows = lax.dynamic_slice_in_dim(w_out, seq_at * group_width, group_width, 0)
    grad_heads = lax.dot_general(
        cotan_all, w_out_rows, (((1,), (1,)), ((), ())), preferred_element_type=jnp.float32
    ).astype(jnp.bfloat16)
    query_grad, key_grad, value_grad = attention_backward(
        query_heads, key_heads, value_heads, attended_heads, grad_heads, lse, cols, counts
    )
    grad_heads_mixed = jnp.concatenate([query_grad, key_grad, value_grad], axis=1)
    term_qkv = contract_rows(normed_all, grad_heads_mixed)
    term_out = contract_rows(attended_heads, cotan_all)
    qkv_cols = term_qkv.shape[1]
    summed, moved_grads = sum_and_exchange(
        jnp.concatenate([term_qkv, term_out.reshape(term_qkv.shape[0], -1)], axis=1),
        grad_heads_mixed,
    )
    grad_mixed = regroup_columns(moved_grads, seq_count, group_width)
    grad_normed = lax.dot_general(
        grad_mixed, w_qkv, (((1,), (1,)), ((), ())), preferred_element_type=jnp.float32
    )
    gained = grad_normed * gain[None, :]
    mean_one = jnp.mean(gained, axis=1, keepdims=True)
    mean_two = jnp.mean(gained * scaled, axis=1, keepdims=True)
    grad_feats = (
        cotan.astype(jnp.float32) + inverse * (gained - mean_one - scaled * mean_two)
    ).astype(jnp.bfloat16)
    term_qkv = summed[:, :qkv_cols]
    term_out = summed[:, qkv_cols:].reshape(term_out.shape)
    grad_qkv = regroup_columns(
        lax.all_to_all(term_qkv, "seq", split_axis=0, concat_axis=1, tiled=True),
        seq_count,
        group_width,
    )
    grad_out = term_out
    return (result, grad_feats, grad_qkv, grad_out)


def solution(mesh):
    in_specs = (
        P(("dp", "seq"), None),
        P(),
        P(),
        P(),
        P("dp", None, None),
        P("dp", None),
        P(("dp", "seq"), None),
    )
    out_specs = (P(("dp", "seq"), None), P(("dp", "seq"), None), P("seq", None), P("seq", None))
    return jax.shard_map(body, mesh=mesh, in_specs=in_specs, out_specs=out_specs, check_vma=False)
```

```python
import functools

import jax
import jax.numpy as jnp
from jax import lax
from jax.experimental import pallas as pl
from jax.experimental.pallas import tpu as pltpu
from jax.sharding import PartitionSpec as P

HD = 64
BLK = 128
MAXB = 8
SCALE = HD ** (-0.5)
NEG = -1e30

EPSILON = 1e-05


def layer_norm(feats, gain):
    values_f = feats.astype(jnp.float32)
    centred = values_f - jnp.mean(values_f, axis=1, keepdims=True)
    inverse = lax.rsqrt(jnp.mean(centred * centred, axis=1, keepdims=True) + EPSILON)
    scaled = centred * inverse
    return (scaled, inverse, (scaled * gain[None, :]).astype(jnp.bfloat16))


def contract_rows(left_cols, right_cols):
    return lax.dot_general(
        left_cols, right_cols, (((0,), (0,)), ((), ())), preferred_element_type=jnp.float32
    )


def head_masks(width):
    lane = lax.broadcasted_iota(jnp.int32, (1, width), 1)
    return [(lane >= h * HD) & (lane < (h + 1) * HD) for h in range(width // HD)]


def stack_heads(x, masks):
    return jnp.concatenate([jnp.where(m, x, jnp.zeros_like(x)) for m in masks], axis=0)


def unstack_heads(y, masks):
    out = y[0:BLK]
    for h in range(1, len(masks)):
        out = jnp.where(masks[h], y[h * BLK : (h + 1) * BLK], out)
    return out


def nt_dot(a, b):
    return lax.dot_general(a, b, (((1,), (1,)), ((), ())), preferred_element_type=jnp.float32)


def tn_dot(a, b):
    return lax.dot_general(a, b, (((0,), (0,)), ((), ())), preferred_element_type=jnp.float32)


def gather_blocks(ref, cols_ref, r):
    return jnp.concatenate(
        [
            ref[pl.ds(pl.multiple_of(cols_ref[r * MAXB + s] * BLK, BLK), BLK), :]
            for s in range(MAXB)
        ],
        axis=0,
    )


def live_lanes(cnt):
    return lax.broadcasted_iota(jnp.int32, (1, MAXB * BLK), 1) < cnt * BLK


def attn_fwd_kernel(cols_ref, counts_ref, q_ref, k_ref, v_ref, o_ref, lse_ref):
    width = q_ref.shape[1]
    nblk = q_ref.shape[0] // BLK
    masks = head_masks(width)
    rows = len(masks) * BLK

    def row_body(r, carry):
        row0 = pl.multiple_of(r * BLK, BLK)
        live = live_lanes(counts_ref[r])
        q2 = stack_heads(q_ref[pl.ds(row0, BLK), :], masks)
        sc = jnp.where(live, nt_dot(q2, gather_blocks(k_ref, cols_ref, r)) * SCALE, NEG)
        m = jnp.max(sc, axis=1, keepdims=True)
        e = jnp.where(live, jnp.exp(sc - m), 0.0)
        l = jnp.sum(e, axis=1, keepdims=True)
        p = (e * (1.0 / l)).astype(jnp.bfloat16)
        acc = jnp.dot(p, gather_blocks(v_ref, cols_ref, r), preferred_element_type=jnp.float32)
        o_ref[pl.ds(row0, BLK), :] = unstack_heads(acc, masks).astype(o_ref.dtype)
        lse_ref[pl.ds(pl.multiple_of(r * rows, rows), rows), :] = jnp.broadcast_to(
            m + jnp.log(l), (rows, lse_ref.shape[1])
        )
        return carry

    lax.fori_loop(0, nblk, row_body, 0)


def attn_bwd_kernel(
    cols_ref, counts_ref, q_ref, k_ref, v_ref, o_ref, do_ref, lse_ref, dq_ref, dk_ref, dv_ref, dk_acc, dv_acc
):
    width = q_ref.shape[1]
    nblk = q_ref.shape[0] // BLK
    masks = head_masks(width)
    rows = len(masks) * BLK
    dk_acc[...] = jnp.zeros_like(dk_acc)
    dv_acc[...] = jnp.zeros_like(dv_acc)

    def row_body(r, carry):
        row0 = pl.multiple_of(r * BLK, BLK)
        cnt = counts_ref[r]
        live = live_lanes(cnt)
        q2 = stack_heads(q_ref[pl.ds(row0, BLK), :], masks)
        do_blk = do_ref[pl.ds(row0, BLK), :]
        do2 = stack_heads(do_blk, masks)
        prod = o_ref[pl.ds(row0, BLK), :].astype(jnp.float32) * do_blk.astype(jnp.float32)
        delta = jnp.concatenate(
            [jnp.sum(jnp.where(m, prod, 0.0), axis=1, keepdims=True) for m in masks], axis=0
        )
        lse = lse_ref[pl.ds(pl.multiple_of(r * rows, rows), rows), :][:, 0:1]
        kc = gather_blocks(k_ref, cols_ref, r)
        vc = gather_blocks(v_ref, cols_ref, r)
        sc = nt_dot(q2, kc) * SCALE
        p = jnp.where(live, jnp.exp(sc - lse), 0.0).astype(jnp.bfloat16)
        dp = nt_dot(do2, vc)
        ds = (p.astype(jnp.float32) * (dp - delta) * SCALE).astype(jnp.bfloat16)
        dq = jnp.dot(ds, kc, preferred_element_type=jnp.float32)
        dq_ref[pl.ds(row0, BLK), :] = unstack_heads(dq, masks).astype(dq_ref.dtype)
        dkc = tn_dot(ds, q2)
        dvc = tn_dot(p, do2)
        for s in range(MAXB):

            @pl.when(s < cnt)
            def _():
                col0 = pl.multiple_of(cols_ref[r * MAXB + s] * BLK, BLK)
                dk_acc[pl.ds(col0, BLK), :] += dkc[s * BLK : (s + 1) * BLK]
                dv_acc[pl.ds(col0, BLK), :] += dvc[s * BLK : (s + 1) * BLK]

        return carry

    lax.fori_loop(0, nblk, row_body, 0)
    dk_ref[...] = dk_acc[...].astype(dk_ref.dtype)
    dv_ref[...] = dv_acc[...].astype(dv_ref.dtype)


def smem_spec():
    return pl.BlockSpec(memory_space=pltpu.SMEM)


def vmem_spec():
    return pl.BlockSpec(memory_space=pltpu.VMEM)


VMEM_LIMIT = 48 * 1024 * 1024


def attention_forward(q, k, v, cols, counts):
    n, width = q.shape
    rows = (width // HD) * BLK
    return pl.pallas_call(
        attn_fwd_kernel,
        out_shape=(
            jax.ShapeDtypeStruct((n, width), jnp.bfloat16),
            jax.ShapeDtypeStruct(((n // BLK) * rows, 128), jnp.float32),
        ),
        in_specs=[smem_spec(), smem_spec(), vmem_spec(), vmem_spec(), vmem_spec()],
        out_specs=(vmem_spec(), vmem_spec()),
        compiler_params=pltpu.CompilerParams(vmem_limit_bytes=VMEM_LIMIT),
    )(cols, counts, q, k, v)


def attention_backward(q, k, v, o, do, lse, cols, counts):
    n, width = q.shape
    return pl.pallas_call(
        attn_bwd_kernel,
        out_shape=tuple(jax.ShapeDtypeStruct((n, width), jnp.bfloat16) for _ in range(3)),
        in_specs=[smem_spec(), smem_spec()] + [vmem_spec()] * 6,
        out_specs=(vmem_spec(), vmem_spec(), vmem_spec()),
        scratch_shapes=[pltpu.VMEM((n, width), jnp.float32), pltpu.VMEM((n, width), jnp.float32)],
        compiler_params=pltpu.CompilerParams(vmem_limit_bytes=VMEM_LIMIT),
    )(cols, counts, q, k, v, o, do, lse)


def regroup_columns(moved, seq_count, group_width):
    rows = moved.shape[0]
    return (
        moved.reshape(rows, seq_count, 3, group_width)
        .transpose(0, 2, 1, 3)
        .reshape(rows, 3 * seq_count * group_width)
    )


MESH = pl.DeviceIdType.MESH


def exchange_kernel(
    n, m, x_ref, g_ref, a_ref, o_ref, moved_ref, att_ref, recv, gath, landed, att_landed, sems, a2a_sems
):
    me = lax.axis_index("dp")
    here = lax.axis_index("seq")
    barrier = pltpu.get_barrier_semaphore()
    for k in range(1, n):
        pl.semaphore_signal(
            barrier, inc=1, device_id={"dp": lax.rem(me + k, n)}, device_id_type=MESH
        )
    for k in range(1, m):
        pl.semaphore_signal(
            barrier, inc=1, device_id={"seq": lax.rem(here + k, m)}, device_id_type=MESH
        )
    pl.semaphore_wait(barrier, n - 1 + m - 1)

    def start_all(src_of, dst, send, arrive, axis, at, size):
        started = []
        for k in range(1, size):
            peer = lax.rem(at + k, size)
            copy = pltpu.make_async_remote_copy(
                src_ref=src_of(peer),
                dst_ref=dst.at[at],
                send_sem=send.at[peer],
                recv_sem=arrive.at[at],
                device_id={axis: peer},
                device_id_type=MESH,
            )
            copy.start()
            started.append(copy)
        return started

    def finish_all(started, src_of, dst, send, arrive, axis, at, size):
        for k in range(1, size):
            source = lax.rem(at + size - k, size)
            pltpu.make_async_remote_copy(
                src_ref=src_of(source),
                dst_ref=dst.at[source],
                send_sem=send.at[source],
                recv_sem=arrive.at[source],
                device_id={axis: source},
                device_id_type=MESH,
            ).wait_recv()
        for copy in started:
            copy.wait_send()

    parts = g_ref.shape[2] // BLK
    group = BLK * m

    def part_copy(t, peer, sender, target):
        return pltpu.make_async_remote_copy(
            src_ref=g_ref.at[peer, :, pl.ds(t * BLK, BLK)],
            dst_ref=landed.at[:, pl.ds(pl.multiple_of(t * group + sender * BLK, BLK), BLK)],
            send_sem=a2a_sems.at[0, t, peer],
            recv_sem=a2a_sems.at[1, t, sender],
            device_id={"seq": target},
            device_id_type=MESH,
        )

    width = a_ref.shape[2]

    def att_copy(peer, sender, target):
        return pltpu.make_async_remote_copy(
            src_ref=a_ref.at[peer],
            dst_ref=att_landed.at[:, pl.ds(pl.multiple_of(sender * width, width), width)],
            send_sem=a2a_sems.at[0, parts, peer],
            recv_sem=a2a_sems.at[1, parts, sender],
            device_id={"seq": target},
            device_id_type=MESH,
        )

    a2a_started = []
    for k in range(1, m):
        peer = lax.rem(here + k, m)
        copy = att_copy(peer, here, peer)
        copy.start()
        a2a_started.append(copy)
    for k in range(1, m):
        peer = lax.rem(here + k, m)
        for t in range(parts):
            copy = part_copy(t, peer, here, peer)
            copy.start()
            a2a_started.append(copy)
    rs = (lambda peer: x_ref.at[peer], recv, sems.at[0], sems.at[1], "dp", me, n)
    finish_all(start_all(*rs), *rs)
    total = x_ref[me]
    for k in range(1, n):
        total = total + recv[lax.rem(me + k, n)]
    gath[me] = total.astype(gath.dtype)
    ag = (lambda peer: gath.at[me], gath, sems.at[2], sems.at[3], "dp", me, n)
    finish_all(start_all(*ag), *ag)
    o_ref[...] = gath[...]
    own = g_ref[here]
    for t in range(parts):
        landed[:, pl.ds(pl.multiple_of(t * group + here * BLK, BLK), BLK)] = own[
            :, t * BLK : (t + 1) * BLK
        ]
    att_landed[:, pl.ds(pl.multiple_of(here * width, width), width)] = a_ref[here]
    for k in range(1, m):
        source = lax.rem(here + m - k, m)
        att_copy(source, source, source).wait_recv()
        for t in range(parts):
            part_copy(t, source, source, source).wait_recv()
    for copy in a2a_started:
        copy.wait_send()
    moved_ref[...] = landed[...]
    att_ref[...] = att_landed[...]


def sum_and_exchange(term, grads, attended_heads):
    n = lax.axis_size("dp")
    m = lax.axis_size("seq")
    rows, cols = term.shape
    chunked = term.reshape(n, rows // n, cols)
    pieces = grads.reshape(m, grads.shape[0] // m, grads.shape[1])
    att_pieces = attended_heads.reshape(m, attended_heads.shape[0] // m, attended_heads.shape[1])
    parts = grads.shape[1] // BLK
    final = (pieces.shape[1], parts * m * BLK)
    att_final = (att_pieces.shape[1], m * att_pieces.shape[2])
    out, moved, attended = pl.pallas_call(
        functools.partial(exchange_kernel, n, m),
        out_shape=(
            jax.ShapeDtypeStruct(chunked.shape, jnp.bfloat16),
            jax.ShapeDtypeStruct(final, pieces.dtype),
            jax.ShapeDtypeStruct(att_final, att_pieces.dtype),
        ),
        in_specs=[vmem_spec(), vmem_spec(), vmem_spec()],
        out_specs=(vmem_spec(), vmem_spec(), vmem_spec()),
        scratch_shapes=[
            pltpu.VMEM(chunked.shape, jnp.float32),
            pltpu.VMEM(chunked.shape, jnp.bfloat16),
            pltpu.VMEM(final, pieces.dtype),
            pltpu.VMEM(att_final, att_pieces.dtype),
            pltpu.SemaphoreType.DMA((4, n)),
            pltpu.SemaphoreType.DMA((2, parts + 1, m)),
        ],
        compiler_params=pltpu.CompilerParams(
            collective_id=0, has_side_effects=True, vmem_limit_bytes=VMEM_LIMIT
        ),
    )(chunked, pieces, att_pieces)
    return out.reshape(rows, cols), moved, attended


def body(feats, gain, w_qkv, w_out, block_cols, block_counts, cotan):
    model_width = feats.shape[1]
    seq_count = lax.axis_size("seq")
    group_width = model_width // seq_count
    seq_at = lax.axis_index("seq")
    scaled, inverse, normed = layer_norm(feats, gain)
    normed_all = lax.all_gather(normed, "seq", axis=0, tiled=True)
    cotan_all = lax.all_gather(cotan, "seq", axis=0, tiled=True)
    w_heads = jnp.concatenate(
        [
            lax.dynamic_slice_in_dim(w_qkv, j * model_width + seq_at * group_width, group_width, 1)
            for j in range(3)
        ],
        axis=1,
    )
    mixed_heads = jnp.dot(normed_all, w_heads, preferred_element_type=jnp.float32).astype(
        jnp.bfloat16
    )
    query_heads = mixed_heads[:, :group_width]
    key_heads = mixed_heads[:, group_width : 2 * group_width]
    value_heads = mixed_heads[:, 2 * group_width :]
    cols = block_cols[0].reshape(-1)
    counts = block_counts[0]
    attended_heads, lse = attention_forward(query_heads, key_heads, value_heads, cols, counts)
    w_out_rows = lax.dynamic_slice_in_dim(w_out, seq_at * group_width, group_width, 0)
    grad_heads = lax.dot_general(
        cotan_all, w_out_rows, (((1,), (1,)), ((), ())), preferred_element_type=jnp.float32
    ).astype(jnp.bfloat16)
    query_grad, key_grad, value_grad = attention_backward(
        query_heads, key_heads, value_heads, attended_heads, grad_heads, lse, cols, counts
    )
    grad_heads_mixed = jnp.concatenate([query_grad, key_grad, value_grad], axis=1)
    term_qkv = contract_rows(normed_all, grad_heads_mixed)
    term_out = contract_rows(attended_heads, cotan_all)
    qkv_cols = term_qkv.shape[1]
    summed, moved_grads, attended = sum_and_exchange(
        jnp.concatenate([term_qkv, term_out.reshape(term_qkv.shape[0], -1)], axis=1),
        grad_heads_mixed,
        attended_heads,
    )
    result = (
        feats.astype(jnp.float32) + jnp.dot(attended, w_out, preferred_element_type=jnp.float32)
    ).astype(jnp.bfloat16)
    grad_mixed = moved_grads
    grad_normed = lax.dot_general(
        grad_mixed, w_qkv, (((1,), (1,)), ((), ())), preferred_element_type=jnp.float32
    )
    gained = grad_normed * gain[None, :]
    mean_one = jnp.mean(gained, axis=1, keepdims=True)
    mean_two = jnp.mean(gained * scaled, axis=1, keepdims=True)
    grad_feats = (
        cotan.astype(jnp.float32) + inverse * (gained - mean_one - scaled * mean_two)
    ).astype(jnp.bfloat16)
    term_qkv = summed[:, :qkv_cols]
    term_out = summed[:, qkv_cols:].reshape(term_out.shape)
    grad_qkv = regroup_columns(
        lax.all_to_all(term_qkv, "seq", split_axis=0, concat_axis=1, tiled=True),
        seq_count,
        group_width,
    )
    grad_out = term_out
    return (result, grad_feats, grad_qkv, grad_out)


def solution(mesh):
    in_specs = (
        P(("dp", "seq"), None),
        P(),
        P(),
        P(),
        P("dp", None, None),
        P("dp", None),
        P(("dp", "seq"), None),
    )
    out_specs = (P(("dp", "seq"), None), P(("dp", "seq"), None), P("seq", None), P("seq", None))
    return jax.shard_map(body, mesh=mesh, in_specs=in_specs, out_specs=out_specs, check_vma=False)
```

```python
import functools

import jax
import jax.numpy as jnp
from jax import lax
from jax.experimental import pallas as pl
from jax.experimental.pallas import tpu as pltpu
from jax.sharding import PartitionSpec as P

HD = 64
BLK = 128
MAXB = 8
SCALE = HD ** (-0.5)
NEG = -1e30

EPSILON = 1e-05


def layer_norm(feats, gain):
    values_f = feats.astype(jnp.float32)
    centred = values_f - jnp.mean(values_f, axis=1, keepdims=True)
    inverse = lax.rsqrt(jnp.mean(centred * centred, axis=1, keepdims=True) + EPSILON)
    scaled = centred * inverse
    return (scaled, inverse, (scaled * gain[None, :]).astype(jnp.bfloat16))


def contract_rows(left_cols, right_cols):
    return lax.dot_general(
        left_cols, right_cols, (((0,), (0,)), ((), ())), preferred_element_type=jnp.float32
    )


def head_masks(width):
    lane = lax.broadcasted_iota(jnp.int32, (1, width), 1)
    return [(lane >= h * HD) & (lane < (h + 1) * HD) for h in range(width // HD)]


def stack_heads(x, masks):
    return jnp.concatenate([jnp.where(m, x, jnp.zeros_like(x)) for m in masks], axis=0)


def unstack_heads(y, masks):
    out = y[0:BLK]
    for h in range(1, len(masks)):
        out = jnp.where(masks[h], y[h * BLK : (h + 1) * BLK], out)
    return out


def nt_dot(a, b):
    return lax.dot_general(a, b, (((1,), (1,)), ((), ())), preferred_element_type=jnp.float32)


def tn_dot(a, b):
    return lax.dot_general(a, b, (((0,), (0,)), ((), ())), preferred_element_type=jnp.float32)


SLOT_TIERS = (2, 4, MAXB)


def gather_blocks(ref, cols_ref, r, slots):
    return jnp.concatenate(
        [
            ref[pl.ds(pl.multiple_of(cols_ref[r * MAXB + s] * BLK, BLK), BLK), :]
            for s in range(slots)
        ],
        axis=0,
    )


def live_lanes(cnt, slots):
    return lax.broadcasted_iota(jnp.int32, (1, slots * BLK), 1) < cnt * BLK


def by_tier(cnt, body):
    low = 0
    for slots in SLOT_TIERS:
        pl.when((cnt > low) & (cnt <= slots))(functools.partial(body, slots))
        low = slots


def attn_fwd_kernel(cols_ref, counts_ref, q_ref, k_ref, v_ref, o_ref, lse_ref):
    width = q_ref.shape[1]
    nblk = q_ref.shape[0] // BLK
    masks = head_masks(width)
    rows = len(masks) * BLK

    def row_body(r, carry):
        row0 = pl.multiple_of(r * BLK, BLK)
        cnt = counts_ref[r]

        def tier(slots):
            live = live_lanes(cnt, slots)
            q2 = stack_heads(q_ref[pl.ds(row0, BLK), :], masks)
            kc = gather_blocks(k_ref, cols_ref, r, slots)
            sc = jnp.where(live, nt_dot(q2, kc) * SCALE, NEG)
            m = jnp.max(sc, axis=1, keepdims=True)
            e = jnp.where(live, jnp.exp(sc - m), 0.0)
            l = jnp.sum(e, axis=1, keepdims=True)
            p = (e * (1.0 / l)).astype(jnp.bfloat16)
            vc = gather_blocks(v_ref, cols_ref, r, slots)
            acc = jnp.dot(p, vc, preferred_element_type=jnp.float32)
            o_ref[pl.ds(row0, BLK), :] = unstack_heads(acc, masks).astype(o_ref.dtype)
            lse_ref[pl.ds(pl.multiple_of(r * rows, rows), rows), :] = jnp.broadcast_to(
                m + jnp.log(l), (rows, lse_ref.shape[1])
            )

        by_tier(cnt, tier)
        return carry

    lax.fori_loop(0, nblk, row_body, 0)


def attn_bwd_kernel(
    cols_ref, counts_ref, q_ref, k_ref, v_ref, o_ref, do_ref, lse_ref, dq_ref, dk_ref, dv_ref, dk_acc, dv_acc
):
    width = q_ref.shape[1]
    nblk = q_ref.shape[0] // BLK
    masks = head_masks(width)
    rows = len(masks) * BLK
    dk_acc[...] = jnp.zeros_like(dk_acc)
    dv_acc[...] = jnp.zeros_like(dv_acc)

    def row_body(r, carry):
        row0 = pl.multiple_of(r * BLK, BLK)
        cnt = counts_ref[r]

        def tier(slots):
            live = live_lanes(cnt, slots)
            q2 = stack_heads(q_ref[pl.ds(row0, BLK), :], masks)
            do_blk = do_ref[pl.ds(row0, BLK), :]
            do2 = stack_heads(do_blk, masks)
            prod = o_ref[pl.ds(row0, BLK), :].astype(jnp.float32) * do_blk.astype(jnp.float32)
            delta = jnp.concatenate(
                [jnp.sum(jnp.where(m, prod, 0.0), axis=1, keepdims=True) for m in masks], axis=0
            )
            lse = lse_ref[pl.ds(pl.multiple_of(r * rows, rows), rows), :][:, 0:1]
            kc = gather_blocks(k_ref, cols_ref, r, slots)
            vc = gather_blocks(v_ref, cols_ref, r, slots)
            sc = nt_dot(q2, kc) * SCALE
            p = jnp.where(live, jnp.exp(sc - lse), 0.0).astype(jnp.bfloat16)
            dp = nt_dot(do2, vc)
            ds = (p.astype(jnp.float32) * (dp - delta) * SCALE).astype(jnp.bfloat16)
            dq = jnp.dot(ds, kc, preferred_element_type=jnp.float32)
            dq_ref[pl.ds(row0, BLK), :] = unstack_heads(dq, masks).astype(dq_ref.dtype)
            dkc = tn_dot(ds, q2)
            dvc = tn_dot(p, do2)
            for s in range(slots):

                @pl.when(s < cnt)
                def _():
                    col0 = pl.multiple_of(cols_ref[r * MAXB + s] * BLK, BLK)
                    dk_acc[pl.ds(col0, BLK), :] += dkc[s * BLK : (s + 1) * BLK]
                    dv_acc[pl.ds(col0, BLK), :] += dvc[s * BLK : (s + 1) * BLK]

        by_tier(cnt, tier)
        return carry

    lax.fori_loop(0, nblk, row_body, 0)
    dk_ref[...] = dk_acc[...].astype(dk_ref.dtype)
    dv_ref[...] = dv_acc[...].astype(dv_ref.dtype)


def smem_spec():
    return pl.BlockSpec(memory_space=pltpu.SMEM)


def vmem_spec():
    return pl.BlockSpec(memory_space=pltpu.VMEM)


VMEM_LIMIT = 48 * 1024 * 1024


def attention_forward(q, k, v, cols, counts):
    n, width = q.shape
    rows = (width // HD) * BLK
    return pl.pallas_call(
        attn_fwd_kernel,
        out_shape=(
            jax.ShapeDtypeStruct((n, width), jnp.bfloat16),
            jax.ShapeDtypeStruct(((n // BLK) * rows, 128), jnp.float32),
        ),
        in_specs=[smem_spec(), smem_spec(), vmem_spec(), vmem_spec(), vmem_spec()],
        out_specs=(vmem_spec(), vmem_spec()),
        compiler_params=pltpu.CompilerParams(vmem_limit_bytes=VMEM_LIMIT),
    )(cols, counts, q, k, v)


def attention_backward(q, k, v, o, do, lse, cols, counts):
    n, width = q.shape
    return pl.pallas_call(
        attn_bwd_kernel,
        out_shape=tuple(jax.ShapeDtypeStruct((n, width), jnp.bfloat16) for _ in range(3)),
        in_specs=[smem_spec(), smem_spec()] + [vmem_spec()] * 6,
        out_specs=(vmem_spec(), vmem_spec(), vmem_spec()),
        scratch_shapes=[pltpu.VMEM((n, width), jnp.float32), pltpu.VMEM((n, width), jnp.float32)],
        compiler_params=pltpu.CompilerParams(vmem_limit_bytes=VMEM_LIMIT),
    )(cols, counts, q, k, v, o, do, lse)


def regroup_columns(moved, seq_count, group_width):
    rows = moved.shape[0]
    return (
        moved.reshape(rows, seq_count, 3, group_width)
        .transpose(0, 2, 1, 3)
        .reshape(rows, 3 * seq_count * group_width)
    )


MESH = pl.DeviceIdType.MESH


def exchange_kernel(
    n, m, x_ref, g_ref, a_ref, o_ref, moved_ref, att_ref, recv, gath, landed, att_landed, sems, a2a_sems
):
    me = lax.axis_index("dp")
    here = lax.axis_index("seq")
    barrier = pltpu.get_barrier_semaphore()
    for k in range(1, n):
        pl.semaphore_signal(
            barrier, inc=1, device_id={"dp": lax.rem(me + k, n)}, device_id_type=MESH
        )
    for k in range(1, m):
        pl.semaphore_signal(
            barrier, inc=1, device_id={"seq": lax.rem(here + k, m)}, device_id_type=MESH
        )
    pl.semaphore_wait(barrier, n - 1 + m - 1)

    def start_all(src_of, dst, send, arrive, axis, at, size):
        started = []
        for k in range(1, size):
            peer = lax.rem(at + k, size)
            copy = pltpu.make_async_remote_copy(
                src_ref=src_of(peer),
                dst_ref=dst.at[at],
                send_sem=send.at[peer],
                recv_sem=arrive.at[at],
                device_id={axis: peer},
                device_id_type=MESH,
            )
            copy.start()
            started.append(copy)
        return started

    def finish_all(started, src_of, dst, send, arrive, axis, at, size):
        for k in range(1, size):
            source = lax.rem(at + size - k, size)
            pltpu.make_async_remote_copy(
                src_ref=src_of(source),
                dst_ref=dst.at[source],
                send_sem=send.at[source],
                recv_sem=arrive.at[source],
                device_id={axis: source},
                device_id_type=MESH,
            ).wait_recv()
        for copy in started:
            copy.wait_send()

    parts = g_ref.shape[2] // BLK
    group = BLK * m

    def part_copy(t, peer, sender, target):
        return pltpu.make_async_remote_copy(
            src_ref=g_ref.at[peer, :, pl.ds(t * BLK, BLK)],
            dst_ref=landed.at[:, pl.ds(pl.multiple_of(t * group + sender * BLK, BLK), BLK)],
            send_sem=a2a_sems.at[0, t, peer],
            recv_sem=a2a_sems.at[1, t, sender],
            device_id={"seq": target},
            device_id_type=MESH,
        )

    width = a_ref.shape[2]

    def att_copy(peer, sender, target):
        return pltpu.make_async_remote_copy(
            src_ref=a_ref.at[peer],
            dst_ref=att_landed.at[:, pl.ds(pl.multiple_of(sender * width, width), width)],
            send_sem=a2a_sems.at[0, parts, peer],
            recv_sem=a2a_sems.at[1, parts, sender],
            device_id={"seq": target},
            device_id_type=MESH,
        )

    a2a_started = []
    for k in range(1, m):
        peer = lax.rem(here + k, m)
        copy = att_copy(peer, here, peer)
        copy.start()
        a2a_started.append(copy)
    for k in range(1, m):
        peer = lax.rem(here + k, m)
        for t in range(parts):
            copy = part_copy(t, peer, here, peer)
            copy.start()
            a2a_started.append(copy)
    rs = (lambda peer: x_ref.at[peer], recv, sems.at[0], sems.at[1], "dp", me, n)
    finish_all(start_all(*rs), *rs)
    total = x_ref[me]
    for k in range(1, n):
        total = total + recv[lax.rem(me + k, n)]
    gath[me] = total.astype(gath.dtype)
    ag = (lambda peer: gath.at[me], gath, sems.at[2], sems.at[3], "dp", me, n)
    finish_all(start_all(*ag), *ag)
    o_ref[...] = gath[...]
    own = g_ref[here]
    for t in range(parts):
        landed[:, pl.ds(pl.multiple_of(t * group + here * BLK, BLK), BLK)] = own[
            :, t * BLK : (t + 1) * BLK
        ]
    att_landed[:, pl.ds(pl.multiple_of(here * width, width), width)] = a_ref[here]
    for k in range(1, m):
        source = lax.rem(here + m - k, m)
        att_copy(source, source, source).wait_recv()
        for t in range(parts):
            part_copy(t, source, source, source).wait_recv()
    for copy in a2a_started:
        copy.wait_send()
    moved_ref[...] = landed[...]
    att_ref[...] = att_landed[...]


def sum_and_exchange(term, grads, attended_heads):
    n = lax.axis_size("dp")
    m = lax.axis_size("seq")
    rows, cols = term.shape
    chunked = term.reshape(n, rows // n, cols)
    pieces = grads.reshape(m, grads.shape[0] // m, grads.shape[1])
    att_pieces = attended_heads.reshape(m, attended_heads.shape[0] // m, attended_heads.shape[1])
    parts = grads.shape[1] // BLK
    final = (pieces.shape[1], parts * m * BLK)
    att_final = (att_pieces.shape[1], m * att_pieces.shape[2])
    out, moved, attended = pl.pallas_call(
        functools.partial(exchange_kernel, n, m),
        out_shape=(
            jax.ShapeDtypeStruct(chunked.shape, jnp.bfloat16),
            jax.ShapeDtypeStruct(final, pieces.dtype),
            jax.ShapeDtypeStruct(att_final, att_pieces.dtype),
        ),
        in_specs=[vmem_spec(), vmem_spec(), vmem_spec()],
        out_specs=(vmem_spec(), vmem_spec(), vmem_spec()),
        scratch_shapes=[
            pltpu.VMEM(chunked.shape, jnp.float32),
            pltpu.VMEM(chunked.shape, jnp.bfloat16),
            pltpu.VMEM(final, pieces.dtype),
            pltpu.VMEM(att_final, att_pieces.dtype),
            pltpu.SemaphoreType.DMA((4, n)),
            pltpu.SemaphoreType.DMA((2, parts + 1, m)),
        ],
        compiler_params=pltpu.CompilerParams(
            collective_id=0, has_side_effects=True, vmem_limit_bytes=VMEM_LIMIT
        ),
    )(chunked, pieces, att_pieces)
    return out.reshape(rows, cols), moved, attended


def body(feats, gain, w_qkv, w_out, block_cols, block_counts, cotan):
    model_width = feats.shape[1]
    seq_count = lax.axis_size("seq")
    group_width = model_width // seq_count
    seq_at = lax.axis_index("seq")
    scaled, inverse, normed = layer_norm(feats, gain)
    normed_all = lax.all_gather(normed, "seq", axis=0, tiled=True)
    cotan_all = lax.all_gather(cotan, "seq", axis=0, tiled=True)
    w_heads = jnp.concatenate(
        [
            lax.dynamic_slice_in_dim(w_qkv, j * model_width + seq_at * group_width, group_width, 1)
            for j in range(3)
        ],
        axis=1,
    )
    mixed_heads = jnp.dot(normed_all, w_heads, preferred_element_type=jnp.float32).astype(
        jnp.bfloat16
    )
    query_heads = mixed_heads[:, :group_width]
    key_heads = mixed_heads[:, group_width : 2 * group_width]
    value_heads = mixed_heads[:, 2 * group_width :]
    cols = block_cols[0].reshape(-1)
    counts = block_counts[0]
    attended_heads, lse = attention_forward(query_heads, key_heads, value_heads, cols, counts)
    w_out_rows = lax.dynamic_slice_in_dim(w_out, seq_at * group_width, group_width, 0)
    grad_heads = lax.dot_general(
        cotan_all, w_out_rows, (((1,), (1,)), ((), ())), preferred_element_type=jnp.float32
    ).astype(jnp.bfloat16)
    query_grad, key_grad, value_grad = attention_backward(
        query_heads, key_heads, value_heads, attended_heads, grad_heads, lse, cols, counts
    )
    grad_heads_mixed = jnp.concatenate([query_grad, key_grad, value_grad], axis=1)
    term_qkv = contract_rows(normed_all, grad_heads_mixed)
    term_out = contract_rows(attended_heads, cotan_all)
    qkv_cols = term_qkv.shape[1]
    summed, moved_grads, attended = sum_and_exchange(
        jnp.concatenate([term_qkv, term_out.reshape(term_qkv.shape[0], -1)], axis=1),
        grad_heads_mixed,
        attended_heads,
    )
    result = (
        feats.astype(jnp.float32) + jnp.dot(attended, w_out, preferred_element_type=jnp.float32)
    ).astype(jnp.bfloat16)
    grad_mixed = moved_grads
    grad_normed = lax.dot_general(
        grad_mixed, w_qkv, (((1,), (1,)), ((), ())), preferred_element_type=jnp.float32
    )
    gained = grad_normed * gain[None, :]
    mean_one = jnp.mean(gained, axis=1, keepdims=True)
    mean_two = jnp.mean(gained * scaled, axis=1, keepdims=True)
    grad_feats = (
        cotan.astype(jnp.float32) + inverse * (gained - mean_one - scaled * mean_two)
    ).astype(jnp.bfloat16)
    term_qkv = summed[:, :qkv_cols]
    term_out = summed[:, qkv_cols:].reshape(term_out.shape)
    grad_qkv = regroup_columns(
        lax.all_to_all(term_qkv, "seq", split_axis=0, concat_axis=1, tiled=True),
        seq_count,
        group_width,
    )
    grad_out = term_out
    return (result, grad_feats, grad_qkv, grad_out)


def solution(mesh):
    in_specs = (
        P(("dp", "seq"), None),
        P(),
        P(),
        P(),
        P("dp", None, None),
        P("dp", None),
        P(("dp", "seq"), None),
    )
    out_specs = (P(("dp", "seq"), None), P(("dp", "seq"), None), P("seq", None), P("seq", None))
    return jax.shard_map(body, mesh=mesh, in_specs=in_specs, out_specs=out_specs, check_vma=False)
```

```python
import functools

import jax
import jax.numpy as jnp
from jax import lax
from jax.experimental import pallas as pl
from jax.experimental.pallas import tpu as pltpu
from jax.sharding import PartitionSpec as P

HD = 64
BLK = 128
MAXB = 8
SCALE = HD ** (-0.5)
NEG = -1e30

EPSILON = 1e-05


def layer_norm(feats, gain):
    values_f = feats.astype(jnp.float32)
    centred = values_f - jnp.mean(values_f, axis=1, keepdims=True)
    inverse = lax.rsqrt(jnp.mean(centred * centred, axis=1, keepdims=True) + EPSILON)
    scaled = centred * inverse
    return (scaled, inverse, (scaled * gain[None, :]).astype(jnp.bfloat16))


def contract_rows(left_cols, right_cols):
    return lax.dot_general(
        left_cols, right_cols, (((0,), (0,)), ((), ())), preferred_element_type=jnp.float32
    )


def head_masks(width):
    lane = lax.broadcasted_iota(jnp.int32, (1, width), 1)
    return [(lane >= h * HD) & (lane < (h + 1) * HD) for h in range(width // HD)]


def stack_heads(x, masks):
    return jnp.concatenate([jnp.where(m, x, jnp.zeros_like(x)) for m in masks], axis=0)


def unstack_heads(y, masks):
    out = y[0:BLK]
    for h in range(1, len(masks)):
        out = jnp.where(masks[h], y[h * BLK : (h + 1) * BLK], out)
    return out


def nt_dot(a, b):
    return lax.dot_general(a, b, (((1,), (1,)), ((), ())), preferred_element_type=jnp.float32)


def tn_dot(a, b):
    return lax.dot_general(a, b, (((0,), (0,)), ((), ())), preferred_element_type=jnp.float32)


SLOT_TIERS = (2, 4, MAXB)


def gather_blocks(ref, cols_ref, r, slots):
    return jnp.concatenate(
        [
            ref[pl.ds(pl.multiple_of(cols_ref[r * MAXB + s] * BLK, BLK), BLK), :]
            for s in range(slots)
        ],
        axis=0,
    )


def live_lanes(cnt, slots):
    return lax.broadcasted_iota(jnp.int32, (1, slots * BLK), 1) < cnt * BLK


def by_tier(cnt, body):
    low = 0
    for slots in SLOT_TIERS:
        pl.when((cnt > low) & (cnt <= slots))(functools.partial(body, slots))
        low = slots


def attn_fwd_kernel(cols_ref, counts_ref, q_ref, k_ref, v_ref, o_ref, lse_ref):
    width = q_ref.shape[1]
    nblk = q_ref.shape[0] // BLK
    masks = head_masks(width)
    rows = len(masks) * BLK

    def row_body(r, carry):
        row0 = pl.multiple_of(r * BLK, BLK)
        cnt = counts_ref[r]

        def tier(slots):
            live = live_lanes(cnt, slots)
            q2 = stack_heads(q_ref[pl.ds(row0, BLK), :], masks)
            kc = gather_blocks(k_ref, cols_ref, r, slots)
            sc = jnp.where(live, nt_dot(q2, kc) * SCALE, NEG)
            m = jnp.max(sc, axis=1, keepdims=True)
            e = jnp.where(live, jnp.exp(sc - m), 0.0)
            l = jnp.sum(e, axis=1, keepdims=True)
            p = (e * (1.0 / l)).astype(jnp.bfloat16)
            vc = gather_blocks(v_ref, cols_ref, r, slots)
            acc = jnp.dot(p, vc, preferred_element_type=jnp.float32)
            o_ref[pl.ds(row0, BLK), :] = unstack_heads(acc, masks).astype(o_ref.dtype)
            lse_ref[pl.ds(pl.multiple_of(r * rows, rows), rows), :] = jnp.broadcast_to(
                m + jnp.log(l), (rows, lse_ref.shape[1])
            )

        by_tier(cnt, tier)
        return carry

    lax.fori_loop(0, nblk, row_body, 0)


def attn_bwd_kernel(
    cols_ref,
    counts_ref,
    q_ref,
    k_ref,
    v_ref,
    o_ref,
    cotan_ref,
    w_ref,
    lse_ref,
    dq_ref,
    dk_ref,
    dv_ref,
    dk_acc,
    dv_acc,
):
    width = q_ref.shape[1]
    nblk = q_ref.shape[0] // BLK
    masks = head_masks(width)
    rows = len(masks) * BLK
    dk_acc[...] = jnp.zeros_like(dk_acc)
    dv_acc[...] = jnp.zeros_like(dv_acc)

    def row_body(r, carry):
        row0 = pl.multiple_of(r * BLK, BLK)
        cnt = counts_ref[r]
        do_blk = nt_dot(cotan_ref[pl.ds(row0, BLK), :], w_ref[...]).astype(jnp.bfloat16)

        def tier(slots):
            live = live_lanes(cnt, slots)
            q2 = stack_heads(q_ref[pl.ds(row0, BLK), :], masks)
            do2 = stack_heads(do_blk, masks)
            prod = o_ref[pl.ds(row0, BLK), :].astype(jnp.float32) * do_blk.astype(jnp.float32)
            delta = jnp.concatenate(
                [jnp.sum(jnp.where(m, prod, 0.0), axis=1, keepdims=True) for m in masks], axis=0
            )
            lse = lse_ref[pl.ds(pl.multiple_of(r * rows, rows), rows), :][:, 0:1]
            kc = gather_blocks(k_ref, cols_ref, r, slots)
            vc = gather_blocks(v_ref, cols_ref, r, slots)
            sc = nt_dot(q2, kc) * SCALE
            p = jnp.where(live, jnp.exp(sc - lse), 0.0).astype(jnp.bfloat16)
            dp = nt_dot(do2, vc)
            ds = (p.astype(jnp.float32) * (dp - delta) * SCALE).astype(jnp.bfloat16)
            dq = jnp.dot(ds, kc, preferred_element_type=jnp.float32)
            dq_ref[pl.ds(row0, BLK), :] = unstack_heads(dq, masks).astype(dq_ref.dtype)
            dkc = tn_dot(ds, q2)
            dvc = tn_dot(p, do2)
            for s in range(slots):

                @pl.when(s < cnt)
                def _():
                    col0 = pl.multiple_of(cols_ref[r * MAXB + s] * BLK, BLK)
                    dk_acc[pl.ds(col0, BLK), :] += dkc[s * BLK : (s + 1) * BLK]
                    dv_acc[pl.ds(col0, BLK), :] += dvc[s * BLK : (s + 1) * BLK]

        by_tier(cnt, tier)
        return carry

    lax.fori_loop(0, nblk, row_body, 0)
    dk_ref[...] = dk_acc[...].astype(dk_ref.dtype)
    dv_ref[...] = dv_acc[...].astype(dv_ref.dtype)


def smem_spec():
    return pl.BlockSpec(memory_space=pltpu.SMEM)


def vmem_spec():
    return pl.BlockSpec(memory_space=pltpu.VMEM)


VMEM_LIMIT = 48 * 1024 * 1024


def attention_forward(q, k, v, cols, counts):
    n, width = q.shape
    rows = (width // HD) * BLK
    return pl.pallas_call(
        attn_fwd_kernel,
        out_shape=(
            jax.ShapeDtypeStruct((n, width), jnp.bfloat16),
            jax.ShapeDtypeStruct(((n // BLK) * rows, 128), jnp.float32),
        ),
        in_specs=[smem_spec(), smem_spec(), vmem_spec(), vmem_spec(), vmem_spec()],
        out_specs=(vmem_spec(), vmem_spec()),
        compiler_params=pltpu.CompilerParams(vmem_limit_bytes=VMEM_LIMIT),
    )(cols, counts, q, k, v)


def attention_backward(q, k, v, o, cotan_all, w_out_rows, lse, cols, counts):
    n, width = q.shape
    return pl.pallas_call(
        attn_bwd_kernel,
        out_shape=tuple(jax.ShapeDtypeStruct((n, width), jnp.bfloat16) for _ in range(3)),
        in_specs=[smem_spec(), smem_spec()] + [vmem_spec()] * 7,
        out_specs=(vmem_spec(), vmem_spec(), vmem_spec()),
        scratch_shapes=[pltpu.VMEM((n, width), jnp.float32), pltpu.VMEM((n, width), jnp.float32)],
        compiler_params=pltpu.CompilerParams(vmem_limit_bytes=VMEM_LIMIT),
    )(cols, counts, q, k, v, o, cotan_all, w_out_rows, lse)


def regroup_columns(moved, seq_count, group_width):
    rows = moved.shape[0]
    return (
        moved.reshape(rows, seq_count, 3, group_width)
        .transpose(0, 2, 1, 3)
        .reshape(rows, 3 * seq_count * group_width)
    )


MESH = pl.DeviceIdType.MESH


def exchange_kernel(
    n, m, x_ref, g_ref, a_ref, o_ref, moved_ref, att_ref, recv, gath, landed, att_landed, sems, a2a_sems
):
    me = lax.axis_index("dp")
    here = lax.axis_index("seq")
    barrier = pltpu.get_barrier_semaphore()
    for k in range(1, n):
        pl.semaphore_signal(
            barrier, inc=1, device_id={"dp": lax.rem(me + k, n)}, device_id_type=MESH
        )
    for k in range(1, m):
        pl.semaphore_signal(
            barrier, inc=1, device_id={"seq": lax.rem(here + k, m)}, device_id_type=MESH
        )
    pl.semaphore_wait(barrier, n - 1 + m - 1)

    def start_all(src_of, dst, send, arrive, axis, at, size):
        started = []
        for k in range(1, size):
            peer = lax.rem(at + k, size)
            copy = pltpu.make_async_remote_copy(
                src_ref=src_of(peer),
                dst_ref=dst.at[at],
                send_sem=send.at[peer],
                recv_sem=arrive.at[at],
                device_id={axis: peer},
                device_id_type=MESH,
            )
            copy.start()
            started.append(copy)
        return started

    def finish_all(started, src_of, dst, send, arrive, axis, at, size):
        for k in range(1, size):
            source = lax.rem(at + size - k, size)
            pltpu.make_async_remote_copy(
                src_ref=src_of(source),
                dst_ref=dst.at[source],
                send_sem=send.at[source],
                recv_sem=arrive.at[source],
                device_id={axis: source},
                device_id_type=MESH,
            ).wait_recv()
        for copy in started:
            copy.wait_send()

    parts = g_ref.shape[2] // BLK
    group = BLK * m

    def part_copy(t, peer, sender, target):
        return pltpu.make_async_remote_copy(
            src_ref=g_ref.at[peer, :, pl.ds(t * BLK, BLK)],
            dst_ref=landed.at[:, pl.ds(pl.multiple_of(t * group + sender * BLK, BLK), BLK)],
            send_sem=a2a_sems.at[0, t, peer],
            recv_sem=a2a_sems.at[1, t, sender],
            device_id={"seq": target},
            device_id_type=MESH,
        )

    width = a_ref.shape[2]

    def att_copy(peer, sender, target):
        return pltpu.make_async_remote_copy(
            src_ref=a_ref.at[peer],
            dst_ref=att_landed.at[:, pl.ds(pl.multiple_of(sender * width, width), width)],
            send_sem=a2a_sems.at[0, parts, peer],
            recv_sem=a2a_sems.at[1, parts, sender],
            device_id={"seq": target},
            device_id_type=MESH,
        )

    a2a_started = []
    for k in range(1, m):
        peer = lax.rem(here + k, m)
        copy = att_copy(peer, here, peer)
        copy.start()
        a2a_started.append(copy)
    for k in range(1, m):
        peer = lax.rem(here + k, m)
        for t in range(parts):
            copy = part_copy(t, peer, here, peer)
            copy.start()
            a2a_started.append(copy)
    rs = (lambda peer: x_ref.at[peer], recv, sems.at[0], sems.at[1], "dp", me, n)
    finish_all(start_all(*rs), *rs)
    total = x_ref[me]
    for k in range(1, n):
        total = total + recv[lax.rem(me + k, n)]
    gath[me] = total.astype(gath.dtype)
    ag = (lambda peer: gath.at[me], gath, sems.at[2], sems.at[3], "dp", me, n)
    finish_all(start_all(*ag), *ag)
    o_ref[...] = gath[...]
    own = g_ref[here]
    for t in range(parts):
        landed[:, pl.ds(pl.multiple_of(t * group + here * BLK, BLK), BLK)] = own[
            :, t * BLK : (t + 1) * BLK
        ]
    att_landed[:, pl.ds(pl.multiple_of(here * width, width), width)] = a_ref[here]
    for k in range(1, m):
        source = lax.rem(here + m - k, m)
        att_copy(source, source, source).wait_recv()
        for t in range(parts):
            part_copy(t, source, source, source).wait_recv()
    for copy in a2a_started:
        copy.wait_send()
    moved_ref[...] = landed[...]
    att_ref[...] = att_landed[...]


def sum_and_exchange(term, grads, attended_heads):
    n = lax.axis_size("dp")
    m = lax.axis_size("seq")
    rows, cols = term.shape
    chunked = term.reshape(n, rows // n, cols)
    pieces = grads.reshape(m, grads.shape[0] // m, grads.shape[1])
    att_pieces = attended_heads.reshape(m, attended_heads.shape[0] // m, attended_heads.shape[1])
    parts = grads.shape[1] // BLK
    final = (pieces.shape[1], parts * m * BLK)
    att_final = (att_pieces.shape[1], m * att_pieces.shape[2])
    out, moved, attended = pl.pallas_call(
        functools.partial(exchange_kernel, n, m),
        out_shape=(
            jax.ShapeDtypeStruct(chunked.shape, jnp.bfloat16),
            jax.ShapeDtypeStruct(final, pieces.dtype),
            jax.ShapeDtypeStruct(att_final, att_pieces.dtype),
        ),
        in_specs=[vmem_spec(), vmem_spec(), vmem_spec()],
        out_specs=(vmem_spec(), vmem_spec(), vmem_spec()),
        scratch_shapes=[
            pltpu.VMEM(chunked.shape, jnp.float32),
            pltpu.VMEM(chunked.shape, jnp.bfloat16),
            pltpu.VMEM(final, pieces.dtype),
            pltpu.VMEM(att_final, att_pieces.dtype),
            pltpu.SemaphoreType.DMA((4, n)),
            pltpu.SemaphoreType.DMA((2, parts + 1, m)),
        ],
        compiler_params=pltpu.CompilerParams(
            collective_id=0, has_side_effects=True, vmem_limit_bytes=VMEM_LIMIT
        ),
    )(chunked, pieces, att_pieces)
    return out.reshape(rows, cols), moved, attended


def body(feats, gain, w_qkv, w_out, block_cols, block_counts, cotan):
    model_width = feats.shape[1]
    seq_count = lax.axis_size("seq")
    group_width = model_width // seq_count
    seq_at = lax.axis_index("seq")
    scaled, inverse, normed = layer_norm(feats, gain)
    normed_all = lax.all_gather(normed, "seq", axis=0, tiled=True)
    cotan_all = lax.all_gather(cotan, "seq", axis=0, tiled=True)
    w_heads = jnp.concatenate(
        [
            lax.dynamic_slice_in_dim(w_qkv, j * model_width + seq_at * group_width, group_width, 1)
            for j in range(3)
        ],
        axis=1,
    )
    mixed_heads = jnp.dot(normed_all, w_heads, preferred_element_type=jnp.float32).astype(
        jnp.bfloat16
    )
    query_heads = mixed_heads[:, :group_width]
    key_heads = mixed_heads[:, group_width : 2 * group_width]
    value_heads = mixed_heads[:, 2 * group_width :]
    cols = block_cols[0].reshape(-1)
    counts = block_counts[0]
    attended_heads, lse = attention_forward(query_heads, key_heads, value_heads, cols, counts)
    w_out_rows = lax.dynamic_slice_in_dim(w_out, seq_at * group_width, group_width, 0)
    query_grad, key_grad, value_grad = attention_backward(
        query_heads, key_heads, value_heads, attended_heads, cotan_all, w_out_rows, lse, cols, counts
    )
    grad_heads_mixed = jnp.concatenate([query_grad, key_grad, value_grad], axis=1)
    term_qkv = contract_rows(normed_all, grad_heads_mixed)
    term_out = contract_rows(attended_heads, cotan_all)
    qkv_cols = term_qkv.shape[1]
    summed, moved_grads, attended = sum_and_exchange(
        jnp.concatenate([term_qkv, term_out.reshape(term_qkv.shape[0], -1)], axis=1),
        grad_heads_mixed,
        attended_heads,
    )
    result = (
        feats.astype(jnp.float32) + jnp.dot(attended, w_out, preferred_element_type=jnp.float32)
    ).astype(jnp.bfloat16)
    grad_mixed = moved_grads
    grad_normed = lax.dot_general(
        grad_mixed, w_qkv, (((1,), (1,)), ((), ())), preferred_element_type=jnp.float32
    )
    gained = grad_normed * gain[None, :]
    mean_one = jnp.mean(gained, axis=1, keepdims=True)
    mean_two = jnp.mean(gained * scaled, axis=1, keepdims=True)
    grad_feats = (
        cotan.astype(jnp.float32) + inverse * (gained - mean_one - scaled * mean_two)
    ).astype(jnp.bfloat16)
    term_qkv = summed[:, :qkv_cols]
    term_out = summed[:, qkv_cols:].reshape(term_out.shape)
    grad_qkv = regroup_columns(
        lax.all_to_all(term_qkv, "seq", split_axis=0, concat_axis=1, tiled=True),
        seq_count,
        group_width,
    )
    grad_out = term_out
    return (result, grad_feats, grad_qkv, grad_out)


def solution(mesh):
    in_specs = (
        P(("dp", "seq"), None),
        P(),
        P(),
        P(),
        P("dp", None, None),
        P("dp", None),
        P(("dp", "seq"), None),
    )
    out_specs = (P(("dp", "seq"), None), P(("dp", "seq"), None), P("seq", None), P("seq", None))
    return jax.shard_map(body, mesh=mesh, in_specs=in_specs, out_specs=out_specs, check_vma=False)
```

```python
import functools

import jax
import jax.numpy as jnp
from jax import lax
from jax.experimental import pallas as pl
from jax.experimental.pallas import tpu as pltpu
from jax.sharding import PartitionSpec as P

HD = 64
BLK = 128
MAXB = 8
SCALE = HD ** (-0.5)
NEG = -1e30

EPSILON = 1e-05


def layer_norm(feats, gain):
    values_f = feats.astype(jnp.float32)
    centred = values_f - jnp.mean(values_f, axis=1, keepdims=True)
    inverse = lax.rsqrt(jnp.mean(centred * centred, axis=1, keepdims=True) + EPSILON)
    scaled = centred * inverse
    return (scaled, inverse, (scaled * gain[None, :]).astype(jnp.bfloat16))


def contract_rows(left_cols, right_cols):
    return lax.dot_general(
        left_cols, right_cols, (((0,), (0,)), ((), ())), preferred_element_type=jnp.float32
    )


def head_masks(width):
    lane = lax.broadcasted_iota(jnp.int32, (1, width), 1)
    return [(lane >= h * HD) & (lane < (h + 1) * HD) for h in range(width // HD)]


def stack_heads(x, masks):
    return jnp.concatenate([jnp.where(m, x, jnp.zeros_like(x)) for m in masks], axis=0)


def unstack_heads(y, masks):
    out = y[0:BLK]
    for h in range(1, len(masks)):
        out = jnp.where(masks[h], y[h * BLK : (h + 1) * BLK], out)
    return out


def nt_dot(a, b):
    return lax.dot_general(a, b, (((1,), (1,)), ((), ())), preferred_element_type=jnp.float32)


def tn_dot(a, b):
    return lax.dot_general(a, b, (((0,), (0,)), ((), ())), preferred_element_type=jnp.float32)


SLOT_TIERS = (2, 4, MAXB)


def gather_blocks(ref, cols_ref, r, slots):
    return jnp.concatenate(
        [
            ref[pl.ds(pl.multiple_of(cols_ref[r * MAXB + s] * BLK, BLK), BLK), :]
            for s in range(slots)
        ],
        axis=0,
    )


def live_lanes(cnt, slots):
    return lax.broadcasted_iota(jnp.int32, (1, slots * BLK), 1) < cnt * BLK


def by_tier(cnt, body):
    low = 0
    for slots in SLOT_TIERS:
        pl.when((cnt > low) & (cnt <= slots))(functools.partial(body, slots))
        low = slots


def attn_fwd_kernel(cols_ref, counts_ref, q_ref, k_ref, v_ref, o_ref, lse_ref):
    width = q_ref.shape[1]
    nblk = q_ref.shape[0] // BLK
    masks = head_masks(width)
    rows = len(masks) * BLK

    def row_body(r, carry):
        row0 = pl.multiple_of(r * BLK, BLK)
        cnt = counts_ref[r]

        def tier(slots):
            live = live_lanes(cnt, slots)
            q2 = stack_heads(q_ref[pl.ds(row0, BLK), :], masks)
            kc = gather_blocks(k_ref, cols_ref, r, slots)
            sc = jnp.where(live, nt_dot(q2, kc) * SCALE, NEG)
            m = jnp.max(sc, axis=1, keepdims=True)
            e = jnp.where(live, jnp.exp(sc - m), 0.0)
            l = jnp.sum(e, axis=1, keepdims=True)
            p = (e * (1.0 / l)).astype(jnp.bfloat16)
            vc = gather_blocks(v_ref, cols_ref, r, slots)
            acc = jnp.dot(p, vc, preferred_element_type=jnp.float32)
            o_ref[pl.ds(row0, BLK), :] = unstack_heads(acc, masks).astype(o_ref.dtype)
            lse_ref[pl.ds(pl.multiple_of(r * rows, rows), rows), :] = jnp.broadcast_to(
                m + jnp.log(l), (rows, lse_ref.shape[1])
            )

        by_tier(cnt, tier)
        return carry

    lax.fori_loop(0, nblk, row_body, 0)


def attn_bwd_kernel(
    cols_ref, counts_ref, q_ref, k_ref, v_ref, o_ref, do_ref, lse_ref, dq_ref, dk_ref, dv_ref, dk_acc, dv_acc
):
    width = q_ref.shape[1]
    nblk = q_ref.shape[0] // BLK
    masks = head_masks(width)
    rows = len(masks) * BLK
    dk_acc[...] = jnp.zeros_like(dk_acc)
    dv_acc[...] = jnp.zeros_like(dv_acc)

    def row_body(r, carry):
        row0 = pl.multiple_of(r * BLK, BLK)
        cnt = counts_ref[r]

        def tier(slots):
            live = live_lanes(cnt, slots)
            q2 = stack_heads(q_ref[pl.ds(row0, BLK), :], masks)
            do_blk = do_ref[pl.ds(row0, BLK), :]
            do2 = stack_heads(do_blk, masks)
            prod = o_ref[pl.ds(row0, BLK), :].astype(jnp.float32) * do_blk.astype(jnp.float32)
            delta = jnp.concatenate(
                [jnp.sum(jnp.where(m, prod, 0.0), axis=1, keepdims=True) for m in masks], axis=0
            )
            lse = lse_ref[pl.ds(pl.multiple_of(r * rows, rows), rows), :][:, 0:1]
            kc = gather_blocks(k_ref, cols_ref, r, slots)
            vc = gather_blocks(v_ref, cols_ref, r, slots)
            sc = nt_dot(q2, kc) * SCALE
            p = jnp.where(live, jnp.exp(sc - lse), 0.0).astype(jnp.bfloat16)
            dp = nt_dot(do2, vc)
            ds = (p.astype(jnp.float32) * (dp - delta) * SCALE).astype(jnp.bfloat16)
            dq = jnp.dot(ds, kc, preferred_element_type=jnp.float32)
            dq_ref[pl.ds(row0, BLK), :] = unstack_heads(dq, masks).astype(dq_ref.dtype)
            dkc = tn_dot(ds, q2)
            dvc = tn_dot(p, do2)
            for s in range(slots):

                @pl.when(s < cnt)
                def _():
                    col0 = pl.multiple_of(cols_ref[r * MAXB + s] * BLK, BLK)
                    dk_acc[pl.ds(col0, BLK), :] += dkc[s * BLK : (s + 1) * BLK]
                    dv_acc[pl.ds(col0, BLK), :] += dvc[s * BLK : (s + 1) * BLK]

        by_tier(cnt, tier)
        return carry

    lax.fori_loop(0, nblk, row_body, 0)
    dk_ref[...] = dk_acc[...].astype(dk_ref.dtype)
    dv_ref[...] = dv_acc[...].astype(dv_ref.dtype)


def smem_spec():
    return pl.BlockSpec(memory_space=pltpu.SMEM)


def vmem_spec():
    return pl.BlockSpec(memory_space=pltpu.VMEM)


VMEM_LIMIT = 48 * 1024 * 1024


def attention_forward(q, k, v, cols, counts):
    n, width = q.shape
    rows = (width // HD) * BLK
    return pl.pallas_call(
        attn_fwd_kernel,
        out_shape=(
            jax.ShapeDtypeStruct((n, width), jnp.bfloat16),
            jax.ShapeDtypeStruct(((n // BLK) * rows, 128), jnp.float32),
        ),
        in_specs=[smem_spec(), smem_spec(), vmem_spec(), vmem_spec(), vmem_spec()],
        out_specs=(vmem_spec(), vmem_spec()),
        compiler_params=pltpu.CompilerParams(vmem_limit_bytes=VMEM_LIMIT),
    )(cols, counts, q, k, v)


def attention_backward(q, k, v, o, do, lse, cols, counts):
    n, width = q.shape
    return pl.pallas_call(
        attn_bwd_kernel,
        out_shape=tuple(jax.ShapeDtypeStruct((n, width), jnp.bfloat16) for _ in range(3)),
        in_specs=[smem_spec(), smem_spec()] + [vmem_spec()] * 6,
        out_specs=(vmem_spec(), vmem_spec(), vmem_spec()),
        scratch_shapes=[pltpu.VMEM((n, width), jnp.float32), pltpu.VMEM((n, width), jnp.float32)],
        compiler_params=pltpu.CompilerParams(vmem_limit_bytes=VMEM_LIMIT),
    )(cols, counts, q, k, v, o, do, lse)


def regroup_columns(moved, seq_count, group_width):
    rows = moved.shape[0]
    return (
        moved.reshape(rows, seq_count, 3, group_width)
        .transpose(0, 2, 1, 3)
        .reshape(rows, 3 * seq_count * group_width)
    )


MESH = pl.DeviceIdType.MESH


def exchange_kernel(
    n,
    m,
    qkv_cols,
    x_ref,
    g_ref,
    a_ref,
    o_ref,
    moved_ref,
    att_ref,
    qkv_ref,
    recv,
    gath,
    landed,
    att_landed,
    qkv_landed,
    sems,
    a2a_sems,
    qkv_sems,
):
    me = lax.axis_index("dp")
    here = lax.axis_index("seq")
    barrier = pltpu.get_barrier_semaphore()
    for k in range(1, n):
        pl.semaphore_signal(
            barrier, inc=1, device_id={"dp": lax.rem(me + k, n)}, device_id_type=MESH
        )
    for k in range(1, m):
        pl.semaphore_signal(
            barrier, inc=1, device_id={"seq": lax.rem(here + k, m)}, device_id_type=MESH
        )
    pl.semaphore_wait(barrier, n - 1 + m - 1)

    def start_all(src_of, dst, send, arrive, axis, at, size):
        started = []
        for k in range(1, size):
            peer = lax.rem(at + k, size)
            copy = pltpu.make_async_remote_copy(
                src_ref=src_of(peer),
                dst_ref=dst.at[at],
                send_sem=send.at[peer],
                recv_sem=arrive.at[at],
                device_id={axis: peer},
                device_id_type=MESH,
            )
            copy.start()
            started.append(copy)
        return started

    def finish_all(started, src_of, dst, send, arrive, axis, at, size):
        for k in range(1, size):
            source = lax.rem(at + size - k, size)
            pltpu.make_async_remote_copy(
                src_ref=src_of(source),
                dst_ref=dst.at[source],
                send_sem=send.at[source],
                recv_sem=arrive.at[source],
                device_id={axis: source},
                device_id_type=MESH,
            ).wait_recv()
        for copy in started:
            copy.wait_send()

    parts = g_ref.shape[2] // BLK
    group = BLK * m

    def part_copy(t, peer, sender, target):
        return pltpu.make_async_remote_copy(
            src_ref=g_ref.at[peer, :, pl.ds(t * BLK, BLK)],
            dst_ref=landed.at[:, pl.ds(pl.multiple_of(t * group + sender * BLK, BLK), BLK)],
            send_sem=a2a_sems.at[0, t, peer],
            recv_sem=a2a_sems.at[1, t, sender],
            device_id={"seq": target},
            device_id_type=MESH,
        )

    width = a_ref.shape[2]

    def att_copy(peer, sender, target):
        return pltpu.make_async_remote_copy(
            src_ref=a_ref.at[peer],
            dst_ref=att_landed.at[:, pl.ds(pl.multiple_of(sender * width, width), width)],
            send_sem=a2a_sems.at[0, parts, peer],
            recv_sem=a2a_sems.at[1, parts, sender],
            device_id={"seq": target},
            device_id_type=MESH,
        )

    a2a_started = []
    for k in range(1, m):
        peer = lax.rem(here + k, m)
        copy = att_copy(peer, here, peer)
        copy.start()
        a2a_started.append(copy)
    for k in range(1, m):
        peer = lax.rem(here + k, m)
        for t in range(parts):
            copy = part_copy(t, peer, here, peer)
            copy.start()
            a2a_started.append(copy)
    rs = (lambda peer: x_ref.at[peer], recv, sems.at[0], sems.at[1], "dp", me, n)
    finish_all(start_all(*rs), *rs)
    total = x_ref[me]
    for k in range(1, n):
        total = total + recv[lax.rem(me + k, n)]
    gath[me] = total.astype(gath.dtype)
    ag = (lambda peer: gath.at[me], gath, sems.at[2], sems.at[3], "dp", me, n)
    finish_all(start_all(*ag), *ag)
    o_ref[...] = gath[...]
    halves = n // m
    half_rows = gath.shape[1]

    def qkv_copy(t, h, peer, sender, target):
        return pltpu.make_async_remote_copy(
            src_ref=gath.at[peer * halves + h, :, pl.ds(t * BLK, BLK)],
            dst_ref=qkv_landed.at[
                pl.ds(h * half_rows, half_rows),
                pl.ds(pl.multiple_of(t * group + sender * BLK, BLK), BLK),
            ],
            send_sem=qkv_sems.at[0, t * halves + h, peer],
            recv_sem=qkv_sems.at[1, t * halves + h, sender],
            device_id={"seq": target},
            device_id_type=MESH,
        )

    qkv_started = []
    for k in range(1, m):
        peer = lax.rem(here + k, m)
        for t in range(qkv_cols // BLK):
            for h in range(halves):
                copy = qkv_copy(t, h, peer, here, peer)
                copy.start()
                qkv_started.append(copy)
    for t in range(qkv_cols // BLK):
        for h in range(halves):
            qkv_landed[
                pl.ds(h * half_rows, half_rows),
                pl.ds(pl.multiple_of(t * group + here * BLK, BLK), BLK),
            ] = gath[here * halves + h, :, t * BLK : (t + 1) * BLK]
    own = g_ref[here]
    for t in range(parts):
        landed[:, pl.ds(pl.multiple_of(t * group + here * BLK, BLK), BLK)] = own[
            :, t * BLK : (t + 1) * BLK
        ]
    att_landed[:, pl.ds(pl.multiple_of(here * width, width), width)] = a_ref[here]
    for k in range(1, m):
        source = lax.rem(here + m - k, m)
        att_copy(source, source, source).wait_recv()
        for t in range(parts):
            part_copy(t, source, source, source).wait_recv()
    for copy in a2a_started:
        copy.wait_send()
    moved_ref[...] = landed[...]
    att_ref[...] = att_landed[...]
    for k in range(1, m):
        source = lax.rem(here + m - k, m)
        for t in range(qkv_cols // BLK):
            for h in range(halves):
                qkv_copy(t, h, source, source, source).wait_recv()
    for copy in qkv_started:
        copy.wait_send()
    qkv_ref[...] = qkv_landed[...]


def sum_and_exchange(term, grads, attended_heads, qkv_cols):
    n = lax.axis_size("dp")
    m = lax.axis_size("seq")
    rows, cols = term.shape
    chunked = term.reshape(n, rows // n, cols)
    pieces = grads.reshape(m, grads.shape[0] // m, grads.shape[1])
    att_pieces = attended_heads.reshape(m, attended_heads.shape[0] // m, attended_heads.shape[1])
    parts = grads.shape[1] // BLK
    final = (pieces.shape[1], parts * m * BLK)
    att_final = (att_pieces.shape[1], m * att_pieces.shape[2])
    qkv_final = (rows // m, (qkv_cols // BLK) * m * BLK)
    halves = n // m
    out, moved, attended, grad_qkv = pl.pallas_call(
        functools.partial(exchange_kernel, n, m, qkv_cols),
        out_shape=(
            jax.ShapeDtypeStruct(chunked.shape, jnp.bfloat16),
            jax.ShapeDtypeStruct(final, pieces.dtype),
            jax.ShapeDtypeStruct(att_final, att_pieces.dtype),
            jax.ShapeDtypeStruct(qkv_final, jnp.bfloat16),
        ),
        in_specs=[vmem_spec(), vmem_spec(), vmem_spec()],
        out_specs=(vmem_spec(), vmem_spec(), vmem_spec(), vmem_spec()),
        scratch_shapes=[
            pltpu.VMEM(chunked.shape, jnp.float32),
            pltpu.VMEM(chunked.shape, jnp.bfloat16),
            pltpu.VMEM(final, pieces.dtype),
            pltpu.VMEM(att_final, att_pieces.dtype),
            pltpu.VMEM(qkv_final, jnp.bfloat16),
            pltpu.SemaphoreType.DMA((4, n)),
            pltpu.SemaphoreType.DMA((2, parts + 1, m)),
            pltpu.SemaphoreType.DMA((2, (qkv_cols // BLK) * halves, m)),
        ],
        compiler_params=pltpu.CompilerParams(
            collective_id=0, has_side_effects=True, vmem_limit_bytes=VMEM_LIMIT
        ),
    )(chunked, pieces, att_pieces)
    return out.reshape(rows, cols), moved, attended, grad_qkv


def body(feats, gain, w_qkv, w_out, block_cols, block_counts, cotan):
    model_width = feats.shape[1]
    seq_count = lax.axis_size("seq")
    group_width = model_width // seq_count
    seq_at = lax.axis_index("seq")
    scaled, inverse, normed = layer_norm(feats, gain)
    normed_all = lax.all_gather(normed, "seq", axis=0, tiled=True)
    cotan_all = lax.all_gather(cotan, "seq", axis=0, tiled=True)
    w_heads = jnp.concatenate(
        [
            lax.dynamic_slice_in_dim(w_qkv, j * model_width + seq_at * group_width, group_width, 1)
            for j in range(3)
        ],
        axis=1,
    )
    mixed_heads = jnp.dot(normed_all, w_heads, preferred_element_type=jnp.float32).astype(
        jnp.bfloat16
    )
    query_heads = mixed_heads[:, :group_width]
    key_heads = mixed_heads[:, group_width : 2 * group_width]
    value_heads = mixed_heads[:, 2 * group_width :]
    cols = block_cols[0].reshape(-1)
    counts = block_counts[0]
    attended_heads, lse = attention_forward(query_heads, key_heads, value_heads, cols, counts)
    w_out_rows = lax.dynamic_slice_in_dim(w_out, seq_at * group_width, group_width, 0)
    grad_heads = lax.dot_general(
        cotan_all, w_out_rows, (((1,), (1,)), ((), ())), preferred_element_type=jnp.float32
    ).astype(jnp.bfloat16)
    query_grad, key_grad, value_grad = attention_backward(
        query_heads, key_heads, value_heads, attended_heads, grad_heads, lse, cols, counts
    )
    grad_heads_mixed = jnp.concatenate([query_grad, key_grad, value_grad], axis=1)
    term_qkv = contract_rows(normed_all, grad_heads_mixed)
    term_out = contract_rows(attended_heads, cotan_all)
    qkv_cols = term_qkv.shape[1]
    summed, moved_grads, attended, grad_qkv = sum_and_exchange(
        jnp.concatenate([term_qkv, term_out.reshape(term_qkv.shape[0], -1)], axis=1),
        grad_heads_mixed,
        attended_heads,
        qkv_cols,
    )
    result = (
        feats.astype(jnp.float32) + jnp.dot(attended, w_out, preferred_element_type=jnp.float32)
    ).astype(jnp.bfloat16)
    grad_mixed = moved_grads
    grad_normed = lax.dot_general(
        grad_mixed, w_qkv, (((1,), (1,)), ((), ())), preferred_element_type=jnp.float32
    )
    gained = grad_normed * gain[None, :]
    mean_one = jnp.mean(gained, axis=1, keepdims=True)
    mean_two = jnp.mean(gained * scaled, axis=1, keepdims=True)
    grad_feats = (
        cotan.astype(jnp.float32) + inverse * (gained - mean_one - scaled * mean_two)
    ).astype(jnp.bfloat16)
    grad_out = summed[:, qkv_cols:].reshape(term_out.shape)
    return (result, grad_feats, grad_qkv, grad_out)


def solution(mesh):
    in_specs = (
        P(("dp", "seq"), None),
        P(),
        P(),
        P(),
        P("dp", None, None),
        P("dp", None),
        P(("dp", "seq"), None),
    )
    out_specs = (P(("dp", "seq"), None), P(("dp", "seq"), None), P("seq", None), P("seq", None))
    return jax.shard_map(body, mesh=mesh, in_specs=in_specs, out_specs=out_specs, check_vma=False)
```

```python
import functools

import jax
import jax.numpy as jnp
from jax import lax
from jax.experimental import pallas as pl
from jax.experimental.pallas import tpu as pltpu
from jax.sharding import PartitionSpec as P

HD = 64
BLK = 128
MAXB = 8
SCALE = HD ** (-0.5)
NEG = -1e30

EPSILON = 1e-05


def layer_norm(feats, gain):
    values_f = feats.astype(jnp.float32)
    centred = values_f - jnp.mean(values_f, axis=1, keepdims=True)
    inverse = lax.rsqrt(jnp.mean(centred * centred, axis=1, keepdims=True) + EPSILON)
    scaled = centred * inverse
    return (scaled, inverse, (scaled * gain[None, :]).astype(jnp.bfloat16))


def contract_rows(left_cols, right_cols):
    return lax.dot_general(
        left_cols, right_cols, (((0,), (0,)), ((), ())), preferred_element_type=jnp.float32
    )


def head_masks(width):
    lane = lax.broadcasted_iota(jnp.int32, (1, width), 1)
    return [(lane >= h * HD) & (lane < (h + 1) * HD) for h in range(width // HD)]


def stack_heads(x, masks):
    return jnp.concatenate([jnp.where(m, x, jnp.zeros_like(x)) for m in masks], axis=0)


def unstack_heads(y, masks):
    out = y[0:BLK]
    for h in range(1, len(masks)):
        out = jnp.where(masks[h], y[h * BLK : (h + 1) * BLK], out)
    return out


def nt_dot(a, b):
    return lax.dot_general(a, b, (((1,), (1,)), ((), ())), preferred_element_type=jnp.float32)


def tn_dot(a, b):
    return lax.dot_general(a, b, (((0,), (0,)), ((), ())), preferred_element_type=jnp.float32)


SLOT_TIERS = (2, 4, MAXB)


def gather_blocks(ref, cols_ref, r, slots):
    return jnp.concatenate(
        [
            ref[pl.ds(pl.multiple_of(cols_ref[r * MAXB + s] * BLK, BLK), BLK), :]
            for s in range(slots)
        ],
        axis=0,
    )


def live_lanes(cnt, slots):
    return lax.broadcasted_iota(jnp.int32, (1, slots * BLK), 1) < cnt * BLK


def by_tier(cnt, body):
    low = 0
    for slots in SLOT_TIERS:
        pl.when((cnt > low) & (cnt <= slots))(functools.partial(body, slots))
        low = slots


def attn_fwd_kernel(cols_ref, counts_ref, q_ref, k_ref, v_ref, o_ref, lse_ref):
    width = q_ref.shape[1]
    nblk = q_ref.shape[0] // BLK
    masks = head_masks(width)
    rows = len(masks) * BLK

    def row_body(r, carry):
        row0 = pl.multiple_of(r * BLK, BLK)
        cnt = counts_ref[r]

        def tier(slots):
            live = live_lanes(cnt, slots)
            q2 = stack_heads(q_ref[pl.ds(row0, BLK), :], masks)
            kc = gather_blocks(k_ref, cols_ref, r, slots)
            sc = jnp.where(live, nt_dot(q2, kc) * SCALE, NEG)
            m = jnp.max(sc, axis=1, keepdims=True)
            e = jnp.where(live, jnp.exp(sc - m), 0.0)
            l = jnp.sum(e, axis=1, keepdims=True)
            p = (e * (1.0 / l)).astype(jnp.bfloat16)
            vc = gather_blocks(v_ref, cols_ref, r, slots)
            acc = jnp.dot(p, vc, preferred_element_type=jnp.float32)
            o_ref[pl.ds(row0, BLK), :] = unstack_heads(acc, masks).astype(o_ref.dtype)
            lse_ref[pl.ds(pl.multiple_of(r * rows, rows), rows), :] = jnp.broadcast_to(
                m + jnp.log(l), (rows, lse_ref.shape[1])
            )

        by_tier(cnt, tier)
        return carry

    lax.fori_loop(0, nblk, row_body, 0)


def attn_bwd_kernel(
    cols_ref, counts_ref, q_ref, k_ref, v_ref, o_ref, do_ref, lse_ref, dq_ref, dk_ref, dv_ref, dk_acc, dv_acc
):
    width = q_ref.shape[1]
    nblk = q_ref.shape[0] // BLK
    masks = head_masks(width)
    rows = len(masks) * BLK
    dk_acc[...] = jnp.zeros_like(dk_acc)
    dv_acc[...] = jnp.zeros_like(dv_acc)

    def row_body(r, carry):
        row0 = pl.multiple_of(r * BLK, BLK)
        cnt = counts_ref[r]

        def tier(slots):
            live = live_lanes(cnt, slots)
            q2 = stack_heads(q_ref[pl.ds(row0, BLK), :], masks)
            do_blk = do_ref[pl.ds(row0, BLK), :]
            do2 = stack_heads(do_blk, masks)
            prod = o_ref[pl.ds(row0, BLK), :].astype(jnp.float32) * do_blk.astype(jnp.float32)
            delta = jnp.concatenate(
                [jnp.sum(jnp.where(m, prod, 0.0), axis=1, keepdims=True) for m in masks], axis=0
            )
            lse = lse_ref[pl.ds(pl.multiple_of(r * rows, rows), rows), :][:, 0:1]
            kc = gather_blocks(k_ref, cols_ref, r, slots)
            vc = gather_blocks(v_ref, cols_ref, r, slots)
            sc = nt_dot(q2, kc) * SCALE
            p = jnp.where(live, jnp.exp(sc - lse), 0.0).astype(jnp.bfloat16)
            dp = nt_dot(do2, vc)
            ds = (p.astype(jnp.float32) * (dp - delta) * SCALE).astype(jnp.bfloat16)
            dq = jnp.dot(ds, kc, preferred_element_type=jnp.float32)
            dq_ref[pl.ds(row0, BLK), :] = unstack_heads(dq, masks).astype(dq_ref.dtype)
            dkc = tn_dot(ds, q2)
            dvc = tn_dot(p, do2)
            for s in range(slots):

                @pl.when(s < cnt)
                def _():
                    col0 = pl.multiple_of(cols_ref[r * MAXB + s] * BLK, BLK)
                    dk_acc[pl.ds(col0, BLK), :] += dkc[s * BLK : (s + 1) * BLK]
                    dv_acc[pl.ds(col0, BLK), :] += dvc[s * BLK : (s + 1) * BLK]

        by_tier(cnt, tier)
        return carry

    lax.fori_loop(0, nblk, row_body, 0)
    dk_ref[...] = dk_acc[...].astype(dk_ref.dtype)
    dv_ref[...] = dv_acc[...].astype(dv_ref.dtype)


def smem_spec():
    return pl.BlockSpec(memory_space=pltpu.SMEM)


def vmem_spec():
    return pl.BlockSpec(memory_space=pltpu.VMEM)


VMEM_LIMIT = 48 * 1024 * 1024


def attention_forward(q, k, v, cols, counts):
    n, width = q.shape
    rows = (width // HD) * BLK
    return pl.pallas_call(
        attn_fwd_kernel,
        out_shape=(
            jax.ShapeDtypeStruct((n, width), jnp.bfloat16),
            jax.ShapeDtypeStruct(((n // BLK) * rows, 128), jnp.float32),
        ),
        in_specs=[smem_spec(), smem_spec(), vmem_spec(), vmem_spec(), vmem_spec()],
        out_specs=(vmem_spec(), vmem_spec()),
        compiler_params=pltpu.CompilerParams(vmem_limit_bytes=VMEM_LIMIT),
    )(cols, counts, q, k, v)


def attention_backward(q, k, v, o, do, lse, cols, counts):
    n, width = q.shape
    return pl.pallas_call(
        attn_bwd_kernel,
        out_shape=tuple(jax.ShapeDtypeStruct((n, width), jnp.bfloat16) for _ in range(3)),
        in_specs=[smem_spec(), smem_spec()] + [vmem_spec()] * 6,
        out_specs=(vmem_spec(), vmem_spec(), vmem_spec()),
        scratch_shapes=[pltpu.VMEM((n, width), jnp.float32), pltpu.VMEM((n, width), jnp.float32)],
        compiler_params=pltpu.CompilerParams(vmem_limit_bytes=VMEM_LIMIT),
    )(cols, counts, q, k, v, o, do, lse)


def regroup_columns(moved, seq_count, group_width):
    rows = moved.shape[0]
    return (
        moved.reshape(rows, seq_count, 3, group_width)
        .transpose(0, 2, 1, 3)
        .reshape(rows, 3 * seq_count * group_width)
    )


MESH = pl.DeviceIdType.MESH


def exchange_kernel(
    n,
    m,
    qkv_cols,
    x_ref,
    g_ref,
    a_ref,
    o_ref,
    moved_ref,
    att_ref,
    qkv_ref,
    recv,
    gath,
    landed,
    att_landed,
    qkv_landed,
    sems,
    a2a_sems,
    qkv_sems,
):
    me = lax.axis_index("dp")
    here = lax.axis_index("seq")
    barrier = pltpu.get_barrier_semaphore()
    flat = me * m + here
    for k in range(1, n * m):
        other = lax.rem(flat + k, n * m)
        pl.semaphore_signal(
            barrier, inc=1, device_id=(other // m, lax.rem(other, m)), device_id_type=MESH
        )
    pl.semaphore_wait(barrier, n * m - 1)

    def start_all(src_of, dst, send, arrive, axis, at, size):
        started = []
        for k in range(1, size):
            peer = lax.rem(at + k, size)
            copy = pltpu.make_async_remote_copy(
                src_ref=src_of(peer),
                dst_ref=dst.at[at],
                send_sem=send.at[peer],
                recv_sem=arrive.at[at],
                device_id={axis: peer},
                device_id_type=MESH,
            )
            copy.start()
            started.append(copy)
        return started

    def finish_all(started, src_of, dst, send, arrive, axis, at, size):
        for k in range(1, size):
            source = lax.rem(at + size - k, size)
            pltpu.make_async_remote_copy(
                src_ref=src_of(source),
                dst_ref=dst.at[source],
                send_sem=send.at[source],
                recv_sem=arrive.at[source],
                device_id={axis: source},
                device_id_type=MESH,
            ).wait_recv()
        for copy in started:
            copy.wait_send()

    parts = g_ref.shape[2] // BLK
    group = BLK * m

    def part_copy(t, peer, sender, target):
        return pltpu.make_async_remote_copy(
            src_ref=g_ref.at[peer, :, pl.ds(t * BLK, BLK)],
            dst_ref=landed.at[:, pl.ds(pl.multiple_of(t * group + sender * BLK, BLK), BLK)],
            send_sem=a2a_sems.at[0, t, peer],
            recv_sem=a2a_sems.at[1, t, sender],
            device_id={"seq": target},
            device_id_type=MESH,
        )

    width = a_ref.shape[2]

    def att_copy(peer, sender, target):
        return pltpu.make_async_remote_copy(
            src_ref=a_ref.at[peer],
            dst_ref=att_landed.at[:, pl.ds(pl.multiple_of(sender * width, width), width)],
            send_sem=a2a_sems.at[0, parts, peer],
            recv_sem=a2a_sems.at[1, parts, sender],
            device_id={"seq": target},
            device_id_type=MESH,
        )

    a2a_started = []
    for k in range(1, m):
        peer = lax.rem(here + k, m)
        copy = att_copy(peer, here, peer)
        copy.start()
        a2a_started.append(copy)
    for k in range(1, m):
        peer = lax.rem(here + k, m)
        for t in range(parts):
            copy = part_copy(t, peer, here, peer)
            copy.start()
            a2a_started.append(copy)
    rs = (lambda peer: x_ref.at[peer], recv, sems.at[0], sems.at[1], "dp", me, n)
    finish_all(start_all(*rs), *rs)
    total = x_ref[me]
    for k in range(1, n):
        total = total + recv[lax.rem(me + k, n)]
    gath[me] = total.astype(gath.dtype)
    halves = n // m
    half_rows = gath.shape[1]
    owner = me // halves
    lower = lax.rem(me, halves)
    qkv_parts = qkv_cols // BLK

    def qkv_copy(t, target_dp, src_dp, row_half, sender_seq, target_seq):
        return pltpu.make_async_remote_copy(
            src_ref=gath.at[src_dp, :, pl.ds(t * BLK, BLK)],
            dst_ref=qkv_landed.at[
                pl.ds(pl.multiple_of(row_half * half_rows, half_rows), half_rows),
                pl.ds(pl.multiple_of(t * group + sender_seq * BLK, BLK), BLK),
            ],
            send_sem=qkv_sems.at[0, t, target_dp],
            recv_sem=qkv_sems.at[1, t * halves + row_half, sender_seq],
            device_id=(target_dp, target_seq),
            device_id_type=MESH,
        )

    not_self = owner != here
    qkv_started = []
    for k in range(n):
        target_dp = lax.rem(me + k, n)
        for t in range(qkv_parts):
            copy = qkv_copy(t, target_dp, me, lower, here, owner)
            if k == 0:
                pl.when(not_self)(copy.start)
            else:
                copy.start()
            qkv_started.append((k, copy))

    @pl.when(owner == here)
    def _():
        for t in range(qkv_parts):
            qkv_landed[
                pl.ds(pl.multiple_of(lower * half_rows, half_rows), half_rows),
                pl.ds(pl.multiple_of(t * group + here * BLK, BLK), BLK),
            ] = gath[me, :, t * BLK : (t + 1) * BLK]

    ag = (lambda peer: gath.at[me], gath, sems.at[2], sems.at[3], "dp", me, n)
    finish_all(start_all(*ag), *ag)
    o_ref[...] = gath[...]
    own = g_ref[here]
    for t in range(parts):
        landed[:, pl.ds(pl.multiple_of(t * group + here * BLK, BLK), BLK)] = own[
            :, t * BLK : (t + 1) * BLK
        ]
    att_landed[:, pl.ds(pl.multiple_of(here * width, width), width)] = a_ref[here]
    for k in range(1, m):
        source = lax.rem(here + m - k, m)
        att_copy(source, source, source).wait_recv()
        for t in range(parts):
            part_copy(t, source, source, source).wait_recv()
    for copy in a2a_started:
        copy.wait_send()
    moved_ref[...] = landed[...]
    att_ref[...] = att_landed[...]
    for h in range(halves):
        source_dp = here * halves + h
        for k in range(m):
            source_seq = lax.rem(here + k, m)
            for t in range(qkv_parts):
                copy = qkv_copy(t, me, source_dp, h, source_seq, here)
                if k == 0:
                    pl.when(source_dp != me)(copy.wait_recv)
                else:
                    copy.wait_recv()
    for k, copy in qkv_started:
        if k == 0:
            pl.when(not_self)(copy.wait_send)
        else:
            copy.wait_send()
    qkv_ref[...] = qkv_landed[...]


def sum_and_exchange(term, grads, attended_heads, qkv_cols):
    n = lax.axis_size("dp")
    m = lax.axis_size("seq")
    rows, cols = term.shape
    chunked = term.reshape(n, rows // n, cols)
    pieces = grads.reshape(m, grads.shape[0] // m, grads.shape[1])
    att_pieces = attended_heads.reshape(m, attended_heads.shape[0] // m, attended_heads.shape[1])
    parts = grads.shape[1] // BLK
    final = (pieces.shape[1], parts * m * BLK)
    att_final = (att_pieces.shape[1], m * att_pieces.shape[2])
    qkv_final = (rows // m, (qkv_cols // BLK) * m * BLK)
    halves = n // m
    out, moved, attended, grad_qkv = pl.pallas_call(
        functools.partial(exchange_kernel, n, m, qkv_cols),
        out_shape=(
            jax.ShapeDtypeStruct(chunked.shape, jnp.bfloat16),
            jax.ShapeDtypeStruct(final, pieces.dtype),
            jax.ShapeDtypeStruct(att_final, att_pieces.dtype),
            jax.ShapeDtypeStruct(qkv_final, jnp.bfloat16),
        ),
        in_specs=[vmem_spec(), vmem_spec(), vmem_spec()],
        out_specs=(vmem_spec(), vmem_spec(), vmem_spec(), vmem_spec()),
        scratch_shapes=[
            pltpu.VMEM(chunked.shape, jnp.float32),
            pltpu.VMEM(chunked.shape, jnp.bfloat16),
            pltpu.VMEM(final, pieces.dtype),
            pltpu.VMEM(att_final, att_pieces.dtype),
            pltpu.VMEM(qkv_final, jnp.bfloat16),
            pltpu.SemaphoreType.DMA((4, n)),
            pltpu.SemaphoreType.DMA((2, parts + 1, m)),
            pltpu.SemaphoreType.DMA((2, (qkv_cols // BLK) * halves, max(n, m))),
        ],
        compiler_params=pltpu.CompilerParams(
            collective_id=0, has_side_effects=True, vmem_limit_bytes=VMEM_LIMIT
        ),
    )(chunked, pieces, att_pieces)
    return out.reshape(rows, cols), moved, attended, grad_qkv


def body(feats, gain, w_qkv, w_out, block_cols, block_counts, cotan):
    model_width = feats.shape[1]
    seq_count = lax.axis_size("seq")
    group_width = model_width // seq_count
    seq_at = lax.axis_index("seq")
    scaled, inverse, normed = layer_norm(feats, gain)
    normed_all = lax.all_gather(normed, "seq", axis=0, tiled=True)
    cotan_all = lax.all_gather(cotan, "seq", axis=0, tiled=True)
    w_heads = jnp.concatenate(
        [
            lax.dynamic_slice_in_dim(w_qkv, j * model_width + seq_at * group_width, group_width, 1)
            for j in range(3)
        ],
        axis=1,
    )
    mixed_heads = jnp.dot(normed_all, w_heads, preferred_element_type=jnp.float32).astype(
        jnp.bfloat16
    )
    query_heads = mixed_heads[:, :group_width]
    key_heads = mixed_heads[:, group_width : 2 * group_width]
    value_heads = mixed_heads[:, 2 * group_width :]
    cols = block_cols[0].reshape(-1)
    counts = block_counts[0]
    attended_heads, lse = attention_forward(query_heads, key_heads, value_heads, cols, counts)
    w_out_rows = lax.dynamic_slice_in_dim(w_out, seq_at * group_width, group_width, 0)
    grad_heads = lax.dot_general(
        cotan_all, w_out_rows, (((1,), (1,)), ((), ())), preferred_element_type=jnp.float32
    ).astype(jnp.bfloat16)
    query_grad, key_grad, value_grad = attention_backward(
        query_heads, key_heads, value_heads, attended_heads, grad_heads, lse, cols, counts
    )
    grad_heads_mixed = jnp.concatenate([query_grad, key_grad, value_grad], axis=1)
    term_qkv = contract_rows(normed_all, grad_heads_mixed)
    term_out = contract_rows(attended_heads, cotan_all)
    qkv_cols = term_qkv.shape[1]
    summed, moved_grads, attended, grad_qkv = sum_and_exchange(
        jnp.concatenate([term_qkv, term_out.reshape(term_qkv.shape[0], -1)], axis=1),
        grad_heads_mixed,
        attended_heads,
        qkv_cols,
    )
    result = (
        feats.astype(jnp.float32) + jnp.dot(attended, w_out, preferred_element_type=jnp.float32)
    ).astype(jnp.bfloat16)
    grad_mixed = moved_grads
    grad_normed = lax.dot_general(
        grad_mixed, w_qkv, (((1,), (1,)), ((), ())), preferred_element_type=jnp.float32
    )
    gained = grad_normed * gain[None, :]
    mean_one = jnp.mean(gained, axis=1, keepdims=True)
    mean_two = jnp.mean(gained * scaled, axis=1, keepdims=True)
    grad_feats = (
        cotan.astype(jnp.float32) + inverse * (gained - mean_one - scaled * mean_two)
    ).astype(jnp.bfloat16)
    grad_out = summed[:, qkv_cols:].reshape(term_out.shape)
    return (result, grad_feats, grad_qkv, grad_out)


def solution(mesh):
    in_specs = (
        P(("dp", "seq"), None),
        P(),
        P(),
        P(),
        P("dp", None, None),
        P("dp", None),
        P(("dp", "seq"), None),
    )
    out_specs = (P(("dp", "seq"), None), P(("dp", "seq"), None), P("seq", None), P("seq", None))
    return jax.shard_map(body, mesh=mesh, in_specs=in_specs, out_specs=out_specs, check_vma=False)
```

```python
import functools

import jax
import jax.numpy as jnp
from jax import lax
from jax.experimental import pallas as pl
from jax.experimental.pallas import tpu as pltpu
from jax.sharding import PartitionSpec as P

HD = 64
BLK = 128
MAXB = 8
SCALE = HD ** (-0.5)
NEG = -1e30

EPSILON = 1e-05


def layer_norm(feats, gain):
    values_f = feats.astype(jnp.float32)
    centred = values_f - jnp.mean(values_f, axis=1, keepdims=True)
    inverse = lax.rsqrt(jnp.mean(centred * centred, axis=1, keepdims=True) + EPSILON)
    scaled = centred * inverse
    return (scaled, inverse, (scaled * gain[None, :]).astype(jnp.bfloat16))


def contract_rows(left_cols, right_cols):
    return lax.dot_general(
        left_cols, right_cols, (((0,), (0,)), ((), ())), preferred_element_type=jnp.float32
    )


def head_masks(width):
    lane = lax.broadcasted_iota(jnp.int32, (1, width), 1)
    return [(lane >= h * HD) & (lane < (h + 1) * HD) for h in range(width // HD)]


def stack_heads(x, masks):
    return jnp.concatenate([jnp.where(m, x, jnp.zeros_like(x)) for m in masks], axis=0)


def unstack_heads(y, masks):
    out = y[0:BLK]
    for h in range(1, len(masks)):
        out = jnp.where(masks[h], y[h * BLK : (h + 1) * BLK], out)
    return out


def nt_dot(a, b):
    return lax.dot_general(a, b, (((1,), (1,)), ((), ())), preferred_element_type=jnp.float32)


def tn_dot(a, b):
    return lax.dot_general(a, b, (((0,), (0,)), ((), ())), preferred_element_type=jnp.float32)


SLOT_TIERS = (2, 4, MAXB)


def gather_blocks(ref, cols_ref, r, slots):
    return jnp.concatenate(
        [
            ref[pl.ds(pl.multiple_of(cols_ref[r * MAXB + s] * BLK, BLK), BLK), :]
            for s in range(slots)
        ],
        axis=0,
    )


def live_lanes(cnt, slots):
    return lax.broadcasted_iota(jnp.int32, (1, slots * BLK), 1) < cnt * BLK


def by_tier(cnt, body):
    low = 0
    for slots in SLOT_TIERS:
        pl.when((cnt > low) & (cnt <= slots))(functools.partial(body, slots))
        low = slots


def attn_fwd_kernel(cols_ref, counts_ref, q_ref, k_ref, v_ref, o_ref, lse_ref):
    width = q_ref.shape[1]
    nblk = q_ref.shape[0] // BLK
    masks = head_masks(width)
    rows = len(masks) * BLK

    def row_body(r, carry):
        row0 = pl.multiple_of(r * BLK, BLK)
        cnt = counts_ref[r]

        def tier(slots):
            live = live_lanes(cnt, slots)
            q2 = stack_heads(q_ref[pl.ds(row0, BLK), :], masks)
            kc = gather_blocks(k_ref, cols_ref, r, slots)
            sc = jnp.where(live, nt_dot(q2, kc) * SCALE, NEG)
            m = jnp.max(sc, axis=1, keepdims=True)
            e = jnp.where(live, jnp.exp(sc - m), 0.0)
            l = jnp.sum(e, axis=1, keepdims=True)
            p = (e * (1.0 / l)).astype(jnp.bfloat16)
            vc = gather_blocks(v_ref, cols_ref, r, slots)
            acc = jnp.dot(p, vc, preferred_element_type=jnp.float32)
            o_ref[pl.ds(row0, BLK), :] = unstack_heads(acc, masks).astype(o_ref.dtype)
            lse_ref[pl.ds(pl.multiple_of(r * rows, rows), rows), :] = jnp.broadcast_to(
                m + jnp.log(l), (rows, lse_ref.shape[1])
            )

        by_tier(cnt, tier)
        return carry

    lax.fori_loop(0, nblk, row_body, 0)


def attn_bwd_kernel(
    cols_ref, counts_ref, q_ref, k_ref, v_ref, o_ref, do_ref, lse_ref, dq_ref, dk_ref, dv_ref, dk_acc, dv_acc
):
    width = q_ref.shape[1]
    nblk = q_ref.shape[0] // BLK
    masks = head_masks(width)
    rows = len(masks) * BLK
    dk_acc[...] = jnp.zeros_like(dk_acc)
    dv_acc[...] = jnp.zeros_like(dv_acc)

    def row_body(r, carry):
        row0 = pl.multiple_of(r * BLK, BLK)
        cnt = counts_ref[r]

        def tier(slots):
            live = live_lanes(cnt, slots)
            q2 = stack_heads(q_ref[pl.ds(row0, BLK), :], masks)
            do_blk = do_ref[pl.ds(row0, BLK), :]
            do2 = stack_heads(do_blk, masks)
            prod = o_ref[pl.ds(row0, BLK), :].astype(jnp.float32) * do_blk.astype(jnp.float32)
            delta = jnp.concatenate(
                [jnp.sum(jnp.where(m, prod, 0.0), axis=1, keepdims=True) for m in masks], axis=0
            )
            lse_t = jnp.transpose(lse_ref[pl.ds(pl.multiple_of(r * rows, rows), rows), :])[0:1, :]
            delta_t = jnp.transpose(jnp.broadcast_to(delta, (rows, BLK)))[0:1, :]
            live_t = lax.broadcasted_iota(jnp.int32, (slots * BLK, 1), 0) < cnt * BLK
            kc = gather_blocks(k_ref, cols_ref, r, slots)
            vc = gather_blocks(v_ref, cols_ref, r, slots)
            sc_t = nt_dot(kc, q2) * SCALE
            p_t = jnp.where(live_t, jnp.exp(sc_t - lse_t), 0.0).astype(jnp.bfloat16)
            dp_t = nt_dot(vc, do2)
            ds_t = (p_t.astype(jnp.float32) * (dp_t - delta_t) * SCALE).astype(jnp.bfloat16)
            dq = tn_dot(ds_t, kc)
            dq_ref[pl.ds(row0, BLK), :] = unstack_heads(dq, masks).astype(dq_ref.dtype)
            dkc = jnp.dot(ds_t, q2, preferred_element_type=jnp.float32)
            dvc = jnp.dot(p_t, do2, preferred_element_type=jnp.float32)
            for s in range(slots):

                @pl.when(s < cnt)
                def _():
                    col0 = pl.multiple_of(cols_ref[r * MAXB + s] * BLK, BLK)
                    dk_acc[pl.ds(col0, BLK), :] += dkc[s * BLK : (s + 1) * BLK]
                    dv_acc[pl.ds(col0, BLK), :] += dvc[s * BLK : (s + 1) * BLK]

        by_tier(cnt, tier)
        return carry

    lax.fori_loop(0, nblk, row_body, 0)
    dk_ref[...] = dk_acc[...].astype(dk_ref.dtype)
    dv_ref[...] = dv_acc[...].astype(dv_ref.dtype)


def smem_spec():
    return pl.BlockSpec(memory_space=pltpu.SMEM)


def vmem_spec():
    return pl.BlockSpec(memory_space=pltpu.VMEM)


VMEM_LIMIT = 48 * 1024 * 1024


def attention_forward(q, k, v, cols, counts):
    n, width = q.shape
    rows = (width // HD) * BLK
    return pl.pallas_call(
        attn_fwd_kernel,
        out_shape=(
            jax.ShapeDtypeStruct((n, width), jnp.bfloat16),
            jax.ShapeDtypeStruct(((n // BLK) * rows, 128), jnp.float32),
        ),
        in_specs=[smem_spec(), smem_spec(), vmem_spec(), vmem_spec(), vmem_spec()],
        out_specs=(vmem_spec(), vmem_spec()),
        compiler_params=pltpu.CompilerParams(vmem_limit_bytes=VMEM_LIMIT),
    )(cols, counts, q, k, v)


def attention_backward(q, k, v, o, do, lse, cols, counts):
    n, width = q.shape
    return pl.pallas_call(
        attn_bwd_kernel,
        out_shape=tuple(jax.ShapeDtypeStruct((n, width), jnp.bfloat16) for _ in range(3)),
        in_specs=[smem_spec(), smem_spec()] + [vmem_spec()] * 6,
        out_specs=(vmem_spec(), vmem_spec(), vmem_spec()),
        scratch_shapes=[pltpu.VMEM((n, width), jnp.float32), pltpu.VMEM((n, width), jnp.float32)],
        compiler_params=pltpu.CompilerParams(vmem_limit_bytes=VMEM_LIMIT),
    )(cols, counts, q, k, v, o, do, lse)


def regroup_columns(moved, seq_count, group_width):
    rows = moved.shape[0]
    return (
        moved.reshape(rows, seq_count, 3, group_width)
        .transpose(0, 2, 1, 3)
        .reshape(rows, 3 * seq_count * group_width)
    )


MESH = pl.DeviceIdType.MESH


def exchange_kernel(
    n, m, x_ref, g_ref, a_ref, o_ref, moved_ref, att_ref, recv, gath, landed, att_landed, sems, a2a_sems
):
    me = lax.axis_index("dp")
    here = lax.axis_index("seq")
    barrier = pltpu.get_barrier_semaphore()
    for k in range(1, n):
        pl.semaphore_signal(
            barrier, inc=1, device_id={"dp": lax.rem(me + k, n)}, device_id_type=MESH
        )
    for k in range(1, m):
        pl.semaphore_signal(
            barrier, inc=1, device_id={"seq": lax.rem(here + k, m)}, device_id_type=MESH
        )
    pl.semaphore_wait(barrier, n - 1 + m - 1)

    def start_all(src_of, dst, send, arrive, axis, at, size):
        started = []
        for k in range(1, size):
            peer = lax.rem(at + k, size)
            copy = pltpu.make_async_remote_copy(
                src_ref=src_of(peer),
                dst_ref=dst.at[at],
                send_sem=send.at[peer],
                recv_sem=arrive.at[at],
                device_id={axis: peer},
                device_id_type=MESH,
            )
            copy.start()
            started.append(copy)
        return started

    def finish_all(started, src_of, dst, send, arrive, axis, at, size):
        for k in range(1, size):
            source = lax.rem(at + size - k, size)
            pltpu.make_async_remote_copy(
                src_ref=src_of(source),
                dst_ref=dst.at[source],
                send_sem=send.at[source],
                recv_sem=arrive.at[source],
                device_id={axis: source},
                device_id_type=MESH,
            ).wait_recv()
        for copy in started:
            copy.wait_send()

    parts = g_ref.shape[2] // BLK
    group = BLK * m

    def part_copy(t, peer, sender, target):
        return pltpu.make_async_remote_copy(
            src_ref=g_ref.at[peer, :, pl.ds(t * BLK, BLK)],
            dst_ref=landed.at[:, pl.ds(pl.multiple_of(t * group + sender * BLK, BLK), BLK)],
            send_sem=a2a_sems.at[0, t, peer],
            recv_sem=a2a_sems.at[1, t, sender],
            device_id={"seq": target},
            device_id_type=MESH,
        )

    width = a_ref.shape[2]

    def att_copy(peer, sender, target):
        return pltpu.make_async_remote_copy(
            src_ref=a_ref.at[peer],
            dst_ref=att_landed.at[:, pl.ds(pl.multiple_of(sender * width, width), width)],
            send_sem=a2a_sems.at[0, parts, peer],
            recv_sem=a2a_sems.at[1, parts, sender],
            device_id={"seq": target},
            device_id_type=MESH,
        )

    a2a_started = []
    for k in range(1, m):
        peer = lax.rem(here + k, m)
        copy = att_copy(peer, here, peer)
        copy.start()
        a2a_started.append(copy)
    for k in range(1, m):
        peer = lax.rem(here + k, m)
        for t in range(parts):
            copy = part_copy(t, peer, here, peer)
            copy.start()
            a2a_started.append(copy)
    rs = (lambda peer: x_ref.at[peer], recv, sems.at[0], sems.at[1], "dp", me, n)
    finish_all(start_all(*rs), *rs)
    total = x_ref[me]
    for k in range(1, n):
        total = total + recv[lax.rem(me + k, n)]
    gath[me] = total.astype(gath.dtype)
    ag = (lambda peer: gath.at[me], gath, sems.at[2], sems.at[3], "dp", me, n)
    finish_all(start_all(*ag), *ag)
    o_ref[...] = gath[...]
    own = g_ref[here]
    for t in range(parts):
        landed[:, pl.ds(pl.multiple_of(t * group + here * BLK, BLK), BLK)] = own[
            :, t * BLK : (t + 1) * BLK
        ]
    att_landed[:, pl.ds(pl.multiple_of(here * width, width), width)] = a_ref[here]
    for k in range(1, m):
        source = lax.rem(here + m - k, m)
        att_copy(source, source, source).wait_recv()
        for t in range(parts):
            part_copy(t, source, source, source).wait_recv()
    for copy in a2a_started:
        copy.wait_send()
    moved_ref[...] = landed[...]
    att_ref[...] = att_landed[...]


def sum_and_exchange(term, grads, attended_heads):
    n = lax.axis_size("dp")
    m = lax.axis_size("seq")
    rows, cols = term.shape
    chunked = term.reshape(n, rows // n, cols)
    pieces = grads.reshape(m, grads.shape[0] // m, grads.shape[1])
    att_pieces = attended_heads.reshape(m, attended_heads.shape[0] // m, attended_heads.shape[1])
    parts = grads.shape[1] // BLK
    final = (pieces.shape[1], parts * m * BLK)
    att_final = (att_pieces.shape[1], m * att_pieces.shape[2])
    out, moved, attended = pl.pallas_call(
        functools.partial(exchange_kernel, n, m),
        out_shape=(
            jax.ShapeDtypeStruct(chunked.shape, jnp.bfloat16),
            jax.ShapeDtypeStruct(final, pieces.dtype),
            jax.ShapeDtypeStruct(att_final, att_pieces.dtype),
        ),
        in_specs=[vmem_spec(), vmem_spec(), vmem_spec()],
        out_specs=(vmem_spec(), vmem_spec(), vmem_spec()),
        scratch_shapes=[
            pltpu.VMEM(chunked.shape, jnp.float32),
            pltpu.VMEM(chunked.shape, jnp.bfloat16),
            pltpu.VMEM(final, pieces.dtype),
            pltpu.VMEM(att_final, att_pieces.dtype),
            pltpu.SemaphoreType.DMA((4, n)),
            pltpu.SemaphoreType.DMA((2, parts + 1, m)),
        ],
        compiler_params=pltpu.CompilerParams(
            collective_id=0, has_side_effects=True, vmem_limit_bytes=VMEM_LIMIT
        ),
    )(chunked, pieces, att_pieces)
    return out.reshape(rows, cols), moved, attended


def body(feats, gain, w_qkv, w_out, block_cols, block_counts, cotan):
    model_width = feats.shape[1]
    seq_count = lax.axis_size("seq")
    group_width = model_width // seq_count
    seq_at = lax.axis_index("seq")
    scaled, inverse, normed = layer_norm(feats, gain)
    normed_all = lax.all_gather(normed, "seq", axis=0, tiled=True)
    cotan_all = lax.all_gather(cotan, "seq", axis=0, tiled=True)
    w_heads = jnp.concatenate(
        [
            lax.dynamic_slice_in_dim(w_qkv, j * model_width + seq_at * group_width, group_width, 1)
            for j in range(3)
        ],
        axis=1,
    )
    mixed_heads = jnp.dot(normed_all, w_heads, preferred_element_type=jnp.float32).astype(
        jnp.bfloat16
    )
    query_heads = mixed_heads[:, :group_width]
    key_heads = mixed_heads[:, group_width : 2 * group_width]
    value_heads = mixed_heads[:, 2 * group_width :]
    cols = block_cols[0].reshape(-1)
    counts = block_counts[0]
    attended_heads, lse = attention_forward(query_heads, key_heads, value_heads, cols, counts)
    w_out_rows = lax.dynamic_slice_in_dim(w_out, seq_at * group_width, group_width, 0)
    grad_heads = lax.dot_general(
        cotan_all, w_out_rows, (((1,), (1,)), ((), ())), preferred_element_type=jnp.float32
    ).astype(jnp.bfloat16)
    query_grad, key_grad, value_grad = attention_backward(
        query_heads, key_heads, value_heads, attended_heads, grad_heads, lse, cols, counts
    )
    grad_heads_mixed = jnp.concatenate([query_grad, key_grad, value_grad], axis=1)
    term_qkv = contract_rows(normed_all, grad_heads_mixed)
    term_out = contract_rows(attended_heads, cotan_all)
    qkv_cols = term_qkv.shape[1]
    summed, moved_grads, attended = sum_and_exchange(
        jnp.concatenate([term_qkv, term_out.reshape(term_qkv.shape[0], -1)], axis=1),
        grad_heads_mixed,
        attended_heads,
    )
    result = (
        feats.astype(jnp.float32) + jnp.dot(attended, w_out, preferred_element_type=jnp.float32)
    ).astype(jnp.bfloat16)
    grad_mixed = moved_grads
    grad_normed = lax.dot_general(
        grad_mixed, w_qkv, (((1,), (1,)), ((), ())), preferred_element_type=jnp.float32
    )
    gained = grad_normed * gain[None, :]
    mean_one = jnp.mean(gained, axis=1, keepdims=True)
    mean_two = jnp.mean(gained * scaled, axis=1, keepdims=True)
    grad_feats = (
        cotan.astype(jnp.float32) + inverse * (gained - mean_one - scaled * mean_two)
    ).astype(jnp.bfloat16)
    term_qkv = summed[:, :qkv_cols]
    term_out = summed[:, qkv_cols:].reshape(term_out.shape)
    grad_qkv = regroup_columns(
        lax.all_to_all(term_qkv, "seq", split_axis=0, concat_axis=1, tiled=True),
        seq_count,
        group_width,
    )
    grad_out = term_out
    return (result, grad_feats, grad_qkv, grad_out)


def solution(mesh):
    in_specs = (
        P(("dp", "seq"), None),
        P(),
        P(),
        P(),
        P("dp", None, None),
        P("dp", None),
        P(("dp", "seq"), None),
    )
    out_specs = (P(("dp", "seq"), None), P(("dp", "seq"), None), P("seq", None), P("seq", None))
    return jax.shard_map(body, mesh=mesh, in_specs=in_specs, out_specs=out_specs, check_vma=False)
```

```python
import functools

import jax
import jax.numpy as jnp
from jax import lax
from jax.experimental import pallas as pl
from jax.experimental.pallas import tpu as pltpu
from jax.sharding import PartitionSpec as P

HD = 64
BLK = 128
MAXB = 8
SCALE = HD ** (-0.5)
NEG = -1e30

EPSILON = 1e-05


def layer_norm(feats, gain):
    values_f = feats.astype(jnp.float32)
    centred = values_f - jnp.mean(values_f, axis=1, keepdims=True)
    inverse = lax.rsqrt(jnp.mean(centred * centred, axis=1, keepdims=True) + EPSILON)
    scaled = centred * inverse
    return (scaled, inverse, (scaled * gain[None, :]).astype(jnp.bfloat16))


def contract_rows(left_cols, right_cols):
    return lax.dot_general(
        left_cols, right_cols, (((0,), (0,)), ((), ())), preferred_element_type=jnp.float32
    )


def head_masks(width):
    lane = lax.broadcasted_iota(jnp.int32, (1, width), 1)
    return [(lane >= h * HD) & (lane < (h + 1) * HD) for h in range(width // HD)]


def stack_heads(x, masks):
    return jnp.concatenate([jnp.where(m, x, jnp.zeros_like(x)) for m in masks], axis=0)


def unstack_heads(y, masks):
    out = y[0:BLK]
    for h in range(1, len(masks)):
        out = jnp.where(masks[h], y[h * BLK : (h + 1) * BLK], out)
    return out


def nt_dot(a, b):
    return lax.dot_general(a, b, (((1,), (1,)), ((), ())), preferred_element_type=jnp.float32)


def tn_dot(a, b):
    return lax.dot_general(a, b, (((0,), (0,)), ((), ())), preferred_element_type=jnp.float32)


SLOT_TIERS = (2, 4, MAXB)


def gather_blocks(ref, cols_ref, r, slots):
    return jnp.concatenate(
        [
            ref[pl.ds(pl.multiple_of(cols_ref[r * MAXB + s] * BLK, BLK), BLK), :]
            for s in range(slots)
        ],
        axis=0,
    )


def live_lanes(cnt, slots):
    return lax.broadcasted_iota(jnp.int32, (1, slots * BLK), 1) < cnt * BLK


FINE_TIERS = (1, 2, 3, 4, 6, MAXB)


def by_tier(cnt, body, tiers=SLOT_TIERS):
    low = 0
    for slots in tiers:
        pl.when((cnt > low) & (cnt <= slots))(functools.partial(body, slots))
        low = slots


def attn_fwd_kernel(cols_ref, counts_ref, q_ref, k_ref, v_ref, o_ref, lse_ref):
    width = q_ref.shape[1]
    nblk = q_ref.shape[0] // BLK
    masks = head_masks(width)
    rows = len(masks) * BLK

    def row_body(r, carry):
        row0 = pl.multiple_of(r * BLK, BLK)
        cnt = counts_ref[r]

        def tier(slots):
            live = live_lanes(cnt, slots)
            q2 = stack_heads(q_ref[pl.ds(row0, BLK), :], masks)
            kc = gather_blocks(k_ref, cols_ref, r, slots)
            sc = jnp.where(live, nt_dot(q2, kc) * SCALE, NEG)
            m = jnp.max(sc, axis=1, keepdims=True)
            e = jnp.where(live, jnp.exp(sc - m), 0.0)
            l = jnp.sum(e, axis=1, keepdims=True)
            p = (e * (1.0 / l)).astype(jnp.bfloat16)
            vc = gather_blocks(v_ref, cols_ref, r, slots)
            acc = jnp.dot(p, vc, preferred_element_type=jnp.float32)
            o_ref[pl.ds(row0, BLK), :] = unstack_heads(acc, masks).astype(o_ref.dtype)
            lse_ref[pl.ds(pl.multiple_of(r * rows, rows), rows), :] = jnp.broadcast_to(
                m + jnp.log(l), (rows, lse_ref.shape[1])
            )

        by_tier(cnt, tier)
        return carry

    lax.fori_loop(0, nblk, row_body, 0)


def attn_bwd_kernel(
    cols_ref, counts_ref, q_ref, k_ref, v_ref, o_ref, do_ref, lse_ref, dq_ref, dk_ref, dv_ref, dk_acc, dv_acc
):
    width = q_ref.shape[1]
    nblk = q_ref.shape[0] // BLK
    masks = head_masks(width)
    rows = len(masks) * BLK
    dk_acc[...] = jnp.zeros_like(dk_acc)
    dv_acc[...] = jnp.zeros_like(dv_acc)

    def row_body(r, carry):
        row0 = pl.multiple_of(r * BLK, BLK)
        cnt = counts_ref[r]

        def tier(slots):
            live = live_lanes(cnt, slots)
            q2 = stack_heads(q_ref[pl.ds(row0, BLK), :], masks)
            do_blk = do_ref[pl.ds(row0, BLK), :]
            do2 = stack_heads(do_blk, masks)
            prod = o_ref[pl.ds(row0, BLK), :].astype(jnp.float32) * do_blk.astype(jnp.float32)
            delta = jnp.concatenate(
                [jnp.sum(jnp.where(m, prod, 0.0), axis=1, keepdims=True) for m in masks], axis=0
            )
            lse = lse_ref[pl.ds(pl.multiple_of(r * rows, rows), rows), :][:, 0:1]
            kc = gather_blocks(k_ref, cols_ref, r, slots)
            vc = gather_blocks(v_ref, cols_ref, r, slots)
            sc = nt_dot(q2, kc) * SCALE
            p = jnp.where(live, jnp.exp(sc - lse), 0.0).astype(jnp.bfloat16)
            dp = nt_dot(do2, vc)
            ds = (p.astype(jnp.float32) * (dp - delta) * SCALE).astype(jnp.bfloat16)
            dq = jnp.dot(ds, kc, preferred_element_type=jnp.float32)
            dq_ref[pl.ds(row0, BLK), :] = unstack_heads(dq, masks).astype(dq_ref.dtype)
            dkc = tn_dot(ds, q2)
            dvc = tn_dot(p, do2)
            for s in range(slots):

                @pl.when(s < cnt)
                def _():
                    col0 = pl.multiple_of(cols_ref[r * MAXB + s] * BLK, BLK)
                    dk_acc[pl.ds(col0, BLK), :] += dkc[s * BLK : (s + 1) * BLK]
                    dv_acc[pl.ds(col0, BLK), :] += dvc[s * BLK : (s + 1) * BLK]

        by_tier(cnt, tier, FINE_TIERS)
        return carry

    lax.fori_loop(0, nblk, row_body, 0)
    dk_ref[...] = dk_acc[...].astype(dk_ref.dtype)
    dv_ref[...] = dv_acc[...].astype(dv_ref.dtype)


def smem_spec():
    return pl.BlockSpec(memory_space=pltpu.SMEM)


def vmem_spec():
    return pl.BlockSpec(memory_space=pltpu.VMEM)


VMEM_LIMIT = 48 * 1024 * 1024


def attention_forward(q, k, v, cols, counts):
    n, width = q.shape
    rows = (width // HD) * BLK
    return pl.pallas_call(
        attn_fwd_kernel,
        out_shape=(
            jax.ShapeDtypeStruct((n, width), jnp.bfloat16),
            jax.ShapeDtypeStruct(((n // BLK) * rows, 128), jnp.float32),
        ),
        in_specs=[smem_spec(), smem_spec(), vmem_spec(), vmem_spec(), vmem_spec()],
        out_specs=(vmem_spec(), vmem_spec()),
        compiler_params=pltpu.CompilerParams(vmem_limit_bytes=VMEM_LIMIT),
    )(cols, counts, q, k, v)


def attention_backward(q, k, v, o, do, lse, cols, counts):
    n, width = q.shape
    return pl.pallas_call(
        attn_bwd_kernel,
        out_shape=tuple(jax.ShapeDtypeStruct((n, width), jnp.bfloat16) for _ in range(3)),
        in_specs=[smem_spec(), smem_spec()] + [vmem_spec()] * 6,
        out_specs=(vmem_spec(), vmem_spec(), vmem_spec()),
        scratch_shapes=[pltpu.VMEM((n, width), jnp.float32), pltpu.VMEM((n, width), jnp.float32)],
        compiler_params=pltpu.CompilerParams(vmem_limit_bytes=VMEM_LIMIT),
    )(cols, counts, q, k, v, o, do, lse)


def regroup_columns(moved, seq_count, group_width):
    rows = moved.shape[0]
    return (
        moved.reshape(rows, seq_count, 3, group_width)
        .transpose(0, 2, 1, 3)
        .reshape(rows, 3 * seq_count * group_width)
    )


MESH = pl.DeviceIdType.MESH


def exchange_kernel(
    n, m, x_ref, g_ref, a_ref, o_ref, moved_ref, att_ref, recv, gath, landed, att_landed, sems, a2a_sems
):
    me = lax.axis_index("dp")
    here = lax.axis_index("seq")
    barrier = pltpu.get_barrier_semaphore()
    for k in range(1, n):
        pl.semaphore_signal(
            barrier, inc=1, device_id={"dp": lax.rem(me + k, n)}, device_id_type=MESH
        )
    for k in range(1, m):
        pl.semaphore_signal(
            barrier, inc=1, device_id={"seq": lax.rem(here + k, m)}, device_id_type=MESH
        )
    pl.semaphore_wait(barrier, n - 1 + m - 1)

    def start_all(src_of, dst, send, arrive, axis, at, size):
        started = []
        for k in range(1, size):
            peer = lax.rem(at + k, size)
            copy = pltpu.make_async_remote_copy(
                src_ref=src_of(peer),
                dst_ref=dst.at[at],
                send_sem=send.at[peer],
                recv_sem=arrive.at[at],
                device_id={axis: peer},
                device_id_type=MESH,
            )
            copy.start()
            started.append(copy)
        return started

    def finish_all(started, src_of, dst, send, arrive, axis, at, size):
        for k in range(1, size):
            source = lax.rem(at + size - k, size)
            pltpu.make_async_remote_copy(
                src_ref=src_of(source),
                dst_ref=dst.at[source],
                send_sem=send.at[source],
                recv_sem=arrive.at[source],
                device_id={axis: source},
                device_id_type=MESH,
            ).wait_recv()
        for copy in started:
            copy.wait_send()

    parts = g_ref.shape[2] // BLK
    group = BLK * m

    def part_copy(t, peer, sender, target):
        return pltpu.make_async_remote_copy(
            src_ref=g_ref.at[peer, :, pl.ds(t * BLK, BLK)],
            dst_ref=landed.at[:, pl.ds(pl.multiple_of(t * group + sender * BLK, BLK), BLK)],
            send_sem=a2a_sems.at[0, t, peer],
            recv_sem=a2a_sems.at[1, t, sender],
            device_id={"seq": target},
            device_id_type=MESH,
        )

    width = a_ref.shape[2]

    def att_copy(peer, sender, target):
        return pltpu.make_async_remote_copy(
            src_ref=a_ref.at[peer],
            dst_ref=att_landed.at[:, pl.ds(pl.multiple_of(sender * width, width), width)],
            send_sem=a2a_sems.at[0, parts, peer],
            recv_sem=a2a_sems.at[1, parts, sender],
            device_id={"seq": target},
            device_id_type=MESH,
        )

    a2a_started = []
    for k in range(1, m):
        peer = lax.rem(here + k, m)
        copy = att_copy(peer, here, peer)
        copy.start()
        a2a_started.append(copy)
    for k in range(1, m):
        peer = lax.rem(here + k, m)
        for t in range(parts):
            copy = part_copy(t, peer, here, peer)
            copy.start()
            a2a_started.append(copy)
    rs = (lambda peer: x_ref.at[peer], recv, sems.at[0], sems.at[1], "dp", me, n)
    finish_all(start_all(*rs), *rs)
    total = x_ref[me]
    for k in range(1, n):
        total = total + recv[lax.rem(me + k, n)]
    gath[me] = total.astype(gath.dtype)
    ag = (lambda peer: gath.at[me], gath, sems.at[2], sems.at[3], "dp", me, n)
    finish_all(start_all(*ag), *ag)
    o_ref[...] = gath[...]
    own = g_ref[here]
    for t in range(parts):
        landed[:, pl.ds(pl.multiple_of(t * group + here * BLK, BLK), BLK)] = own[
            :, t * BLK : (t + 1) * BLK
        ]
    att_landed[:, pl.ds(pl.multiple_of(here * width, width), width)] = a_ref[here]
    for k in range(1, m):
        source = lax.rem(here + m - k, m)
        att_copy(source, source, source).wait_recv()
        for t in range(parts):
            part_copy(t, source, source, source).wait_recv()
    for copy in a2a_started:
        copy.wait_send()
    moved_ref[...] = landed[...]
    att_ref[...] = att_landed[...]


def sum_and_exchange(term, grads, attended_heads):
    n = lax.axis_size("dp")
    m = lax.axis_size("seq")
    rows, cols = term.shape
    chunked = term.reshape(n, rows // n, cols)
    pieces = grads.reshape(m, grads.shape[0] // m, grads.shape[1])
    att_pieces = attended_heads.reshape(m, attended_heads.shape[0] // m, attended_heads.shape[1])
    parts = grads.shape[1] // BLK
    final = (pieces.shape[1], parts * m * BLK)
    att_final = (att_pieces.shape[1], m * att_pieces.shape[2])
    out, moved, attended = pl.pallas_call(
        functools.partial(exchange_kernel, n, m),
        out_shape=(
            jax.ShapeDtypeStruct(chunked.shape, jnp.bfloat16),
            jax.ShapeDtypeStruct(final, pieces.dtype),
            jax.ShapeDtypeStruct(att_final, att_pieces.dtype),
        ),
        in_specs=[vmem_spec(), vmem_spec(), vmem_spec()],
        out_specs=(vmem_spec(), vmem_spec(), vmem_spec()),
        scratch_shapes=[
            pltpu.VMEM(chunked.shape, jnp.float32),
            pltpu.VMEM(chunked.shape, jnp.bfloat16),
            pltpu.VMEM(final, pieces.dtype),
            pltpu.VMEM(att_final, att_pieces.dtype),
            pltpu.SemaphoreType.DMA((4, n)),
            pltpu.SemaphoreType.DMA((2, parts + 1, m)),
        ],
        compiler_params=pltpu.CompilerParams(
            collective_id=0, has_side_effects=True, vmem_limit_bytes=VMEM_LIMIT
        ),
    )(chunked, pieces, att_pieces)
    return out.reshape(rows, cols), moved, attended


def body(feats, gain, w_qkv, w_out, block_cols, block_counts, cotan):
    model_width = feats.shape[1]
    seq_count = lax.axis_size("seq")
    group_width = model_width // seq_count
    seq_at = lax.axis_index("seq")
    scaled, inverse, normed = layer_norm(feats, gain)
    normed_all = lax.all_gather(normed, "seq", axis=0, tiled=True)
    cotan_all = lax.all_gather(cotan, "seq", axis=0, tiled=True)
    w_heads = jnp.concatenate(
        [
            lax.dynamic_slice_in_dim(w_qkv, j * model_width + seq_at * group_width, group_width, 1)
            for j in range(3)
        ],
        axis=1,
    )
    mixed_heads = jnp.dot(normed_all, w_heads, preferred_element_type=jnp.float32).astype(
        jnp.bfloat16
    )
    query_heads = mixed_heads[:, :group_width]
    key_heads = mixed_heads[:, group_width : 2 * group_width]
    value_heads = mixed_heads[:, 2 * group_width :]
    cols = block_cols[0].reshape(-1)
    counts = block_counts[0]
    attended_heads, lse = attention_forward(query_heads, key_heads, value_heads, cols, counts)
    w_out_rows = lax.dynamic_slice_in_dim(w_out, seq_at * group_width, group_width, 0)
    grad_heads = lax.dot_general(
        cotan_all, w_out_rows, (((1,), (1,)), ((), ())), preferred_element_type=jnp.float32
    ).astype(jnp.bfloat16)
    query_grad, key_grad, value_grad = attention_backward(
        query_heads, key_heads, value_heads, attended_heads, grad_heads, lse, cols, counts
    )
    grad_heads_mixed = jnp.concatenate([query_grad, key_grad, value_grad], axis=1)
    term_qkv = contract_rows(normed_all, grad_heads_mixed)
    term_out = contract_rows(attended_heads, cotan_all)
    qkv_cols = term_qkv.shape[1]
    summed, moved_grads, attended = sum_and_exchange(
        jnp.concatenate([term_qkv, term_out.reshape(term_qkv.shape[0], -1)], axis=1),
        grad_heads_mixed,
        attended_heads,
    )
    result = (
        feats.astype(jnp.float32) + jnp.dot(attended, w_out, preferred_element_type=jnp.float32)
    ).astype(jnp.bfloat16)
    grad_mixed = moved_grads
    grad_normed = lax.dot_general(
        grad_mixed, w_qkv, (((1,), (1,)), ((), ())), preferred_element_type=jnp.float32
    )
    gained = grad_normed * gain[None, :]
    mean_one = jnp.mean(gained, axis=1, keepdims=True)
    mean_two = jnp.mean(gained * scaled, axis=1, keepdims=True)
    grad_feats = (
        cotan.astype(jnp.float32) + inverse * (gained - mean_one - scaled * mean_two)
    ).astype(jnp.bfloat16)
    term_qkv = summed[:, :qkv_cols]
    term_out = summed[:, qkv_cols:].reshape(term_out.shape)
    grad_qkv = regroup_columns(
        lax.all_to_all(term_qkv, "seq", split_axis=0, concat_axis=1, tiled=True),
        seq_count,
        group_width,
    )
    grad_out = term_out
    return (result, grad_feats, grad_qkv, grad_out)


def solution(mesh):
    in_specs = (
        P(("dp", "seq"), None),
        P(),
        P(),
        P(),
        P("dp", None, None),
        P("dp", None),
        P(("dp", "seq"), None),
    )
    out_specs = (P(("dp", "seq"), None), P(("dp", "seq"), None), P("seq", None), P("seq", None))
    return jax.shard_map(body, mesh=mesh, in_specs=in_specs, out_specs=out_specs, check_vma=False)
```

```python
import functools

import jax
import jax.numpy as jnp
from jax import lax
from jax.experimental import pallas as pl
from jax.experimental.pallas import tpu as pltpu
from jax.sharding import PartitionSpec as P

HD = 64
BLK = 128
MAXB = 8
SCALE = HD ** (-0.5)
NEG = -1e30

EPSILON = 1e-05


def layer_norm(feats, gain):
    values_f = feats.astype(jnp.float32)
    centred = values_f - jnp.mean(values_f, axis=1, keepdims=True)
    inverse = lax.rsqrt(jnp.mean(centred * centred, axis=1, keepdims=True) + EPSILON)
    scaled = centred * inverse
    return (scaled, inverse, (scaled * gain[None, :]).astype(jnp.bfloat16))


def contract_rows(left_cols, right_cols):
    return lax.dot_general(
        left_cols, right_cols, (((0,), (0,)), ((), ())), preferred_element_type=jnp.float32
    )


def head_masks(width):
    lane = lax.broadcasted_iota(jnp.int32, (1, width), 1)
    return [(lane >= h * HD) & (lane < (h + 1) * HD) for h in range(width // HD)]


def stack_heads(x, masks):
    return jnp.concatenate([jnp.where(m, x, jnp.zeros_like(x)) for m in masks], axis=0)


def unstack_heads(y, masks):
    out = y[0:BLK]
    for h in range(1, len(masks)):
        out = jnp.where(masks[h], y[h * BLK : (h + 1) * BLK], out)
    return out


def nt_dot(a, b):
    return lax.dot_general(a, b, (((1,), (1,)), ((), ())), preferred_element_type=jnp.float32)


def tn_dot(a, b):
    return lax.dot_general(a, b, (((0,), (0,)), ((), ())), preferred_element_type=jnp.float32)


SLOT_TIERS = (2, 4, MAXB)


def gather_blocks(ref, cols_ref, r, slots):
    return jnp.concatenate(
        [
            ref[pl.ds(pl.multiple_of(cols_ref[r * MAXB + s] * BLK, BLK), BLK), :]
            for s in range(slots)
        ],
        axis=0,
    )


def live_lanes(cnt, slots):
    return lax.broadcasted_iota(jnp.int32, (1, slots * BLK), 1) < cnt * BLK


FINE_TIERS = (1, 2, 3, 4, 6, MAXB)


def by_tier(cnt, body, tiers=SLOT_TIERS):
    low = 0
    for slots in tiers:
        pl.when((cnt > low) & (cnt <= slots))(functools.partial(body, slots))
        low = slots


def attn_fwd_kernel(cols_ref, counts_ref, q_ref, k_ref, v_ref, o_ref, lse_ref):
    width = q_ref.shape[1]
    nblk = q_ref.shape[0] // BLK
    masks = head_masks(width)
    rows = len(masks) * BLK

    def row_body(r, carry):
        row0 = pl.multiple_of(r * BLK, BLK)
        cnt = counts_ref[r]

        def tier(slots):
            live = live_lanes(cnt, slots)
            q2 = stack_heads(q_ref[pl.ds(row0, BLK), :], masks)
            kc = gather_blocks(k_ref, cols_ref, r, slots)
            sc = jnp.where(live, nt_dot(q2, kc) * SCALE, NEG)
            m = jnp.max(sc, axis=1, keepdims=True)
            e = jnp.where(live, jnp.exp(sc - m), 0.0)
            l = jnp.sum(e, axis=1, keepdims=True)
            p = (e * (1.0 / l)).astype(jnp.bfloat16)
            vc = gather_blocks(v_ref, cols_ref, r, slots)
            acc = jnp.dot(p, vc, preferred_element_type=jnp.float32)
            o_ref[pl.ds(row0, BLK), :] = unstack_heads(acc, masks).astype(o_ref.dtype)
            lse_ref[pl.ds(pl.multiple_of(r * rows, rows), rows), :] = jnp.broadcast_to(
                m + jnp.log(l), (rows, lse_ref.shape[1])
            )

        by_tier(cnt, tier)
        return carry

    lax.fori_loop(0, nblk, row_body, 0)


def attn_bwd_kernel(
    cols_ref, counts_ref, q_ref, k_ref, v_ref, o_ref, do_ref, lse_ref, dq_ref, dk_ref, dv_ref, dk_acc, dv_acc
):
    width = q_ref.shape[1]
    nblk = q_ref.shape[0] // BLK
    masks = head_masks(width)
    rows = len(masks) * BLK
    dk_acc[...] = jnp.zeros_like(dk_acc)
    dv_acc[...] = jnp.zeros_like(dv_acc)

    def row_body(r, carry):
        row0 = pl.multiple_of(r * BLK, BLK)
        cnt = counts_ref[r]

        def tier(slots):
            live = live_lanes(cnt, slots)
            q2 = stack_heads(q_ref[pl.ds(row0, BLK), :], masks)
            do_blk = do_ref[pl.ds(row0, BLK), :]
            do2 = stack_heads(do_blk, masks)
            prod = o_ref[pl.ds(row0, BLK), :].astype(jnp.float32) * do_blk.astype(jnp.float32)
            delta = jnp.concatenate(
                [jnp.sum(jnp.where(m, prod, 0.0), axis=1, keepdims=True) for m in masks], axis=0
            )
            lse = lse_ref[pl.ds(pl.multiple_of(r * rows, rows), rows), :][:, 0:1]
            kc = gather_blocks(k_ref, cols_ref, r, slots)
            vc = gather_blocks(v_ref, cols_ref, r, slots)
            sc = nt_dot(q2, kc) * SCALE
            p = jnp.where(live, jnp.exp(sc - lse), 0.0).astype(jnp.bfloat16)
            dp = nt_dot(do2, vc)
            ds = (p.astype(jnp.float32) * (dp - delta) * SCALE).astype(jnp.bfloat16)
            dq = jnp.dot(ds, kc, preferred_element_type=jnp.float32)
            dq_ref[pl.ds(row0, BLK), :] = unstack_heads(dq, masks).astype(dq_ref.dtype)
            dkc = tn_dot(ds, q2)
            dvc = tn_dot(p, do2)
            for s in range(slots):

                @pl.when(s < cnt)
                def _():
                    col0 = pl.multiple_of(cols_ref[r * MAXB + s] * BLK, BLK)
                    dk_acc[pl.ds(col0, BLK), :] += dkc[s * BLK : (s + 1) * BLK]
                    dv_acc[pl.ds(col0, BLK), :] += dvc[s * BLK : (s + 1) * BLK]

        by_tier(cnt, tier, FINE_TIERS)
        return carry

    lax.fori_loop(0, nblk, row_body, 0)
    dk_ref[...] = dk_acc[...].astype(dk_ref.dtype)
    dv_ref[...] = dv_acc[...].astype(dv_ref.dtype)


def smem_spec():
    return pl.BlockSpec(memory_space=pltpu.SMEM)


def vmem_spec():
    return pl.BlockSpec(memory_space=pltpu.VMEM)


VMEM_LIMIT = 48 * 1024 * 1024


def attention_forward(q, k, v, cols, counts):
    n, width = q.shape
    rows = (width // HD) * BLK
    return pl.pallas_call(
        attn_fwd_kernel,
        out_shape=(
            jax.ShapeDtypeStruct((n, width), jnp.bfloat16),
            jax.ShapeDtypeStruct(((n // BLK) * rows, 128), jnp.float32),
        ),
        in_specs=[smem_spec(), smem_spec(), vmem_spec(), vmem_spec(), vmem_spec()],
        out_specs=(vmem_spec(), vmem_spec()),
        compiler_params=pltpu.CompilerParams(vmem_limit_bytes=VMEM_LIMIT),
    )(cols, counts, q, k, v)


def attention_backward(q, k, v, o, do, lse, cols, counts):
    n, width = q.shape
    return pl.pallas_call(
        attn_bwd_kernel,
        out_shape=tuple(jax.ShapeDtypeStruct((n, width), jnp.bfloat16) for _ in range(3)),
        in_specs=[smem_spec(), smem_spec()] + [vmem_spec()] * 6,
        out_specs=(vmem_spec(), vmem_spec(), vmem_spec()),
        scratch_shapes=[pltpu.VMEM((n, width), jnp.float32), pltpu.VMEM((n, width), jnp.float32)],
        compiler_params=pltpu.CompilerParams(vmem_limit_bytes=VMEM_LIMIT),
    )(cols, counts, q, k, v, o, do, lse)


def regroup_columns(moved, seq_count, group_width):
    rows = moved.shape[0]
    return (
        moved.reshape(rows, seq_count, 3, group_width)
        .transpose(0, 2, 1, 3)
        .reshape(rows, 3 * seq_count * group_width)
    )


MESH = pl.DeviceIdType.MESH


def exchange_kernel(
    n, m, x_ref, g_ref, a_ref, o_ref, moved_ref, att_ref, recv, gath, landed, att_landed, sems, a2a_sems
):
    me = lax.axis_index("dp")
    here = lax.axis_index("seq")
    barrier = pltpu.get_barrier_semaphore()
    for k in range(1, n):
        pl.semaphore_signal(
            barrier, inc=1, device_id={"dp": lax.rem(me + k, n)}, device_id_type=MESH
        )
    for k in range(1, m):
        pl.semaphore_signal(
            barrier, inc=1, device_id={"seq": lax.rem(here + k, m)}, device_id_type=MESH
        )
    pl.semaphore_wait(barrier, n - 1 + m - 1)

    def start_all(src_of, dst, send, arrive, axis, at, size):
        started = []
        for k in range(1, size):
            peer = lax.rem(at + k, size)
            copy = pltpu.make_async_remote_copy(
                src_ref=src_of(peer),
                dst_ref=dst.at[at],
                send_sem=send.at[peer],
                recv_sem=arrive.at[at],
                device_id={axis: peer},
                device_id_type=MESH,
            )
            copy.start()
            started.append(copy)
        return started

    def finish_all(started, src_of, dst, send, arrive, axis, at, size):
        for k in range(1, size):
            source = lax.rem(at + size - k, size)
            pltpu.make_async_remote_copy(
                src_ref=src_of(source),
                dst_ref=dst.at[source],
                send_sem=send.at[source],
                recv_sem=arrive.at[source],
                device_id={axis: source},
                device_id_type=MESH,
            ).wait_recv()
        for copy in started:
            copy.wait_send()

    parts = g_ref.shape[2] // BLK
    group = BLK * m

    def part_copy(t, peer, sender, target):
        return pltpu.make_async_remote_copy(
            src_ref=g_ref.at[peer, :, pl.ds(t * BLK, BLK)],
            dst_ref=landed.at[:, pl.ds(pl.multiple_of(t * group + sender * BLK, BLK), BLK)],
            send_sem=a2a_sems.at[0, t, peer],
            recv_sem=a2a_sems.at[1, t, sender],
            device_id={"seq": target},
            device_id_type=MESH,
        )

    width = a_ref.shape[2]

    def att_copy(peer, sender, target):
        return pltpu.make_async_remote_copy(
            src_ref=a_ref.at[peer],
            dst_ref=att_landed.at[:, pl.ds(pl.multiple_of(sender * width, width), width)],
            send_sem=a2a_sems.at[0, parts, peer],
            recv_sem=a2a_sems.at[1, parts, sender],
            device_id={"seq": target},
            device_id_type=MESH,
        )

    rs = (lambda peer: x_ref.at[peer], recv, sems.at[0], sems.at[1], "dp", me, n)
    rs_started = start_all(*rs)
    a2a_started = []
    for k in range(1, m):
        peer = lax.rem(here + k, m)
        copy = att_copy(peer, here, peer)
        copy.start()
        a2a_started.append(copy)
    for k in range(1, m):
        peer = lax.rem(here + k, m)
        for t in range(parts):
            copy = part_copy(t, peer, here, peer)
            copy.start()
            a2a_started.append(copy)
    finish_all(rs_started, *rs)
    total = x_ref[me]
    for k in range(1, n):
        total = total + recv[lax.rem(me + k, n)]
    gath[me] = total.astype(gath.dtype)
    ag = (lambda peer: gath.at[me], gath, sems.at[2], sems.at[3], "dp", me, n)
    finish_all(start_all(*ag), *ag)
    o_ref[...] = gath[...]
    own = g_ref[here]
    for t in range(parts):
        landed[:, pl.ds(pl.multiple_of(t * group + here * BLK, BLK), BLK)] = own[
            :, t * BLK : (t + 1) * BLK
        ]
    att_landed[:, pl.ds(pl.multiple_of(here * width, width), width)] = a_ref[here]
    for k in range(1, m):
        source = lax.rem(here + m - k, m)
        att_copy(source, source, source).wait_recv()
        for t in range(parts):
            part_copy(t, source, source, source).wait_recv()
    for copy in a2a_started:
        copy.wait_send()
    moved_ref[...] = landed[...]
    att_ref[...] = att_landed[...]


def sum_and_exchange(term, grads, attended_heads):
    n = lax.axis_size("dp")
    m = lax.axis_size("seq")
    rows, cols = term.shape
    chunked = term.reshape(n, rows // n, cols)
    pieces = grads.reshape(m, grads.shape[0] // m, grads.shape[1])
    att_pieces = attended_heads.reshape(m, attended_heads.shape[0] // m, attended_heads.shape[1])
    parts = grads.shape[1] // BLK
    final = (pieces.shape[1], parts * m * BLK)
    att_final = (att_pieces.shape[1], m * att_pieces.shape[2])
    out, moved, attended = pl.pallas_call(
        functools.partial(exchange_kernel, n, m),
        out_shape=(
            jax.ShapeDtypeStruct(chunked.shape, jnp.bfloat16),
            jax.ShapeDtypeStruct(final, pieces.dtype),
            jax.ShapeDtypeStruct(att_final, att_pieces.dtype),
        ),
        in_specs=[vmem_spec(), vmem_spec(), vmem_spec()],
        out_specs=(vmem_spec(), vmem_spec(), vmem_spec()),
        scratch_shapes=[
            pltpu.VMEM(chunked.shape, jnp.float32),
            pltpu.VMEM(chunked.shape, jnp.bfloat16),
            pltpu.VMEM(final, pieces.dtype),
            pltpu.VMEM(att_final, att_pieces.dtype),
            pltpu.SemaphoreType.DMA((4, n)),
            pltpu.SemaphoreType.DMA((2, parts + 1, m)),
        ],
        compiler_params=pltpu.CompilerParams(
            collective_id=0, has_side_effects=True, vmem_limit_bytes=VMEM_LIMIT
        ),
    )(chunked, pieces, att_pieces)
    return out.reshape(rows, cols), moved, attended


def body(feats, gain, w_qkv, w_out, block_cols, block_counts, cotan):
    model_width = feats.shape[1]
    seq_count = lax.axis_size("seq")
    group_width = model_width // seq_count
    seq_at = lax.axis_index("seq")
    scaled, inverse, normed = layer_norm(feats, gain)
    normed_all = lax.all_gather(normed, "seq", axis=0, tiled=True)
    cotan_all = lax.all_gather(cotan, "seq", axis=0, tiled=True)
    w_heads = jnp.concatenate(
        [
            lax.dynamic_slice_in_dim(w_qkv, j * model_width + seq_at * group_width, group_width, 1)
            for j in range(3)
        ],
        axis=1,
    )
    mixed_heads = jnp.dot(normed_all, w_heads, preferred_element_type=jnp.float32).astype(
        jnp.bfloat16
    )
    query_heads = mixed_heads[:, :group_width]
    key_heads = mixed_heads[:, group_width : 2 * group_width]
    value_heads = mixed_heads[:, 2 * group_width :]
    cols = block_cols[0].reshape(-1)
    counts = block_counts[0]
    attended_heads, lse = attention_forward(query_heads, key_heads, value_heads, cols, counts)
    w_out_rows = lax.dynamic_slice_in_dim(w_out, seq_at * group_width, group_width, 0)
    grad_heads = lax.dot_general(
        cotan_all, w_out_rows, (((1,), (1,)), ((), ())), preferred_element_type=jnp.float32
    ).astype(jnp.bfloat16)
    query_grad, key_grad, value_grad = attention_backward(
        query_heads, key_heads, value_heads, attended_heads, grad_heads, lse, cols, counts
    )
    grad_heads_mixed = jnp.concatenate([query_grad, key_grad, value_grad], axis=1)
    term_qkv = contract_rows(normed_all, grad_heads_mixed)
    term_out = contract_rows(attended_heads, cotan_all)
    qkv_cols = term_qkv.shape[1]
    summed, moved_grads, attended = sum_and_exchange(
        jnp.concatenate([term_qkv, term_out.reshape(term_qkv.shape[0], -1)], axis=1),
        grad_heads_mixed,
        attended_heads,
    )
    result = (
        feats.astype(jnp.float32) + jnp.dot(attended, w_out, preferred_element_type=jnp.float32)
    ).astype(jnp.bfloat16)
    grad_mixed = moved_grads
    grad_normed = lax.dot_general(
        grad_mixed, w_qkv, (((1,), (1,)), ((), ())), preferred_element_type=jnp.float32
    )
    gained = grad_normed * gain[None, :]
    mean_one = jnp.mean(gained, axis=1, keepdims=True)
    mean_two = jnp.mean(gained * scaled, axis=1, keepdims=True)
    grad_feats = (
        cotan.astype(jnp.float32) + inverse * (gained - mean_one - scaled * mean_two)
    ).astype(jnp.bfloat16)
    term_qkv = summed[:, :qkv_cols]
    term_out = summed[:, qkv_cols:].reshape(term_out.shape)
    grad_qkv = regroup_columns(
        lax.all_to_all(term_qkv, "seq", split_axis=0, concat_axis=1, tiled=True),
        seq_count,
        group_width,
    )
    grad_out = term_out
    return (result, grad_feats, grad_qkv, grad_out)


def solution(mesh):
    in_specs = (
        P(("dp", "seq"), None),
        P(),
        P(),
        P(),
        P("dp", None, None),
        P("dp", None),
        P(("dp", "seq"), None),
    )
    out_specs = (P(("dp", "seq"), None), P(("dp", "seq"), None), P("seq", None), P("seq", None))
    return jax.shard_map(body, mesh=mesh, in_specs=in_specs, out_specs=out_specs, check_vma=False)
```

```python
import functools

import jax
import jax.numpy as jnp
from jax import lax
from jax.experimental import pallas as pl
from jax.experimental.pallas import tpu as pltpu
from jax.sharding import PartitionSpec as P

HD = 64
BLK = 128
MAXB = 8
SCALE = HD ** (-0.5)
NEG = -1e30

EPSILON = 1e-05


def layer_norm(feats, gain):
    values_f = feats.astype(jnp.float32)
    centred = values_f - jnp.mean(values_f, axis=1, keepdims=True)
    inverse = lax.rsqrt(jnp.mean(centred * centred, axis=1, keepdims=True) + EPSILON)
    scaled = centred * inverse
    return (scaled, inverse, (scaled * gain[None, :]).astype(jnp.bfloat16))


def contract_rows(left_cols, right_cols):
    return lax.dot_general(
        left_cols, right_cols, (((0,), (0,)), ((), ())), preferred_element_type=jnp.float32
    )


def head_masks(width):
    lane = lax.broadcasted_iota(jnp.int32, (1, width), 1)
    return [(lane >= h * HD) & (lane < (h + 1) * HD) for h in range(width // HD)]


def stack_heads(x, masks):
    return jnp.concatenate([jnp.where(m, x, jnp.zeros_like(x)) for m in masks], axis=0)


def unstack_heads(y, masks):
    out = y[0:BLK]
    for h in range(1, len(masks)):
        out = jnp.where(masks[h], y[h * BLK : (h + 1) * BLK], out)
    return out


def nt_dot(a, b):
    return lax.dot_general(a, b, (((1,), (1,)), ((), ())), preferred_element_type=jnp.float32)


def tn_dot(a, b):
    return lax.dot_general(a, b, (((0,), (0,)), ((), ())), preferred_element_type=jnp.float32)


SLOT_TIERS = (2, 4, MAXB)


def gather_blocks(ref, cols_ref, r, slots):
    return jnp.concatenate(
        [
            ref[pl.ds(pl.multiple_of(cols_ref[r * MAXB + s] * BLK, BLK), BLK), :]
            for s in range(slots)
        ],
        axis=0,
    )


def live_lanes(cnt, slots):
    return lax.broadcasted_iota(jnp.int32, (1, slots * BLK), 1) < cnt * BLK


FINE_TIERS = (1, 2, 3, 4, 6, MAXB)


def by_tier(cnt, body, tiers=SLOT_TIERS):
    low = 0
    for slots in tiers:
        pl.when((cnt > low) & (cnt <= slots))(functools.partial(body, slots))
        low = slots


def attn_fwd_kernel(cols_ref, counts_ref, q_ref, k_ref, v_ref, o_ref, lse_ref):
    width = q_ref.shape[1]
    nblk = q_ref.shape[0] // BLK
    masks = head_masks(width)
    rows = len(masks) * BLK

    def row_body(r, carry):
        row0 = pl.multiple_of(r * BLK, BLK)
        cnt = counts_ref[r]

        def tier(slots):
            live = live_lanes(cnt, slots)
            q2 = stack_heads(q_ref[pl.ds(row0, BLK), :], masks)
            kc = gather_blocks(k_ref, cols_ref, r, slots)
            sc = jnp.where(live, nt_dot(q2, kc) * SCALE, NEG)
            m = jnp.max(sc, axis=1, keepdims=True)
            e = jnp.where(live, jnp.exp(sc - m), 0.0)
            l = jnp.sum(e, axis=1, keepdims=True)
            p = (e * (1.0 / l)).astype(jnp.bfloat16)
            vc = gather_blocks(v_ref, cols_ref, r, slots)
            acc = jnp.dot(p, vc, preferred_element_type=jnp.float32)
            o_ref[pl.ds(row0, BLK), :] = unstack_heads(acc, masks).astype(o_ref.dtype)
            lse_ref[pl.ds(pl.multiple_of(r * rows, rows), rows), :] = jnp.broadcast_to(
                m + jnp.log(l), (rows, lse_ref.shape[1])
            )

        by_tier(cnt, tier)
        return carry

    lax.fori_loop(0, nblk, row_body, 0)


def attn_bwd_kernel(
    cols_ref, counts_ref, q_ref, k_ref, v_ref, o_ref, do_ref, lse_ref, dq_ref, dk_ref, dv_ref, dk_acc, dv_acc
):
    width = q_ref.shape[1]
    nblk = q_ref.shape[0] // BLK
    masks = head_masks(width)
    rows = len(masks) * BLK
    dk_acc[...] = jnp.zeros_like(dk_acc)
    dv_acc[...] = jnp.zeros_like(dv_acc)

    def row_body(r, carry):
        row0 = pl.multiple_of(r * BLK, BLK)
        cnt = counts_ref[r]

        def tier(slots):
            live = live_lanes(cnt, slots)
            q2 = stack_heads(q_ref[pl.ds(row0, BLK), :], masks)
            do_blk = do_ref[pl.ds(row0, BLK), :]
            do2 = stack_heads(do_blk, masks)
            prod = o_ref[pl.ds(row0, BLK), :].astype(jnp.float32) * do_blk.astype(jnp.float32)
            delta = jnp.concatenate(
                [jnp.sum(jnp.where(m, prod, 0.0), axis=1, keepdims=True) for m in masks], axis=0
            )
            lse = lse_ref[pl.ds(pl.multiple_of(r * rows, rows), rows), :][:, 0:1]
            kc = gather_blocks(k_ref, cols_ref, r, slots)
            vc = gather_blocks(v_ref, cols_ref, r, slots)
            sc = nt_dot(q2, kc) * SCALE
            p = jnp.where(live, jnp.exp(sc - lse), 0.0).astype(jnp.bfloat16)
            dp = nt_dot(do2, vc)
            ds = (p.astype(jnp.float32) * (dp - delta) * SCALE).astype(jnp.bfloat16)
            dq = jnp.dot(ds, kc, preferred_element_type=jnp.float32)
            dq_ref[pl.ds(row0, BLK), :] = unstack_heads(dq, masks).astype(dq_ref.dtype)
            dkc = tn_dot(ds, q2)
            dvc = tn_dot(p, do2)
            for s in range(slots):

                @pl.when(s < cnt)
                def _():
                    col0 = pl.multiple_of(cols_ref[r * MAXB + s] * BLK, BLK)
                    dk_acc[pl.ds(col0, BLK), :] += dkc[s * BLK : (s + 1) * BLK]
                    dv_acc[pl.ds(col0, BLK), :] += dvc[s * BLK : (s + 1) * BLK]

        by_tier(cnt, tier, FINE_TIERS)
        return carry

    lax.fori_loop(0, nblk, row_body, 0)
    dk_ref[...] = dk_acc[...].astype(dk_ref.dtype)
    dv_ref[...] = dv_acc[...].astype(dv_ref.dtype)


def smem_spec():
    return pl.BlockSpec(memory_space=pltpu.SMEM)


def vmem_spec():
    return pl.BlockSpec(memory_space=pltpu.VMEM)


VMEM_LIMIT = 48 * 1024 * 1024


def attention_forward(q, k, v, cols, counts):
    n, width = q.shape
    rows = (width // HD) * BLK
    return pl.pallas_call(
        attn_fwd_kernel,
        out_shape=(
            jax.ShapeDtypeStruct((n, width), jnp.bfloat16),
            jax.ShapeDtypeStruct(((n // BLK) * rows, 128), jnp.float32),
        ),
        in_specs=[smem_spec(), smem_spec(), vmem_spec(), vmem_spec(), vmem_spec()],
        out_specs=(vmem_spec(), vmem_spec()),
        compiler_params=pltpu.CompilerParams(vmem_limit_bytes=VMEM_LIMIT),
    )(cols, counts, q, k, v)


def attention_backward(q, k, v, o, do, lse, cols, counts):
    n, width = q.shape
    return pl.pallas_call(
        attn_bwd_kernel,
        out_shape=tuple(jax.ShapeDtypeStruct((n, width), jnp.bfloat16) for _ in range(3)),
        in_specs=[smem_spec(), smem_spec()] + [vmem_spec()] * 6,
        out_specs=(vmem_spec(), vmem_spec(), vmem_spec()),
        scratch_shapes=[pltpu.VMEM((n, width), jnp.float32), pltpu.VMEM((n, width), jnp.float32)],
        compiler_params=pltpu.CompilerParams(vmem_limit_bytes=VMEM_LIMIT),
    )(cols, counts, q, k, v, o, do, lse)


def regroup_columns(moved, seq_count, group_width):
    rows = moved.shape[0]
    return (
        moved.reshape(rows, seq_count, 3, group_width)
        .transpose(0, 2, 1, 3)
        .reshape(rows, 3 * seq_count * group_width)
    )


MESH = pl.DeviceIdType.MESH


def exchange_kernel(
    n,
    m,
    na_ref,
    xo_ref,
    g_ref,
    a_ref,
    o_ref,
    moved_ref,
    att_ref,
    x_ref,
    recv,
    gath,
    landed,
    att_landed,
    sems,
    a2a_sems,
):
    me = lax.axis_index("dp")
    here = lax.axis_index("seq")
    barrier = pltpu.get_barrier_semaphore()
    for k in range(1, n):
        pl.semaphore_signal(
            barrier, inc=1, device_id={"dp": lax.rem(me + k, n)}, device_id_type=MESH
        )
    for k in range(1, m):
        pl.semaphore_signal(
            barrier, inc=1, device_id={"seq": lax.rem(here + k, m)}, device_id_type=MESH
        )
    pl.semaphore_wait(barrier, n - 1 + m - 1)

    def start_all(src_of, dst, send, arrive, axis, at, size):
        started = []
        for k in range(1, size):
            peer = lax.rem(at + k, size)
            copy = pltpu.make_async_remote_copy(
                src_ref=src_of(peer),
                dst_ref=dst.at[at],
                send_sem=send.at[peer],
                recv_sem=arrive.at[at],
                device_id={axis: peer},
                device_id_type=MESH,
            )
            copy.start()
            started.append(copy)
        return started

    def finish_all(started, src_of, dst, send, arrive, axis, at, size):
        for k in range(1, size):
            source = lax.rem(at + size - k, size)
            pltpu.make_async_remote_copy(
                src_ref=src_of(source),
                dst_ref=dst.at[source],
                send_sem=send.at[source],
                recv_sem=arrive.at[source],
                device_id={axis: source},
                device_id_type=MESH,
            ).wait_recv()
        for copy in started:
            copy.wait_send()

    parts = g_ref.shape[2] // BLK
    group = BLK * m

    def part_copy(t, peer, sender, target):
        return pltpu.make_async_remote_copy(
            src_ref=g_ref.at[peer, :, pl.ds(t * BLK, BLK)],
            dst_ref=landed.at[:, pl.ds(pl.multiple_of(t * group + sender * BLK, BLK), BLK)],
            send_sem=a2a_sems.at[0, t, peer],
            recv_sem=a2a_sems.at[1, t, sender],
            device_id={"seq": target},
            device_id_type=MESH,
        )

    width = a_ref.shape[2]

    def att_copy(peer, sender, target):
        return pltpu.make_async_remote_copy(
            src_ref=a_ref.at[peer],
            dst_ref=att_landed.at[:, pl.ds(pl.multiple_of(sender * width, width), width)],
            send_sem=a2a_sems.at[0, parts, peer],
            recv_sem=a2a_sems.at[1, parts, sender],
            device_id={"seq": target},
            device_id_type=MESH,
        )

    a2a_started = []
    for k in range(1, m):
        peer = lax.rem(here + k, m)
        copy = att_copy(peer, here, peer)
        copy.start()
        a2a_started.append(copy)
    for k in range(1, m):
        peer = lax.rem(here + k, m)
        for t in range(parts):
            copy = part_copy(t, peer, here, peer)
            copy.start()
            a2a_started.append(copy)
    share = g_ref.shape[1]
    qkv = tn_dot(na_ref[0:share, :], g_ref[0])
    for c in range(1, m):
        qkv = qkv + tn_dot(na_ref[c * share : (c + 1) * share, :], g_ref[c])
    qkv_cols = g_ref.shape[2]
    x_ref[:, :, 0:qkv_cols] = qkv.reshape(n, x_ref.shape[1], qkv_cols)
    x_ref[:, :, qkv_cols:] = xo_ref[...]
    rs = (lambda peer: x_ref.at[peer], recv, sems.at[0], sems.at[1], "dp", me, n)
    finish_all(start_all(*rs), *rs)
    total = x_ref[me]
    for k in range(1, n):
        total = total + recv[lax.rem(me + k, n)]
    gath[me] = total.astype(gath.dtype)
    ag = (lambda peer: gath.at[me], gath, sems.at[2], sems.at[3], "dp", me, n)
    finish_all(start_all(*ag), *ag)
    o_ref[...] = gath[...]
    own = g_ref[here]
    for t in range(parts):
        landed[:, pl.ds(pl.multiple_of(t * group + here * BLK, BLK), BLK)] = own[
            :, t * BLK : (t + 1) * BLK
        ]
    att_landed[:, pl.ds(pl.multiple_of(here * width, width), width)] = a_ref[here]
    for k in range(1, m):
        source = lax.rem(here + m - k, m)
        att_copy(source, source, source).wait_recv()
        for t in range(parts):
            part_copy(t, source, source, source).wait_recv()
    for copy in a2a_started:
        copy.wait_send()
    moved_ref[...] = landed[...]
    att_ref[...] = att_landed[...]


def sum_and_exchange(normed_all, term_out, grads, attended_heads):
    n = lax.axis_size("dp")
    m = lax.axis_size("seq")
    rows = normed_all.shape[1]
    qkv_cols = grads.shape[1]
    extra = term_out.size // rows
    cols = qkv_cols + extra
    chunk_shape = (n, rows // n, cols)
    term_part = term_out.reshape(n, rows // n, extra)
    pieces = grads.reshape(m, grads.shape[0] // m, grads.shape[1])
    att_pieces = attended_heads.reshape(m, attended_heads.shape[0] // m, attended_heads.shape[1])
    parts = grads.shape[1] // BLK
    final = (pieces.shape[1], parts * m * BLK)
    att_final = (att_pieces.shape[1], m * att_pieces.shape[2])
    out, moved, attended = pl.pallas_call(
        functools.partial(exchange_kernel, n, m),
        out_shape=(
            jax.ShapeDtypeStruct(chunk_shape, jnp.bfloat16),
            jax.ShapeDtypeStruct(final, pieces.dtype),
            jax.ShapeDtypeStruct(att_final, att_pieces.dtype),
        ),
        in_specs=[vmem_spec(), vmem_spec(), vmem_spec(), vmem_spec()],
        out_specs=(vmem_spec(), vmem_spec(), vmem_spec()),
        scratch_shapes=[
            pltpu.VMEM(chunk_shape, jnp.float32),
            pltpu.VMEM(chunk_shape, jnp.float32),
            pltpu.VMEM(chunk_shape, jnp.bfloat16),
            pltpu.VMEM(final, pieces.dtype),
            pltpu.VMEM(att_final, att_pieces.dtype),
            pltpu.SemaphoreType.DMA((4, n)),
            pltpu.SemaphoreType.DMA((2, parts + 1, m)),
        ],
        compiler_params=pltpu.CompilerParams(
            collective_id=0, has_side_effects=True, vmem_limit_bytes=VMEM_LIMIT
        ),
    )(normed_all, term_part, pieces, att_pieces)
    return out.reshape(rows, cols), moved, attended


def body(feats, gain, w_qkv, w_out, block_cols, block_counts, cotan):
    model_width = feats.shape[1]
    seq_count = lax.axis_size("seq")
    group_width = model_width // seq_count
    seq_at = lax.axis_index("seq")
    scaled, inverse, normed = layer_norm(feats, gain)
    normed_all = lax.all_gather(normed, "seq", axis=0, tiled=True)
    cotan_all = lax.all_gather(cotan, "seq", axis=0, tiled=True)
    w_heads = jnp.concatenate(
        [
            lax.dynamic_slice_in_dim(w_qkv, j * model_width + seq_at * group_width, group_width, 1)
            for j in range(3)
        ],
        axis=1,
    )
    mixed_heads = jnp.dot(normed_all, w_heads, preferred_element_type=jnp.float32).astype(
        jnp.bfloat16
    )
    query_heads = mixed_heads[:, :group_width]
    key_heads = mixed_heads[:, group_width : 2 * group_width]
    value_heads = mixed_heads[:, 2 * group_width :]
    cols = block_cols[0].reshape(-1)
    counts = block_counts[0]
    attended_heads, lse = attention_forward(query_heads, key_heads, value_heads, cols, counts)
    w_out_rows = lax.dynamic_slice_in_dim(w_out, seq_at * group_width, group_width, 0)
    grad_heads = lax.dot_general(
        cotan_all, w_out_rows, (((1,), (1,)), ((), ())), preferred_element_type=jnp.float32
    ).astype(jnp.bfloat16)
    query_grad, key_grad, value_grad = attention_backward(
        query_heads, key_heads, value_heads, attended_heads, grad_heads, lse, cols, counts
    )
    grad_heads_mixed = jnp.concatenate([query_grad, key_grad, value_grad], axis=1)
    term_out = contract_rows(attended_heads, cotan_all)
    qkv_cols = grad_heads_mixed.shape[1]
    summed, moved_grads, attended = sum_and_exchange(
        normed_all, term_out, grad_heads_mixed, attended_heads
    )
    result = (
        feats.astype(jnp.float32) + jnp.dot(attended, w_out, preferred_element_type=jnp.float32)
    ).astype(jnp.bfloat16)
    grad_mixed = moved_grads
    grad_normed = lax.dot_general(
        grad_mixed, w_qkv, (((1,), (1,)), ((), ())), preferred_element_type=jnp.float32
    )
    gained = grad_normed * gain[None, :]
    mean_one = jnp.mean(gained, axis=1, keepdims=True)
    mean_two = jnp.mean(gained * scaled, axis=1, keepdims=True)
    grad_feats = (
        cotan.astype(jnp.float32) + inverse * (gained - mean_one - scaled * mean_two)
    ).astype(jnp.bfloat16)
    term_qkv = summed[:, :qkv_cols]
    term_out = summed[:, qkv_cols:].reshape(term_out.shape)
    grad_qkv = regroup_columns(
        lax.all_to_all(term_qkv, "seq", split_axis=0, concat_axis=1, tiled=True),
        seq_count,
        group_width,
    )
    grad_out = term_out
    return (result, grad_feats, grad_qkv, grad_out)


def solution(mesh):
    in_specs = (
        P(("dp", "seq"), None),
        P(),
        P(),
        P(),
        P("dp", None, None),
        P("dp", None),
        P(("dp", "seq"), None),
    )
    out_specs = (P(("dp", "seq"), None), P(("dp", "seq"), None), P("seq", None), P("seq", None))
    return jax.shard_map(body, mesh=mesh, in_specs=in_specs, out_specs=out_specs, check_vma=False)
```

```python
import functools

import jax
import jax.numpy as jnp
from jax import lax
from jax.experimental import pallas as pl
from jax.experimental.pallas import tpu as pltpu
from jax.sharding import PartitionSpec as P

HD = 64
BLK = 128
MAXB = 8
SCALE = HD ** (-0.5)
NEG = -1e30

EPSILON = 1e-05


def layer_norm(feats, gain):
    values_f = feats.astype(jnp.float32)
    centred = values_f - jnp.mean(values_f, axis=1, keepdims=True)
    inverse = lax.rsqrt(jnp.mean(centred * centred, axis=1, keepdims=True) + EPSILON)
    scaled = centred * inverse
    return (scaled, inverse, (scaled * gain[None, :]).astype(jnp.bfloat16))


def contract_rows(left_cols, right_cols):
    return lax.dot_general(
        left_cols, right_cols, (((0,), (0,)), ((), ())), preferred_element_type=jnp.float32
    )


def head_masks(width):
    lane = lax.broadcasted_iota(jnp.int32, (1, width), 1)
    return [(lane >= h * HD) & (lane < (h + 1) * HD) for h in range(width // HD)]


def stack_heads(x, masks):
    return jnp.concatenate([jnp.where(m, x, jnp.zeros_like(x)) for m in masks], axis=0)


def unstack_heads(y, masks):
    out = y[0:BLK]
    for h in range(1, len(masks)):
        out = jnp.where(masks[h], y[h * BLK : (h + 1) * BLK], out)
    return out


def nt_dot(a, b):
    return lax.dot_general(a, b, (((1,), (1,)), ((), ())), preferred_element_type=jnp.float32)


def tn_dot(a, b):
    return lax.dot_general(a, b, (((0,), (0,)), ((), ())), preferred_element_type=jnp.float32)


SLOT_TIERS = (2, 4, MAXB)


def gather_blocks(ref, cols_ref, r, slots):
    return jnp.concatenate(
        [
            ref[pl.ds(pl.multiple_of(cols_ref[r * MAXB + s] * BLK, BLK), BLK), :]
            for s in range(slots)
        ],
        axis=0,
    )


def live_lanes(cnt, slots):
    return lax.broadcasted_iota(jnp.int32, (1, slots * BLK), 1) < cnt * BLK


FINE_TIERS = (1, 2, 3, 4, 6, MAXB)


def by_tier(cnt, body, tiers=SLOT_TIERS):
    low = 0
    for slots in tiers:
        pl.when((cnt > low) & (cnt <= slots))(functools.partial(body, slots))
        low = slots


def attn_fwd_kernel(cols_ref, counts_ref, q_ref, k_ref, v_ref, o_ref, lse_ref):
    width = q_ref.shape[1]
    nblk = q_ref.shape[0] // BLK
    masks = head_masks(width)
    rows = len(masks) * BLK

    def row_body(r, carry):
        row0 = pl.multiple_of(r * BLK, BLK)
        cnt = counts_ref[r]

        def tier(slots):
            live = live_lanes(cnt, slots)
            q2 = stack_heads(q_ref[pl.ds(row0, BLK), :], masks)
            kc = gather_blocks(k_ref, cols_ref, r, slots)
            sc = jnp.where(live, nt_dot(q2, kc) * SCALE, NEG)
            m = jnp.max(sc, axis=1, keepdims=True)
            e = jnp.where(live, jnp.exp(sc - m), 0.0)
            l = jnp.sum(e, axis=1, keepdims=True)
            p = (e * (1.0 / l)).astype(jnp.bfloat16)
            vc = gather_blocks(v_ref, cols_ref, r, slots)
            acc = jnp.dot(p, vc, preferred_element_type=jnp.float32)
            o_ref[pl.ds(row0, BLK), :] = unstack_heads(acc, masks).astype(o_ref.dtype)
            lse_ref[pl.ds(pl.multiple_of(r * rows, rows), rows), :] = jnp.broadcast_to(
                m + jnp.log(l), (rows, lse_ref.shape[1])
            )

        by_tier(cnt, tier)
        return carry

    lax.fori_loop(0, nblk, row_body, 0)


def attn_bwd_kernel(
    cols_ref, counts_ref, q_ref, k_ref, v_ref, o_ref, do_ref, lse_ref, dq_ref, dk_ref, dv_ref, dk_acc, dv_acc
):
    width = q_ref.shape[1]
    nblk = q_ref.shape[0] // BLK
    masks = head_masks(width)
    rows = len(masks) * BLK
    dk_acc[...] = jnp.zeros_like(dk_acc)
    dv_acc[...] = jnp.zeros_like(dv_acc)

    def row_body(r, carry):
        row0 = pl.multiple_of(r * BLK, BLK)
        cnt = counts_ref[r]

        def tier(slots):
            live = live_lanes(cnt, slots)
            q2 = stack_heads(q_ref[pl.ds(row0, BLK), :], masks)
            do_blk = do_ref[pl.ds(row0, BLK), :]
            do2 = stack_heads(do_blk, masks)
            prod = o_ref[pl.ds(row0, BLK), :].astype(jnp.float32) * do_blk.astype(jnp.float32)
            delta = jnp.concatenate(
                [jnp.sum(jnp.where(m, prod, 0.0), axis=1, keepdims=True) for m in masks], axis=0
            )
            lse = lse_ref[pl.ds(pl.multiple_of(r * rows, rows), rows), :][:, 0:1]
            kc = gather_blocks(k_ref, cols_ref, r, slots)
            vc = gather_blocks(v_ref, cols_ref, r, slots)
            sc = nt_dot(q2, kc) * SCALE
            p = jnp.where(live, jnp.exp(sc - lse), 0.0).astype(jnp.bfloat16)
            dp = nt_dot(do2, vc)
            ds = (p.astype(jnp.float32) * (dp - delta) * SCALE).astype(jnp.bfloat16)
            dq = jnp.dot(ds, kc, preferred_element_type=jnp.float32)
            dq_ref[pl.ds(row0, BLK), :] = unstack_heads(dq, masks).astype(dq_ref.dtype)
            dkc = tn_dot(ds, q2)
            dvc = tn_dot(p, do2)
            for s in range(slots):

                @pl.when(s < cnt)
                def _():
                    col0 = pl.multiple_of(cols_ref[r * MAXB + s] * BLK, BLK)
                    dk_acc[pl.ds(col0, BLK), :] += dkc[s * BLK : (s + 1) * BLK]
                    dv_acc[pl.ds(col0, BLK), :] += dvc[s * BLK : (s + 1) * BLK]

        by_tier(cnt, tier, FINE_TIERS)
        return carry

    lax.fori_loop(0, nblk, row_body, 0)
    dk_ref[...] = dk_acc[...].astype(dk_ref.dtype)
    dv_ref[...] = dv_acc[...].astype(dv_ref.dtype)


def smem_spec():
    return pl.BlockSpec(memory_space=pltpu.SMEM)


def vmem_spec():
    return pl.BlockSpec(memory_space=pltpu.VMEM)


VMEM_LIMIT = 48 * 1024 * 1024


def attention_forward(q, k, v, cols, counts):
    n, width = q.shape
    rows = (width // HD) * BLK
    return pl.pallas_call(
        attn_fwd_kernel,
        out_shape=(
            jax.ShapeDtypeStruct((n, width), jnp.bfloat16),
            jax.ShapeDtypeStruct(((n // BLK) * rows, 128), jnp.float32),
        ),
        in_specs=[smem_spec(), smem_spec(), vmem_spec(), vmem_spec(), vmem_spec()],
        out_specs=(vmem_spec(), vmem_spec()),
        compiler_params=pltpu.CompilerParams(vmem_limit_bytes=VMEM_LIMIT),
    )(cols, counts, q, k, v)


def attention_backward(q, k, v, o, do, lse, cols, counts):
    n, width = q.shape
    return pl.pallas_call(
        attn_bwd_kernel,
        out_shape=tuple(jax.ShapeDtypeStruct((n, width), jnp.bfloat16) for _ in range(3)),
        in_specs=[smem_spec(), smem_spec()] + [vmem_spec()] * 6,
        out_specs=(vmem_spec(), vmem_spec(), vmem_spec()),
        scratch_shapes=[pltpu.VMEM((n, width), jnp.float32), pltpu.VMEM((n, width), jnp.float32)],
        compiler_params=pltpu.CompilerParams(vmem_limit_bytes=VMEM_LIMIT),
    )(cols, counts, q, k, v, o, do, lse)


def regroup_columns(moved, seq_count, group_width):
    rows = moved.shape[0]
    return (
        moved.reshape(rows, seq_count, 3, group_width)
        .transpose(0, 2, 1, 3)
        .reshape(rows, 3 * seq_count * group_width)
    )


MESH = pl.DeviceIdType.MESH


def exchange_kernel(
    n,
    m,
    na_ref,
    co_ref,
    g_ref,
    a_ref,
    o_ref,
    oo_ref,
    moved_ref,
    att_ref,
    x_ref,
    recv,
    gath,
    xo_ref,
    recv_o,
    gath_o,
    landed,
    att_landed,
    sems,
    a2a_sems,
):
    me = lax.axis_index("dp")
    here = lax.axis_index("seq")
    barrier = pltpu.get_barrier_semaphore()
    for k in range(1, n):
        pl.semaphore_signal(
            barrier, inc=1, device_id={"dp": lax.rem(me + k, n)}, device_id_type=MESH
        )
    for k in range(1, m):
        pl.semaphore_signal(
            barrier, inc=1, device_id={"seq": lax.rem(here + k, m)}, device_id_type=MESH
        )
    pl.semaphore_wait(barrier, n - 1 + m - 1)

    def start_all(src_of, dst, send, arrive, axis, at, size):
        started = []
        for k in range(1, size):
            peer = lax.rem(at + k, size)
            copy = pltpu.make_async_remote_copy(
                src_ref=src_of(peer),
                dst_ref=dst.at[at],
                send_sem=send.at[peer],
                recv_sem=arrive.at[at],
                device_id={axis: peer},
                device_id_type=MESH,
            )
            copy.start()
            started.append(copy)
        return started

    def finish_all(started, src_of, dst, send, arrive, axis, at, size):
        for k in range(1, size):
            source = lax.rem(at + size - k, size)
            pltpu.make_async_remote_copy(
                src_ref=src_of(source),
                dst_ref=dst.at[source],
                send_sem=send.at[source],
                recv_sem=arrive.at[source],
                device_id={axis: source},
                device_id_type=MESH,
            ).wait_recv()
        for copy in started:
            copy.wait_send()

    parts = g_ref.shape[2] // BLK
    group = BLK * m

    def part_copy(t, peer, sender, target):
        return pltpu.make_async_remote_copy(
            src_ref=g_ref.at[peer, :, pl.ds(t * BLK, BLK)],
            dst_ref=landed.at[:, pl.ds(pl.multiple_of(t * group + sender * BLK, BLK), BLK)],
            send_sem=a2a_sems.at[0, t, peer],
            recv_sem=a2a_sems.at[1, t, sender],
            device_id={"seq": target},
            device_id_type=MESH,
        )

    width = a_ref.shape[2]

    def att_copy(peer, sender, target):
        return pltpu.make_async_remote_copy(
            src_ref=a_ref.at[peer],
            dst_ref=att_landed.at[:, pl.ds(pl.multiple_of(sender * width, width), width)],
            send_sem=a2a_sems.at[0, parts, peer],
            recv_sem=a2a_sems.at[1, parts, sender],
            device_id={"seq": target},
            device_id_type=MESH,
        )

    a2a_started = []
    for k in range(1, m):
        peer = lax.rem(here + k, m)
        copy = att_copy(peer, here, peer)
        copy.start()
        a2a_started.append(copy)
    for k in range(1, m):
        peer = lax.rem(here + k, m)
        for t in range(parts):
            copy = part_copy(t, peer, here, peer)
            copy.start()
            a2a_started.append(copy)
    share = g_ref.shape[1]
    qkv = tn_dot(na_ref[0:share, :], g_ref[0])
    for c in range(1, m):
        qkv = qkv + tn_dot(na_ref[c * share : (c + 1) * share, :], g_ref[c])
    x_ref[...] = qkv.reshape(x_ref.shape)
    cshare = a_ref.shape[1]
    term_out = tn_dot(a_ref[0], co_ref[0:cshare, :])
    for c in range(1, m):
        term_out = term_out + tn_dot(a_ref[c], co_ref[c * cshare : (c + 1) * cshare, :])
    xo_ref[...] = term_out.reshape(xo_ref.shape)
    rs = (lambda peer: x_ref.at[peer], recv, sems.at[0], sems.at[1], "dp", me, n)
    rs_o = (lambda peer: xo_ref.at[peer], recv_o, sems.at[4], sems.at[5], "dp", me, n)
    rs_started = start_all(*rs)
    rs_o_started = start_all(*rs_o)
    finish_all(rs_started, *rs)
    finish_all(rs_o_started, *rs_o)
    total = x_ref[me]
    total_o = xo_ref[me]
    for k in range(1, n):
        total = total + recv[lax.rem(me + k, n)]
        total_o = total_o + recv_o[lax.rem(me + k, n)]
    gath[me] = total.astype(gath.dtype)
    gath_o[me] = total_o.astype(gath_o.dtype)
    ag = (lambda peer: gath.at[me], gath, sems.at[2], sems.at[3], "dp", me, n)
    ag_o = (lambda peer: gath_o.at[me], gath_o, sems.at[6], sems.at[7], "dp", me, n)
    ag_started = start_all(*ag)
    ag_o_started = start_all(*ag_o)
    finish_all(ag_started, *ag)
    finish_all(ag_o_started, *ag_o)
    o_ref[...] = gath[...]
    oo_ref[...] = gath_o[...]
    own = g_ref[here]
    for t in range(parts):
        landed[:, pl.ds(pl.multiple_of(t * group + here * BLK, BLK), BLK)] = own[
            :, t * BLK : (t + 1) * BLK
        ]
    att_landed[:, pl.ds(pl.multiple_of(here * width, width), width)] = a_ref[here]
    for k in range(1, m):
        source = lax.rem(here + m - k, m)
        att_copy(source, source, source).wait_recv()
        for t in range(parts):
            part_copy(t, source, source, source).wait_recv()
    for copy in a2a_started:
        copy.wait_send()
    moved_ref[...] = landed[...]
    att_ref[...] = att_landed[...]


def sum_and_exchange(normed_all, cotan_all, grads, attended_heads):
    n = lax.axis_size("dp")
    m = lax.axis_size("seq")
    rows = normed_all.shape[1]
    qkv_cols = grads.shape[1]
    out_rows, out_cols = attended_heads.shape[1], cotan_all.shape[1]
    chunk_shape = (n, rows // n, qkv_cols)
    out_chunks = (n, out_rows // n, out_cols)
    pieces = grads.reshape(m, grads.shape[0] // m, grads.shape[1])
    att_pieces = attended_heads.reshape(m, attended_heads.shape[0] // m, attended_heads.shape[1])
    parts = grads.shape[1] // BLK
    final = (pieces.shape[1], parts * m * BLK)
    att_final = (att_pieces.shape[1], m * att_pieces.shape[2])
    out, out_o, moved, attended = pl.pallas_call(
        functools.partial(exchange_kernel, n, m),
        out_shape=(
            jax.ShapeDtypeStruct(chunk_shape, jnp.bfloat16),
            jax.ShapeDtypeStruct(out_chunks, jnp.bfloat16),
            jax.ShapeDtypeStruct(final, pieces.dtype),
            jax.ShapeDtypeStruct(att_final, att_pieces.dtype),
        ),
        in_specs=[vmem_spec(), vmem_spec(), vmem_spec(), vmem_spec()],
        out_specs=(vmem_spec(), vmem_spec(), vmem_spec(), vmem_spec()),
        scratch_shapes=[
            pltpu.VMEM(chunk_shape, jnp.float32),
            pltpu.VMEM(chunk_shape, jnp.float32),
            pltpu.VMEM(chunk_shape, jnp.bfloat16),
            pltpu.VMEM(out_chunks, jnp.float32),
            pltpu.VMEM(out_chunks, jnp.float32),
            pltpu.VMEM(out_chunks, jnp.bfloat16),
            pltpu.VMEM(final, pieces.dtype),
            pltpu.VMEM(att_final, att_pieces.dtype),
            pltpu.SemaphoreType.DMA((8, n)),
            pltpu.SemaphoreType.DMA((2, parts + 1, m)),
        ],
        compiler_params=pltpu.CompilerParams(
            collective_id=0, has_side_effects=True, vmem_limit_bytes=VMEM_LIMIT
        ),
    )(normed_all, cotan_all, pieces, att_pieces)
    return out.reshape(rows, qkv_cols), out_o.reshape(out_rows, out_cols), moved, attended


def body(feats, gain, w_qkv, w_out, block_cols, block_counts, cotan):
    model_width = feats.shape[1]
    seq_count = lax.axis_size("seq")
    group_width = model_width // seq_count
    seq_at = lax.axis_index("seq")
    scaled, inverse, normed = layer_norm(feats, gain)
    normed_all = lax.all_gather(normed, "seq", axis=0, tiled=True)
    cotan_all = lax.all_gather(cotan, "seq", axis=0, tiled=True)
    w_heads = jnp.concatenate(
        [
            lax.dynamic_slice_in_dim(w_qkv, j * model_width + seq_at * group_width, group_width, 1)
            for j in range(3)
        ],
        axis=1,
    )
    mixed_heads = jnp.dot(normed_all, w_heads, preferred_element_type=jnp.float32).astype(
        jnp.bfloat16
    )
    query_heads = mixed_heads[:, :group_width]
    key_heads = mixed_heads[:, group_width : 2 * group_width]
    value_heads = mixed_heads[:, 2 * group_width :]
    cols = block_cols[0].reshape(-1)
    counts = block_counts[0]
    attended_heads, lse = attention_forward(query_heads, key_heads, value_heads, cols, counts)
    w_out_rows = lax.dynamic_slice_in_dim(w_out, seq_at * group_width, group_width, 0)
    grad_heads = lax.dot_general(
        cotan_all, w_out_rows, (((1,), (1,)), ((), ())), preferred_element_type=jnp.float32
    ).astype(jnp.bfloat16)
    query_grad, key_grad, value_grad = attention_backward(
        query_heads, key_heads, value_heads, attended_heads, grad_heads, lse, cols, counts
    )
    grad_heads_mixed = jnp.concatenate([query_grad, key_grad, value_grad], axis=1)
    term_qkv, grad_out, moved_grads, attended = sum_and_exchange(
        normed_all, cotan_all, grad_heads_mixed, attended_heads
    )
    result = (
        feats.astype(jnp.float32) + jnp.dot(attended, w_out, preferred_element_type=jnp.float32)
    ).astype(jnp.bfloat16)
    grad_mixed = moved_grads
    grad_normed = lax.dot_general(
        grad_mixed, w_qkv, (((1,), (1,)), ((), ())), preferred_element_type=jnp.float32
    )
    gained = grad_normed * gain[None, :]
    mean_one = jnp.mean(gained, axis=1, keepdims=True)
    mean_two = jnp.mean(gained * scaled, axis=1, keepdims=True)
    grad_feats = (
        cotan.astype(jnp.float32) + inverse * (gained - mean_one - scaled * mean_two)
    ).astype(jnp.bfloat16)
    grad_qkv = regroup_columns(
        lax.all_to_all(term_qkv, "seq", split_axis=0, concat_axis=1, tiled=True),
        seq_count,
        group_width,
    )
    return (result, grad_feats, grad_qkv, grad_out)


def solution(mesh):
    in_specs = (
        P(("dp", "seq"), None),
        P(),
        P(),
        P(),
        P("dp", None, None),
        P("dp", None),
        P(("dp", "seq"), None),
    )
    out_specs = (P(("dp", "seq"), None), P(("dp", "seq"), None), P("seq", None), P("seq", None))
    return jax.shard_map(body, mesh=mesh, in_specs=in_specs, out_specs=out_specs, check_vma=False)
```

```python
import functools

import jax
import jax.numpy as jnp
from jax import lax
from jax.experimental import pallas as pl
from jax.experimental.pallas import tpu as pltpu
from jax.sharding import PartitionSpec as P

HD = 64
BLK = 128
MAXB = 8
SCALE = HD ** (-0.5)
NEG = -1e30

EPSILON = 1e-05


def layer_norm(feats, gain):
    values_f = feats.astype(jnp.float32)
    centred = values_f - jnp.mean(values_f, axis=1, keepdims=True)
    inverse = lax.rsqrt(jnp.mean(centred * centred, axis=1, keepdims=True) + EPSILON)
    scaled = centred * inverse
    return (scaled, inverse, (scaled * gain[None, :]).astype(jnp.bfloat16))


def contract_rows(left_cols, right_cols):
    return lax.dot_general(
        left_cols, right_cols, (((0,), (0,)), ((), ())), preferred_element_type=jnp.float32
    )


def head_masks(width):
    lane = lax.broadcasted_iota(jnp.int32, (1, width), 1)
    return [(lane >= h * HD) & (lane < (h + 1) * HD) for h in range(width // HD)]


def stack_heads(x, masks):
    return jnp.concatenate([jnp.where(m, x, jnp.zeros_like(x)) for m in masks], axis=0)


def unstack_heads(y, masks):
    out = y[0:BLK]
    for h in range(1, len(masks)):
        out = jnp.where(masks[h], y[h * BLK : (h + 1) * BLK], out)
    return out


def nt_dot(a, b):
    return lax.dot_general(a, b, (((1,), (1,)), ((), ())), preferred_element_type=jnp.float32)


def tn_dot(a, b):
    return lax.dot_general(a, b, (((0,), (0,)), ((), ())), preferred_element_type=jnp.float32)


SLOT_TIERS = (2, 4, MAXB)


def gather_blocks(ref, cols_ref, r, slots):
    return jnp.concatenate(
        [
            ref[pl.ds(pl.multiple_of(cols_ref[r * MAXB + s] * BLK, BLK), BLK), :]
            for s in range(slots)
        ],
        axis=0,
    )


def live_lanes(cnt, slots):
    return lax.broadcasted_iota(jnp.int32, (1, slots * BLK), 1) < cnt * BLK


FINE_TIERS = tuple(range(1, MAXB + 1))


def by_tier(cnt, body, tiers=SLOT_TIERS):
    low = 0
    for slots in tiers:
        pl.when((cnt > low) & (cnt <= slots))(functools.partial(body, slots))
        low = slots


def attn_fwd_kernel(cols_ref, counts_ref, q_ref, k_ref, v_ref, o_ref, lse_ref):
    width = q_ref.shape[1]
    nblk = q_ref.shape[0] // BLK
    masks = head_masks(width)
    rows = len(masks) * BLK

    def row_body(r, carry):
        row0 = pl.multiple_of(r * BLK, BLK)
        cnt = counts_ref[r]

        def tier(slots):
            live = live_lanes(cnt, slots)
            q2 = stack_heads(q_ref[pl.ds(row0, BLK), :], masks)
            kc = gather_blocks(k_ref, cols_ref, r, slots)
            sc = jnp.where(live, nt_dot(q2, kc) * SCALE, NEG)
            m = jnp.max(sc, axis=1, keepdims=True)
            e = jnp.where(live, jnp.exp(sc - m), 0.0)
            l = jnp.sum(e, axis=1, keepdims=True)
            p = (e * (1.0 / l)).astype(jnp.bfloat16)
            vc = gather_blocks(v_ref, cols_ref, r, slots)
            acc = jnp.dot(p, vc, preferred_element_type=jnp.float32)
            o_ref[pl.ds(row0, BLK), :] = unstack_heads(acc, masks).astype(o_ref.dtype)
            lse_ref[pl.ds(pl.multiple_of(r * rows, rows), rows), :] = jnp.broadcast_to(
                m + jnp.log(l), (rows, lse_ref.shape[1])
            )

        by_tier(cnt, tier)
        return carry

    lax.fori_loop(0, nblk, row_body, 0)


def attn_bwd_kernel(
    cols_ref, counts_ref, q_ref, k_ref, v_ref, o_ref, do_ref, lse_ref, dq_ref, dk_ref, dv_ref, dk_acc, dv_acc
):
    width = q_ref.shape[1]
    nblk = q_ref.shape[0] // BLK
    masks = head_masks(width)
    rows = len(masks) * BLK
    dk_acc[...] = jnp.zeros_like(dk_acc)
    dv_acc[...] = jnp.zeros_like(dv_acc)

    def row_body(r, carry):
        row0 = pl.multiple_of(r * BLK, BLK)
        cnt = counts_ref[r]

        def tier(slots):
            live = live_lanes(cnt, slots)
            q2 = stack_heads(q_ref[pl.ds(row0, BLK), :], masks)
            do_blk = do_ref[pl.ds(row0, BLK), :]
            do2 = stack_heads(do_blk, masks)
            prod = o_ref[pl.ds(row0, BLK), :].astype(jnp.float32) * do_blk.astype(jnp.float32)
            delta = jnp.concatenate(
                [jnp.sum(jnp.where(m, prod, 0.0), axis=1, keepdims=True) for m in masks], axis=0
            )
            lse = lse_ref[pl.ds(pl.multiple_of(r * rows, rows), rows), :][:, 0:1]
            kc = gather_blocks(k_ref, cols_ref, r, slots)
            vc = gather_blocks(v_ref, cols_ref, r, slots)
            sc = nt_dot(q2, kc) * SCALE
            p = jnp.where(live, jnp.exp(sc - lse), 0.0).astype(jnp.bfloat16)
            dp = nt_dot(do2, vc)
            ds = (p.astype(jnp.float32) * (dp - delta) * SCALE).astype(jnp.bfloat16)
            dq = jnp.dot(ds, kc, preferred_element_type=jnp.float32)
            dq_ref[pl.ds(row0, BLK), :] = unstack_heads(dq, masks).astype(dq_ref.dtype)
            dkc = tn_dot(ds, q2)
            dvc = tn_dot(p, do2)
            for s in range(slots):

                @pl.when(s < cnt)
                def _():
                    col0 = pl.multiple_of(cols_ref[r * MAXB + s] * BLK, BLK)
                    dk_acc[pl.ds(col0, BLK), :] += dkc[s * BLK : (s + 1) * BLK]
                    dv_acc[pl.ds(col0, BLK), :] += dvc[s * BLK : (s + 1) * BLK]

        by_tier(cnt, tier, FINE_TIERS)
        return carry

    lax.fori_loop(0, nblk, row_body, 0)
    dk_ref[...] = dk_acc[...].astype(dk_ref.dtype)
    dv_ref[...] = dv_acc[...].astype(dv_ref.dtype)


def smem_spec():
    return pl.BlockSpec(memory_space=pltpu.SMEM)


def vmem_spec():
    return pl.BlockSpec(memory_space=pltpu.VMEM)


VMEM_LIMIT = 48 * 1024 * 1024


def attention_forward(q, k, v, cols, counts):
    n, width = q.shape
    rows = (width // HD) * BLK
    return pl.pallas_call(
        attn_fwd_kernel,
        out_shape=(
            jax.ShapeDtypeStruct((n, width), jnp.bfloat16),
            jax.ShapeDtypeStruct(((n // BLK) * rows, 8), jnp.float32),
        ),
        in_specs=[smem_spec(), smem_spec(), vmem_spec(), vmem_spec(), vmem_spec()],
        out_specs=(vmem_spec(), vmem_spec()),
        compiler_params=pltpu.CompilerParams(vmem_limit_bytes=VMEM_LIMIT),
    )(cols, counts, q, k, v)


def attention_backward(q, k, v, o, do, lse, cols, counts):
    n, width = q.shape
    return pl.pallas_call(
        attn_bwd_kernel,
        out_shape=tuple(jax.ShapeDtypeStruct((n, width), jnp.bfloat16) for _ in range(3)),
        in_specs=[smem_spec(), smem_spec()] + [vmem_spec()] * 6,
        out_specs=(vmem_spec(), vmem_spec(), vmem_spec()),
        scratch_shapes=[pltpu.VMEM((n, width), jnp.float32), pltpu.VMEM((n, width), jnp.float32)],
        compiler_params=pltpu.CompilerParams(vmem_limit_bytes=VMEM_LIMIT),
    )(cols, counts, q, k, v, o, do, lse)


def regroup_columns(moved, seq_count, group_width):
    rows = moved.shape[0]
    return (
        moved.reshape(rows, seq_count, 3, group_width)
        .transpose(0, 2, 1, 3)
        .reshape(rows, 3 * seq_count * group_width)
    )


MESH = pl.DeviceIdType.MESH


def exchange_kernel(
    n,
    m,
    na_ref,
    co_ref,
    g_ref,
    a_ref,
    o_ref,
    oo_ref,
    moved_ref,
    att_ref,
    x_ref,
    recv,
    gath,
    xo_ref,
    recv_o,
    gath_o,
    landed,
    att_landed,
    sems,
    a2a_sems,
):
    me = lax.axis_index("dp")
    here = lax.axis_index("seq")
    barrier = pltpu.get_barrier_semaphore()
    for k in range(1, n):
        pl.semaphore_signal(
            barrier, inc=1, device_id={"dp": lax.rem(me + k, n)}, device_id_type=MESH
        )
    for k in range(1, m):
        pl.semaphore_signal(
            barrier, inc=1, device_id={"seq": lax.rem(here + k, m)}, device_id_type=MESH
        )
    pl.semaphore_wait(barrier, n - 1 + m - 1)

    def start_all(src_of, dst, send, arrive, axis, at, size):
        started = []
        for k in range(1, size):
            peer = lax.rem(at + k, size)
            copy = pltpu.make_async_remote_copy(
                src_ref=src_of(peer),
                dst_ref=dst.at[at],
                send_sem=send.at[peer],
                recv_sem=arrive.at[at],
                device_id={axis: peer},
                device_id_type=MESH,
            )
            copy.start()
            started.append(copy)
        return started

    def finish_all(started, src_of, dst, send, arrive, axis, at, size):
        for k in range(1, size):
            source = lax.rem(at + size - k, size)
            pltpu.make_async_remote_copy(
                src_ref=src_of(source),
                dst_ref=dst.at[source],
                send_sem=send.at[source],
                recv_sem=arrive.at[source],
                device_id={axis: source},
                device_id_type=MESH,
            ).wait_recv()
        for copy in started:
            copy.wait_send()

    parts = g_ref.shape[2] // BLK
    group = BLK * m

    def part_copy(t, peer, sender, target):
        return pltpu.make_async_remote_copy(
            src_ref=g_ref.at[peer, :, pl.ds(t * BLK, BLK)],
            dst_ref=landed.at[:, pl.ds(pl.multiple_of(t * group + sender * BLK, BLK), BLK)],
            send_sem=a2a_sems.at[0, t, peer],
            recv_sem=a2a_sems.at[1, t, sender],
            device_id={"seq": target},
            device_id_type=MESH,
        )

    width = a_ref.shape[2]

    def att_copy(peer, sender, target):
        return pltpu.make_async_remote_copy(
            src_ref=a_ref.at[peer],
            dst_ref=att_landed.at[:, pl.ds(pl.multiple_of(sender * width, width), width)],
            send_sem=a2a_sems.at[0, parts, peer],
            recv_sem=a2a_sems.at[1, parts, sender],
            device_id={"seq": target},
            device_id_type=MESH,
        )

    a2a_started = []
    for k in range(1, m):
        peer = lax.rem(here + k, m)
        copy = att_copy(peer, here, peer)
        copy.start()
        a2a_started.append(copy)
    for k in range(1, m):
        peer = lax.rem(here + k, m)
        for t in range(parts):
            copy = part_copy(t, peer, here, peer)
            copy.start()
            a2a_started.append(copy)
    share = g_ref.shape[1]
    qkv = tn_dot(na_ref[0:share, :], g_ref[0])
    for c in range(1, m):
        qkv = qkv + tn_dot(na_ref[c * share : (c + 1) * share, :], g_ref[c])
    x_ref[...] = qkv.reshape(x_ref.shape)
    cshare = a_ref.shape[1]
    term_out = tn_dot(a_ref[0], co_ref[0:cshare, :])
    for c in range(1, m):
        term_out = term_out + tn_dot(a_ref[c], co_ref[c * cshare : (c + 1) * cshare, :])
    xo_ref[...] = term_out.reshape(xo_ref.shape)
    rs = (lambda peer: x_ref.at[peer], recv, sems.at[0], sems.at[1], "dp", me, n)
    rs_o = (lambda peer: xo_ref.at[peer], recv_o, sems.at[4], sems.at[5], "dp", me, n)
    rs_started = start_all(*rs)
    rs_o_started = start_all(*rs_o)
    finish_all(rs_started, *rs)
    finish_all(rs_o_started, *rs_o)
    total = x_ref[me]
    total_o = xo_ref[me]
    for k in range(1, n):
        total = total + recv[lax.rem(me + k, n)]
        total_o = total_o + recv_o[lax.rem(me + k, n)]
    gath[me] = total.astype(gath.dtype)
    gath_o[me] = total_o.astype(gath_o.dtype)
    ag = (lambda peer: gath.at[me], gath, sems.at[2], sems.at[3], "dp", me, n)
    ag_o = (lambda peer: gath_o.at[me], gath_o, sems.at[6], sems.at[7], "dp", me, n)
    ag_started = start_all(*ag)
    ag_o_started = start_all(*ag_o)
    finish_all(ag_started, *ag)
    finish_all(ag_o_started, *ag_o)
    o_ref[...] = gath[...]
    oo_ref[...] = gath_o[...]
    own = g_ref[here]
    for t in range(parts):
        landed[:, pl.ds(pl.multiple_of(t * group + here * BLK, BLK), BLK)] = own[
            :, t * BLK : (t + 1) * BLK
        ]
    att_landed[:, pl.ds(pl.multiple_of(here * width, width), width)] = a_ref[here]
    for k in range(1, m):
        source = lax.rem(here + m - k, m)
        att_copy(source, source, source).wait_recv()
        for t in range(parts):
            part_copy(t, source, source, source).wait_recv()
    for copy in a2a_started:
        copy.wait_send()
    moved_ref[...] = landed[...]
    att_ref[...] = att_landed[...]


def sum_and_exchange(normed_all, cotan_all, grads, attended_heads):
    n = lax.axis_size("dp")
    m = lax.axis_size("seq")
    rows = normed_all.shape[1]
    qkv_cols = grads.shape[1]
    out_rows, out_cols = attended_heads.shape[1], cotan_all.shape[1]
    chunk_shape = (n, rows // n, qkv_cols)
    out_chunks = (n, out_rows // n, out_cols)
    pieces = grads.reshape(m, grads.shape[0] // m, grads.shape[1])
    att_pieces = attended_heads.reshape(m, attended_heads.shape[0] // m, attended_heads.shape[1])
    parts = grads.shape[1] // BLK
    final = (pieces.shape[1], parts * m * BLK)
    att_final = (att_pieces.shape[1], m * att_pieces.shape[2])
    out, out_o, moved, attended = pl.pallas_call(
        functools.partial(exchange_kernel, n, m),
        out_shape=(
            jax.ShapeDtypeStruct(chunk_shape, jnp.bfloat16),
            jax.ShapeDtypeStruct(out_chunks, jnp.bfloat16),
            jax.ShapeDtypeStruct(final, pieces.dtype),
            jax.ShapeDtypeStruct(att_final, att_pieces.dtype),
        ),
        in_specs=[vmem_spec(), vmem_spec(), vmem_spec(), vmem_spec()],
        out_specs=(vmem_spec(), vmem_spec(), vmem_spec(), vmem_spec()),
        scratch_shapes=[
            pltpu.VMEM(chunk_shape, jnp.float32),
            pltpu.VMEM(chunk_shape, jnp.float32),
            pltpu.VMEM(chunk_shape, jnp.bfloat16),
            pltpu.VMEM(out_chunks, jnp.float32),
            pltpu.VMEM(out_chunks, jnp.float32),
            pltpu.VMEM(out_chunks, jnp.bfloat16),
            pltpu.VMEM(final, pieces.dtype),
            pltpu.VMEM(att_final, att_pieces.dtype),
            pltpu.SemaphoreType.DMA((8, n)),
            pltpu.SemaphoreType.DMA((2, parts + 1, m)),
        ],
        compiler_params=pltpu.CompilerParams(
            collective_id=0, has_side_effects=True, vmem_limit_bytes=VMEM_LIMIT
        ),
    )(normed_all, cotan_all, pieces, att_pieces)
    return out.reshape(rows, qkv_cols), out_o.reshape(out_rows, out_cols), moved, attended


def body(feats, gain, w_qkv, w_out, block_cols, block_counts, cotan):
    model_width = feats.shape[1]
    seq_count = lax.axis_size("seq")
    group_width = model_width // seq_count
    seq_at = lax.axis_index("seq")
    scaled, inverse, normed = layer_norm(feats, gain)
    normed_all = lax.all_gather(normed, "seq", axis=0, tiled=True)
    cotan_all = lax.all_gather(cotan, "seq", axis=0, tiled=True)
    w_heads = jnp.concatenate(
        [
            lax.dynamic_slice_in_dim(w_qkv, j * model_width + seq_at * group_width, group_width, 1)
            for j in range(3)
        ],
        axis=1,
    )
    mixed_heads = jnp.dot(normed_all, w_heads, preferred_element_type=jnp.float32).astype(
        jnp.bfloat16
    )
    query_heads = mixed_heads[:, :group_width]
    key_heads = mixed_heads[:, group_width : 2 * group_width]
    value_heads = mixed_heads[:, 2 * group_width :]
    cols = block_cols[0].reshape(-1)
    counts = block_counts[0]
    attended_heads, lse = attention_forward(query_heads, key_heads, value_heads, cols, counts)
    w_out_rows = lax.dynamic_slice_in_dim(w_out, seq_at * group_width, group_width, 0)
    grad_heads = lax.dot_general(
        cotan_all, w_out_rows, (((1,), (1,)), ((), ())), preferred_element_type=jnp.float32
    ).astype(jnp.bfloat16)
    query_grad, key_grad, value_grad = attention_backward(
        query_heads, key_heads, value_heads, attended_heads, grad_heads, lse, cols, counts
    )
    grad_heads_mixed = jnp.concatenate([query_grad, key_grad, value_grad], axis=1)
    term_qkv, grad_out, moved_grads, attended = sum_and_exchange(
        normed_all, cotan_all, grad_heads_mixed, attended_heads
    )
    result = (
        feats.astype(jnp.float32) + jnp.dot(attended, w_out, preferred_element_type=jnp.float32)
    ).astype(jnp.bfloat16)
    grad_mixed = moved_grads
    grad_normed = lax.dot_general(
        grad_mixed, w_qkv, (((1,), (1,)), ((), ())), preferred_element_type=jnp.float32
    )
    gained = grad_normed * gain[None, :]
    mean_one = jnp.mean(gained, axis=1, keepdims=True)
    mean_two = jnp.mean(gained * scaled, axis=1, keepdims=True)
    grad_feats = (
        cotan.astype(jnp.float32) + inverse * (gained - mean_one - scaled * mean_two)
    ).astype(jnp.bfloat16)
    grad_qkv = regroup_columns(
        lax.all_to_all(term_qkv, "seq", split_axis=0, concat_axis=1, tiled=True),
        seq_count,
        group_width,
    )
    return (result, grad_feats, grad_qkv, grad_out)


def solution(mesh):
    in_specs = (
        P(("dp", "seq"), None),
        P(),
        P(),
        P(),
        P("dp", None, None),
        P("dp", None),
        P(("dp", "seq"), None),
    )
    out_specs = (P(("dp", "seq"), None), P(("dp", "seq"), None), P("seq", None), P("seq", None))
    return jax.shard_map(body, mesh=mesh, in_specs=in_specs, out_specs=out_specs, check_vma=False)
```

```python
import functools

import jax
import jax.numpy as jnp
from jax import lax
from jax.experimental import pallas as pl
from jax.experimental.pallas import tpu as pltpu
from jax.sharding import PartitionSpec as P

HD = 64
BLK = 128
MAXB = 8
SCALE = HD ** (-0.5)
NEG = -1e30

EPSILON = 1e-05


def layer_norm(feats, gain):
    values_f = feats.astype(jnp.float32)
    centred = values_f - jnp.mean(values_f, axis=1, keepdims=True)
    inverse = lax.rsqrt(jnp.mean(centred * centred, axis=1, keepdims=True) + EPSILON)
    scaled = centred * inverse
    return (scaled, inverse, (scaled * gain[None, :]).astype(jnp.bfloat16))


def contract_rows(left_cols, right_cols):
    return lax.dot_general(
        left_cols, right_cols, (((0,), (0,)), ((), ())), preferred_element_type=jnp.float32
    )


def head_masks(width):
    lane = lax.broadcasted_iota(jnp.int32, (1, width), 1)
    return [(lane >= h * HD) & (lane < (h + 1) * HD) for h in range(width // HD)]


def stack_heads(x, masks):
    return jnp.concatenate([jnp.where(m, x, jnp.zeros_like(x)) for m in masks], axis=0)


def unstack_heads(y, masks):
    out = y[0:BLK]
    for h in range(1, len(masks)):
        out = jnp.where(masks[h], y[h * BLK : (h + 1) * BLK], out)
    return out


def nt_dot(a, b):
    return lax.dot_general(a, b, (((1,), (1,)), ((), ())), preferred_element_type=jnp.float32)


def tn_dot(a, b):
    return lax.dot_general(a, b, (((0,), (0,)), ((), ())), preferred_element_type=jnp.float32)


SLOT_TIERS = (2, 4, MAXB)


def gather_blocks(ref, cols_ref, r, slots):
    return jnp.concatenate(
        [
            ref[pl.ds(pl.multiple_of(cols_ref[r * MAXB + s] * BLK, BLK), BLK), :]
            for s in range(slots)
        ],
        axis=0,
    )


def live_lanes(cnt, slots):
    return lax.broadcasted_iota(jnp.int32, (1, slots * BLK), 1) < cnt * BLK


FINE_TIERS = (1, 2, 3, 4, 6, MAXB)


def by_tier(cnt, body, tiers=SLOT_TIERS):
    low = 0
    for slots in tiers:
        pl.when((cnt > low) & (cnt <= slots))(functools.partial(body, slots))
        low = slots


def attn_fwd_kernel(cols_ref, counts_ref, q_ref, k_ref, v_ref, o_ref, lse_ref):
    width = q_ref.shape[1]
    nblk = q_ref.shape[0] // BLK
    masks = head_masks(width)
    rows = len(masks) * BLK

    def row_body(r, carry):
        row0 = pl.multiple_of(r * BLK, BLK)
        cnt = counts_ref[r]

        def tier(slots):
            live = live_lanes(cnt, slots)
            q2 = stack_heads(q_ref[pl.ds(row0, BLK), :], masks)
            kc = gather_blocks(k_ref, cols_ref, r, slots)
            sc = jnp.where(live, nt_dot(q2, kc) * SCALE, NEG)
            m = jnp.max(sc, axis=1, keepdims=True)
            e = jnp.where(live, jnp.exp(sc - m), 0.0)
            l = jnp.sum(e, axis=1, keepdims=True)
            p = (e * (1.0 / l)).astype(jnp.bfloat16)
            vc = gather_blocks(v_ref, cols_ref, r, slots)
            acc = jnp.dot(p, vc, preferred_element_type=jnp.float32)
            o_ref[pl.ds(row0, BLK), :] = unstack_heads(acc, masks).astype(o_ref.dtype)
            lse_ref[pl.ds(pl.multiple_of(r * rows, rows), rows), :] = jnp.broadcast_to(
                m + jnp.log(l), (rows, lse_ref.shape[1])
            )

        by_tier(cnt, tier)
        return carry

    lax.fori_loop(0, nblk, row_body, 0)


def attn_bwd_kernel(
    cols_ref, counts_ref, q_ref, k_ref, v_ref, o_ref, do_ref, lse_ref, dq_ref, dk_ref, dv_ref, dk_acc, dv_acc
):
    width = q_ref.shape[1]
    nblk = q_ref.shape[0] // BLK
    masks = head_masks(width)
    rows = len(masks) * BLK
    dk_acc[...] = jnp.zeros_like(dk_acc)
    dv_acc[...] = jnp.zeros_like(dv_acc)

    def row_body(r, carry):
        row0 = pl.multiple_of(r * BLK, BLK)
        cnt = counts_ref[r]

        def tier(slots):
            live = live_lanes(cnt, slots)
            q2 = stack_heads(q_ref[pl.ds(row0, BLK), :], masks)
            do_blk = do_ref[pl.ds(row0, BLK), :]
            do2 = stack_heads(do_blk, masks)
            prod = o_ref[pl.ds(row0, BLK), :].astype(jnp.float32) * do_blk.astype(jnp.float32)
            delta = jnp.concatenate(
                [jnp.sum(jnp.where(m, prod, 0.0), axis=1, keepdims=True) for m in masks], axis=0
            )
            lse = lse_ref[pl.ds(pl.multiple_of(r * rows, rows), rows), :][:, 0:1]
            kc = gather_blocks(k_ref, cols_ref, r, slots)
            vc = gather_blocks(v_ref, cols_ref, r, slots)
            sc = nt_dot(q2, kc) * SCALE
            p = jnp.where(live, jnp.exp(sc - lse), 0.0).astype(jnp.bfloat16)
            dp = nt_dot(do2, vc)
            ds = (p.astype(jnp.float32) * (dp - delta) * SCALE).astype(jnp.bfloat16)
            dq = jnp.dot(ds, kc, preferred_element_type=jnp.float32)
            dq_ref[pl.ds(row0, BLK), :] = unstack_heads(dq, masks).astype(dq_ref.dtype)
            dkc = tn_dot(ds, q2)
            dvc = tn_dot(p, do2)
            for s in range(slots):

                @pl.when(s < cnt)
                def _():
                    col0 = pl.multiple_of(cols_ref[r * MAXB + s] * BLK, BLK)
                    dk_acc[pl.ds(col0, BLK), :] += dkc[s * BLK : (s + 1) * BLK]
                    dv_acc[pl.ds(col0, BLK), :] += dvc[s * BLK : (s + 1) * BLK]

        by_tier(cnt, tier, FINE_TIERS)
        return carry

    lax.fori_loop(0, nblk, row_body, 0)
    dk_ref[...] = dk_acc[...].astype(dk_ref.dtype)
    dv_ref[...] = dv_acc[...].astype(dv_ref.dtype)


def smem_spec():
    return pl.BlockSpec(memory_space=pltpu.SMEM)


def vmem_spec():
    return pl.BlockSpec(memory_space=pltpu.VMEM)


VMEM_LIMIT = 48 * 1024 * 1024


def attention_forward(q, k, v, cols, counts):
    n, width = q.shape
    rows = (width // HD) * BLK
    return pl.pallas_call(
        attn_fwd_kernel,
        out_shape=(
            jax.ShapeDtypeStruct((n, width), jnp.bfloat16),
            jax.ShapeDtypeStruct(((n // BLK) * rows, 128), jnp.float32),
        ),
        in_specs=[smem_spec(), smem_spec(), vmem_spec(), vmem_spec(), vmem_spec()],
        out_specs=(vmem_spec(), vmem_spec()),
        compiler_params=pltpu.CompilerParams(vmem_limit_bytes=VMEM_LIMIT),
    )(cols, counts, q, k, v)


def attention_backward(q, k, v, o, do, lse, cols, counts):
    n, width = q.shape
    return pl.pallas_call(
        attn_bwd_kernel,
        out_shape=tuple(jax.ShapeDtypeStruct((n, width), jnp.bfloat16) for _ in range(3)),
        in_specs=[smem_spec(), smem_spec()] + [vmem_spec()] * 6,
        out_specs=(vmem_spec(), vmem_spec(), vmem_spec()),
        scratch_shapes=[pltpu.VMEM((n, width), jnp.float32), pltpu.VMEM((n, width), jnp.float32)],
        compiler_params=pltpu.CompilerParams(vmem_limit_bytes=VMEM_LIMIT),
    )(cols, counts, q, k, v, o, do, lse)


def regroup_columns(moved, seq_count, group_width):
    rows = moved.shape[0]
    return (
        moved.reshape(rows, seq_count, 3, group_width)
        .transpose(0, 2, 1, 3)
        .reshape(rows, 3 * seq_count * group_width)
    )


MESH = pl.DeviceIdType.MESH


def exchange_kernel(
    n,
    m,
    na_ref,
    co_ref,
    g_ref,
    a_ref,
    o_ref,
    oo_ref,
    moved_ref,
    att_ref,
    x_ref,
    recv,
    gath,
    xo_ref,
    recv_o,
    gath_o,
    landed,
    att_landed,
    sems,
    a2a_sems,
):
    me = lax.axis_index("dp")
    here = lax.axis_index("seq")
    barrier = pltpu.get_barrier_semaphore()
    for k in range(1, n):
        pl.semaphore_signal(
            barrier, inc=1, device_id={"dp": lax.rem(me + k, n)}, device_id_type=MESH
        )
    for k in range(1, m):
        pl.semaphore_signal(
            barrier, inc=1, device_id={"seq": lax.rem(here + k, m)}, device_id_type=MESH
        )
    pl.semaphore_wait(barrier, n - 1 + m - 1)

    def start_all(src_of, dst, send, arrive, axis, at, size):
        started = []
        for k in range(1, size):
            peer = lax.rem(at + k, size)
            copy = pltpu.make_async_remote_copy(
                src_ref=src_of(peer),
                dst_ref=dst.at[at],
                send_sem=send.at[peer],
                recv_sem=arrive.at[at],
                device_id={axis: peer},
                device_id_type=MESH,
            )
            copy.start()
            started.append(copy)
        return started

    def finish_all(started, src_of, dst, send, arrive, axis, at, size):
        for k in range(1, size):
            source = lax.rem(at + size - k, size)
            pltpu.make_async_remote_copy(
                src_ref=src_of(source),
                dst_ref=dst.at[source],
                send_sem=send.at[source],
                recv_sem=arrive.at[source],
                device_id={axis: source},
                device_id_type=MESH,
            ).wait_recv()
        for copy in started:
            copy.wait_send()

    parts = g_ref.shape[2] // BLK
    group = BLK * m

    def part_copy(t, peer, sender, target):
        return pltpu.make_async_remote_copy(
            src_ref=g_ref.at[peer, :, pl.ds(t * BLK, BLK)],
            dst_ref=landed.at[:, pl.ds(pl.multiple_of(t * group + sender * BLK, BLK), BLK)],
            send_sem=a2a_sems.at[0, t, peer],
            recv_sem=a2a_sems.at[1, t, sender],
            device_id={"seq": target},
            device_id_type=MESH,
        )

    width = a_ref.shape[2]

    def att_copy(peer, sender, target):
        return pltpu.make_async_remote_copy(
            src_ref=a_ref.at[peer],
            dst_ref=att_landed.at[:, pl.ds(pl.multiple_of(sender * width, width), width)],
            send_sem=a2a_sems.at[0, parts, peer],
            recv_sem=a2a_sems.at[1, parts, sender],
            device_id={"seq": target},
            device_id_type=MESH,
        )

    a2a_started = []
    for k in range(1, m):
        peer = lax.rem(here + k, m)
        copy = att_copy(peer, here, peer)
        copy.start()
        a2a_started.append(copy)
    for k in range(1, m):
        peer = lax.rem(here + k, m)
        for t in range(parts):
            copy = part_copy(t, peer, here, peer)
            copy.start()
            a2a_started.append(copy)
    cshare = a_ref.shape[1]
    term_out = tn_dot(a_ref[0], co_ref[0:cshare, :])
    for c in range(1, m):
        term_out = term_out + tn_dot(a_ref[c], co_ref[c * cshare : (c + 1) * cshare, :])
    xo_ref[...] = term_out.reshape(xo_ref.shape)
    rs_o = (lambda peer: xo_ref.at[peer], recv_o, sems.at[4], sems.at[5], "dp", me, n)
    rs_o_started = start_all(*rs_o)
    share = g_ref.shape[1]
    qkv = tn_dot(na_ref[0:share, :], g_ref[0])
    for c in range(1, m):
        qkv = qkv + tn_dot(na_ref[c * share : (c + 1) * share, :], g_ref[c])
    x_ref[...] = qkv.reshape(x_ref.shape)
    rs = (lambda peer: x_ref.at[peer], recv, sems.at[0], sems.at[1], "dp", me, n)
    rs_started = start_all(*rs)
    finish_all(rs_started, *rs)
    finish_all(rs_o_started, *rs_o)
    total = x_ref[me]
    total_o = xo_ref[me]
    for k in range(1, n):
        total = total + recv[lax.rem(me + k, n)]
        total_o = total_o + recv_o[lax.rem(me + k, n)]
    gath[me] = total.astype(gath.dtype)
    gath_o[me] = total_o.astype(gath_o.dtype)
    ag = (lambda peer: gath.at[me], gath, sems.at[2], sems.at[3], "dp", me, n)
    ag_o = (lambda peer: gath_o.at[me], gath_o, sems.at[6], sems.at[7], "dp", me, n)
    ag_started = start_all(*ag)
    ag_o_started = start_all(*ag_o)
    finish_all(ag_started, *ag)
    finish_all(ag_o_started, *ag_o)
    o_ref[...] = gath[...]
    oo_ref[...] = gath_o[...]
    own = g_ref[here]
    for t in range(parts):
        landed[:, pl.ds(pl.multiple_of(t * group + here * BLK, BLK), BLK)] = own[
            :, t * BLK : (t + 1) * BLK
        ]
    att_landed[:, pl.ds(pl.multiple_of(here * width, width), width)] = a_ref[here]
    for k in range(1, m):
        source = lax.rem(here + m - k, m)
        att_copy(source, source, source).wait_recv()
        for t in range(parts):
            part_copy(t, source, source, source).wait_recv()
    for copy in a2a_started:
        copy.wait_send()
    moved_ref[...] = landed[...]
    att_ref[...] = att_landed[...]


def sum_and_exchange(normed_all, cotan_all, grads, attended_heads):
    n = lax.axis_size("dp")
    m = lax.axis_size("seq")
    rows = normed_all.shape[1]
    qkv_cols = grads.shape[1]
    out_rows, out_cols = attended_heads.shape[1], cotan_all.shape[1]
    chunk_shape = (n, rows // n, qkv_cols)
    out_chunks = (n, out_rows // n, out_cols)
    pieces = grads.reshape(m, grads.shape[0] // m, grads.shape[1])
    att_pieces = attended_heads.reshape(m, attended_heads.shape[0] // m, attended_heads.shape[1])
    parts = grads.shape[1] // BLK
    final = (pieces.shape[1], parts * m * BLK)
    att_final = (att_pieces.shape[1], m * att_pieces.shape[2])
    out, out_o, moved, attended = pl.pallas_call(
        functools.partial(exchange_kernel, n, m),
        out_shape=(
            jax.ShapeDtypeStruct(chunk_shape, jnp.bfloat16),
            jax.ShapeDtypeStruct(out_chunks, jnp.bfloat16),
            jax.ShapeDtypeStruct(final, pieces.dtype),
            jax.ShapeDtypeStruct(att_final, att_pieces.dtype),
        ),
        in_specs=[vmem_spec(), vmem_spec(), vmem_spec(), vmem_spec()],
        out_specs=(vmem_spec(), vmem_spec(), vmem_spec(), vmem_spec()),
        scratch_shapes=[
            pltpu.VMEM(chunk_shape, jnp.float32),
            pltpu.VMEM(chunk_shape, jnp.float32),
            pltpu.VMEM(chunk_shape, jnp.bfloat16),
            pltpu.VMEM(out_chunks, jnp.float32),
            pltpu.VMEM(out_chunks, jnp.float32),
            pltpu.VMEM(out_chunks, jnp.bfloat16),
            pltpu.VMEM(final, pieces.dtype),
            pltpu.VMEM(att_final, att_pieces.dtype),
            pltpu.SemaphoreType.DMA((8, n)),
            pltpu.SemaphoreType.DMA((2, parts + 1, m)),
        ],
        compiler_params=pltpu.CompilerParams(
            collective_id=0, has_side_effects=True, vmem_limit_bytes=VMEM_LIMIT
        ),
    )(normed_all, cotan_all, pieces, att_pieces)
    return out.reshape(rows, qkv_cols), out_o.reshape(out_rows, out_cols), moved, attended


def body(feats, gain, w_qkv, w_out, block_cols, block_counts, cotan):
    model_width = feats.shape[1]
    seq_count = lax.axis_size("seq")
    group_width = model_width // seq_count
    seq_at = lax.axis_index("seq")
    scaled, inverse, normed = layer_norm(feats, gain)
    normed_all = lax.all_gather(normed, "seq", axis=0, tiled=True)
    cotan_all = lax.all_gather(cotan, "seq", axis=0, tiled=True)
    w_heads = jnp.concatenate(
        [
            lax.dynamic_slice_in_dim(w_qkv, j * model_width + seq_at * group_width, group_width, 1)
            for j in range(3)
        ],
        axis=1,
    )
    mixed_heads = jnp.dot(normed_all, w_heads, preferred_element_type=jnp.float32).astype(
        jnp.bfloat16
    )
    query_heads = mixed_heads[:, :group_width]
    key_heads = mixed_heads[:, group_width : 2 * group_width]
    value_heads = mixed_heads[:, 2 * group_width :]
    cols = block_cols[0].reshape(-1)
    counts = block_counts[0]
    attended_heads, lse = attention_forward(query_heads, key_heads, value_heads, cols, counts)
    w_out_rows = lax.dynamic_slice_in_dim(w_out, seq_at * group_width, group_width, 0)
    grad_heads = lax.dot_general(
        cotan_all, w_out_rows, (((1,), (1,)), ((), ())), preferred_element_type=jnp.float32
    ).astype(jnp.bfloat16)
    query_grad, key_grad, value_grad = attention_backward(
        query_heads, key_heads, value_heads, attended_heads, grad_heads, lse, cols, counts
    )
    grad_heads_mixed = jnp.concatenate([query_grad, key_grad, value_grad], axis=1)
    term_qkv, grad_out, moved_grads, attended = sum_and_exchange(
        normed_all, cotan_all, grad_heads_mixed, attended_heads
    )
    result = (
        feats.astype(jnp.float32) + jnp.dot(attended, w_out, preferred_element_type=jnp.float32)
    ).astype(jnp.bfloat16)
    grad_mixed = moved_grads
    grad_normed = lax.dot_general(
        grad_mixed, w_qkv, (((1,), (1,)), ((), ())), preferred_element_type=jnp.float32
    )
    gained = grad_normed * gain[None, :]
    mean_one = jnp.mean(gained, axis=1, keepdims=True)
    mean_two = jnp.mean(gained * scaled, axis=1, keepdims=True)
    grad_feats = (
        cotan.astype(jnp.float32) + inverse * (gained - mean_one - scaled * mean_two)
    ).astype(jnp.bfloat16)
    grad_qkv = regroup_columns(
        lax.all_to_all(term_qkv, "seq", split_axis=0, concat_axis=1, tiled=True),
        seq_count,
        group_width,
    )
    return (result, grad_feats, grad_qkv, grad_out)


def solution(mesh):
    in_specs = (
        P(("dp", "seq"), None),
        P(),
        P(),
        P(),
        P("dp", None, None),
        P("dp", None),
        P(("dp", "seq"), None),
    )
    out_specs = (P(("dp", "seq"), None), P(("dp", "seq"), None), P("seq", None), P("seq", None))
    return jax.shard_map(body, mesh=mesh, in_specs=in_specs, out_specs=out_specs, check_vma=False)
```

```python
import functools

import jax
import jax.numpy as jnp
from jax import lax
from jax.experimental import pallas as pl
from jax.experimental.pallas import tpu as pltpu
from jax.sharding import PartitionSpec as P

HD = 64
BLK = 128
MAXB = 8
SCALE = HD ** (-0.5)
NEG = -1e30

EPSILON = 1e-05


def layer_norm(feats, gain):
    values_f = feats.astype(jnp.float32)
    centred = values_f - jnp.mean(values_f, axis=1, keepdims=True)
    inverse = lax.rsqrt(jnp.mean(centred * centred, axis=1, keepdims=True) + EPSILON)
    scaled = centred * inverse
    return (scaled, inverse, (scaled * gain[None, :]).astype(jnp.bfloat16))


def contract_rows(left_cols, right_cols):
    return lax.dot_general(
        left_cols, right_cols, (((0,), (0,)), ((), ())), preferred_element_type=jnp.float32
    )


def head_masks(width):
    lane = lax.broadcasted_iota(jnp.int32, (1, width), 1)
    return [(lane >= h * HD) & (lane < (h + 1) * HD) for h in range(width // HD)]


def stack_heads(x, masks):
    return jnp.concatenate([jnp.where(m, x, jnp.zeros_like(x)) for m in masks], axis=0)


def unstack_heads(y, masks):
    out = y[0:BLK]
    for h in range(1, len(masks)):
        out = jnp.where(masks[h], y[h * BLK : (h + 1) * BLK], out)
    return out


def nt_dot(a, b):
    return lax.dot_general(a, b, (((1,), (1,)), ((), ())), preferred_element_type=jnp.float32)


def tn_dot(a, b):
    return lax.dot_general(a, b, (((0,), (0,)), ((), ())), preferred_element_type=jnp.float32)


SLOT_TIERS = (2, 4, MAXB)


def gather_blocks(ref, cols_ref, r, slots):
    return jnp.concatenate(
        [
            ref[pl.ds(pl.multiple_of(cols_ref[r * MAXB + s] * BLK, BLK), BLK), :]
            for s in range(slots)
        ],
        axis=0,
    )


def live_lanes(cnt, slots):
    return lax.broadcasted_iota(jnp.int32, (1, slots * BLK), 1) < cnt * BLK


FINE_TIERS = (1, 2, 3, 4, 6, MAXB)


def by_tier(cnt, body, tiers=SLOT_TIERS):
    low = 0
    for slots in tiers:
        pl.when((cnt > low) & (cnt <= slots))(functools.partial(body, slots))
        low = slots


def attn_fwd_kernel(cols_ref, counts_ref, q_ref, k_ref, v_ref, o_ref, lse_ref):
    width = q_ref.shape[1]
    nblk = q_ref.shape[0] // BLK
    masks = head_masks(width)
    rows = len(masks) * BLK

    def row_body(r, carry):
        row0 = pl.multiple_of(r * BLK, BLK)
        cnt = counts_ref[r]

        def tier(slots):
            live = live_lanes(cnt, slots)
            q2 = stack_heads(q_ref[pl.ds(row0, BLK), :], masks)
            kc = gather_blocks(k_ref, cols_ref, r, slots)
            sc = jnp.where(live, nt_dot(q2, kc) * SCALE, NEG)
            m = jnp.max(sc, axis=1, keepdims=True)
            e = jnp.where(live, jnp.exp(sc - m), 0.0)
            l = jnp.sum(e, axis=1, keepdims=True)
            p = (e * (1.0 / l)).astype(jnp.bfloat16)
            vc = gather_blocks(v_ref, cols_ref, r, slots)
            acc = jnp.dot(p, vc, preferred_element_type=jnp.float32)
            o_ref[pl.ds(row0, BLK), :] = unstack_heads(acc, masks).astype(o_ref.dtype)
            lse_ref[pl.ds(pl.multiple_of(r * rows, rows), rows), :] = jnp.broadcast_to(
                m + jnp.log(l), (rows, lse_ref.shape[1])
            )

        by_tier(cnt, tier)
        return carry

    lax.fori_loop(0, nblk, row_body, 0)


def attn_bwd_kernel(
    cols_ref, counts_ref, q_ref, k_ref, v_ref, o_ref, do_ref, lse_ref, dq_ref, dk_ref, dv_ref, dk_acc, dv_acc
):
    width = q_ref.shape[1]
    nblk = q_ref.shape[0] // BLK
    masks = head_masks(width)
    rows = len(masks) * BLK
    dk_acc[...] = jnp.zeros_like(dk_acc)
    dv_acc[...] = jnp.zeros_like(dv_acc)

    def row_body(r, carry):
        row0 = pl.multiple_of(r * BLK, BLK)
        cnt = counts_ref[r]

        def tier(slots):
            live = live_lanes(cnt, slots)
            q2 = stack_heads(q_ref[pl.ds(row0, BLK), :], masks)
            do_blk = do_ref[pl.ds(row0, BLK), :]
            do2 = stack_heads(do_blk, masks)
            prod = o_ref[pl.ds(row0, BLK), :].astype(jnp.float32) * do_blk.astype(jnp.float32)
            delta = jnp.concatenate(
                [jnp.sum(jnp.where(m, prod, 0.0), axis=1, keepdims=True) for m in masks], axis=0
            )
            lse = lse_ref[pl.ds(pl.multiple_of(r * rows, rows), rows), :][:, 0:1]
            kc = gather_blocks(k_ref, cols_ref, r, slots)
            vc = gather_blocks(v_ref, cols_ref, r, slots)
            sc = nt_dot(q2, kc) * SCALE
            p = jnp.where(live, jnp.exp(sc - lse), 0.0).astype(jnp.bfloat16)
            dp = nt_dot(do2, vc)
            ds = (p.astype(jnp.float32) * (dp - delta) * SCALE).astype(jnp.bfloat16)
            dq = jnp.dot(ds, kc, preferred_element_type=jnp.float32)
            dq_ref[pl.ds(row0, BLK), :] = unstack_heads(dq, masks).astype(dq_ref.dtype)
            dkc = tn_dot(ds, q2)
            dvc = tn_dot(p, do2)
            for s in range(slots):

                @pl.when(s < cnt)
                def _():
                    col0 = pl.multiple_of(cols_ref[r * MAXB + s] * BLK, BLK)
                    dk_acc[pl.ds(col0, BLK), :] += dkc[s * BLK : (s + 1) * BLK]
                    dv_acc[pl.ds(col0, BLK), :] += dvc[s * BLK : (s + 1) * BLK]

        by_tier(cnt, tier, FINE_TIERS)
        return carry

    lax.fori_loop(0, nblk, row_body, 0)
    dk_ref[...] = dk_acc[...].astype(dk_ref.dtype)
    dv_ref[...] = dv_acc[...].astype(dv_ref.dtype)


def smem_spec():
    return pl.BlockSpec(memory_space=pltpu.SMEM)


def vmem_spec():
    return pl.BlockSpec(memory_space=pltpu.VMEM)


VMEM_LIMIT = 48 * 1024 * 1024


def attention_forward(q, k, v, cols, counts):
    n, width = q.shape
    rows = (width // HD) * BLK
    return pl.pallas_call(
        attn_fwd_kernel,
        out_shape=(
            jax.ShapeDtypeStruct((n, width), jnp.bfloat16),
            jax.ShapeDtypeStruct(((n // BLK) * rows, 128), jnp.float32),
        ),
        in_specs=[smem_spec(), smem_spec(), vmem_spec(), vmem_spec(), vmem_spec()],
        out_specs=(vmem_spec(), vmem_spec()),
        compiler_params=pltpu.CompilerParams(vmem_limit_bytes=VMEM_LIMIT),
    )(cols, counts, q, k, v)


def attention_backward(q, k, v, o, do, lse, cols, counts):
    n, width = q.shape
    return pl.pallas_call(
        attn_bwd_kernel,
        out_shape=tuple(jax.ShapeDtypeStruct((n, width), jnp.bfloat16) for _ in range(3)),
        in_specs=[smem_spec(), smem_spec()] + [vmem_spec()] * 6,
        out_specs=(vmem_spec(), vmem_spec(), vmem_spec()),
        scratch_shapes=[pltpu.VMEM((n, width), jnp.float32), pltpu.VMEM((n, width), jnp.float32)],
        compiler_params=pltpu.CompilerParams(vmem_limit_bytes=VMEM_LIMIT),
    )(cols, counts, q, k, v, o, do, lse)


def regroup_columns(moved, seq_count, group_width):
    rows = moved.shape[0]
    return (
        moved.reshape(rows, seq_count, 3, group_width)
        .transpose(0, 2, 1, 3)
        .reshape(rows, 3 * seq_count * group_width)
    )


MESH = pl.DeviceIdType.MESH


def exchange_kernel(
    n,
    m,
    na_ref,
    co_ref,
    g_ref,
    a_ref,
    o_ref,
    oo_ref,
    moved_ref,
    att_ref,
    x_ref,
    recv,
    gath,
    xo_ref,
    recv_o,
    gath_o,
    landed,
    att_landed,
    sems,
    a2a_sems,
):
    me = lax.axis_index("dp")
    here = lax.axis_index("seq")
    barrier = pltpu.get_barrier_semaphore()
    for k in range(1, n):
        pl.semaphore_signal(
            barrier, inc=1, device_id={"dp": lax.rem(me + k, n)}, device_id_type=MESH
        )
    for k in range(1, m):
        pl.semaphore_signal(
            barrier, inc=1, device_id={"seq": lax.rem(here + k, m)}, device_id_type=MESH
        )
    pl.semaphore_wait(barrier, n - 1 + m - 1)

    def start_all(src_of, dst, send, arrive, axis, at, size):
        started = []
        for k in range(1, size):
            peer = lax.rem(at + k, size)
            copy = pltpu.make_async_remote_copy(
                src_ref=src_of(peer),
                dst_ref=dst.at[at],
                send_sem=send.at[peer],
                recv_sem=arrive.at[at],
                device_id={axis: peer},
                device_id_type=MESH,
            )
            copy.start()
            started.append(copy)
        return started

    def finish_all(started, src_of, dst, send, arrive, axis, at, size):
        for k in range(1, size):
            source = lax.rem(at + size - k, size)
            pltpu.make_async_remote_copy(
                src_ref=src_of(source),
                dst_ref=dst.at[source],
                send_sem=send.at[source],
                recv_sem=arrive.at[source],
                device_id={axis: source},
                device_id_type=MESH,
            ).wait_recv()
        for copy in started:
            copy.wait_send()

    parts = g_ref.shape[2] // BLK
    group = BLK * m

    def part_copy(t, peer, sender, target):
        return pltpu.make_async_remote_copy(
            src_ref=g_ref.at[peer, :, pl.ds(t * BLK, BLK)],
            dst_ref=landed.at[:, pl.ds(pl.multiple_of(t * group + sender * BLK, BLK), BLK)],
            send_sem=a2a_sems.at[0, t, peer],
            recv_sem=a2a_sems.at[1, t, sender],
            device_id={"seq": target},
            device_id_type=MESH,
        )

    width = a_ref.shape[2]

    def att_copy(peer, sender, target):
        return pltpu.make_async_remote_copy(
            src_ref=a_ref.at[peer],
            dst_ref=att_landed.at[:, pl.ds(pl.multiple_of(sender * width, width), width)],
            send_sem=a2a_sems.at[0, parts, peer],
            recv_sem=a2a_sems.at[1, parts, sender],
            device_id={"seq": target},
            device_id_type=MESH,
        )

    a2a_started = []
    for k in range(1, m):
        peer = lax.rem(here + k, m)
        copy = att_copy(peer, here, peer)
        copy.start()
        a2a_started.append(copy)
    for k in range(1, m):
        peer = lax.rem(here + k, m)
        for t in range(parts):
            copy = part_copy(t, peer, here, peer)
            copy.start()
            a2a_started.append(copy)
    cshare = a_ref.shape[1]
    term_out = tn_dot(a_ref[0], co_ref[0:cshare, :])
    for c in range(1, m):
        term_out = term_out + tn_dot(a_ref[c], co_ref[c * cshare : (c + 1) * cshare, :])
    xo_ref[...] = term_out.reshape(xo_ref.shape)
    rs_o = (lambda peer: xo_ref.at[peer], recv_o, sems.at[4], sems.at[5], "dp", me, n)
    rs_o_started = start_all(*rs_o)
    share = g_ref.shape[1]
    qkv = tn_dot(na_ref[0:share, :], g_ref[0])
    for c in range(1, m):
        qkv = qkv + tn_dot(na_ref[c * share : (c + 1) * share, :], g_ref[c])
    x_ref[...] = qkv.reshape(x_ref.shape)
    rs = (lambda peer: x_ref.at[peer], recv, sems.at[0], sems.at[1], "dp", me, n)
    rs_started = start_all(*rs)
    finish_all(rs_o_started, *rs_o)
    total_o = xo_ref[me]
    for k in range(1, n):
        total_o = total_o + recv_o[lax.rem(me + k, n)]
    gath_o[me] = total_o.astype(gath_o.dtype)
    ag_o = (lambda peer: gath_o.at[me], gath_o, sems.at[6], sems.at[7], "dp", me, n)
    ag_o_started = start_all(*ag_o)
    finish_all(rs_started, *rs)
    total = x_ref[me]
    for k in range(1, n):
        total = total + recv[lax.rem(me + k, n)]
    gath[me] = total.astype(gath.dtype)
    ag = (lambda peer: gath.at[me], gath, sems.at[2], sems.at[3], "dp", me, n)
    ag_started = start_all(*ag)
    finish_all(ag_o_started, *ag_o)
    finish_all(ag_started, *ag)
    o_ref[...] = gath[...]
    oo_ref[...] = gath_o[...]
    own = g_ref[here]
    for t in range(parts):
        landed[:, pl.ds(pl.multiple_of(t * group + here * BLK, BLK), BLK)] = own[
            :, t * BLK : (t + 1) * BLK
        ]
    att_landed[:, pl.ds(pl.multiple_of(here * width, width), width)] = a_ref[here]
    for k in range(1, m):
        source = lax.rem(here + m - k, m)
        att_copy(source, source, source).wait_recv()
        for t in range(parts):
            part_copy(t, source, source, source).wait_recv()
    for copy in a2a_started:
        copy.wait_send()
    moved_ref[...] = landed[...]
    att_ref[...] = att_landed[...]


def sum_and_exchange(normed_all, cotan_all, grads, attended_heads):
    n = lax.axis_size("dp")
    m = lax.axis_size("seq")
    rows = normed_all.shape[1]
    qkv_cols = grads.shape[1]
    out_rows, out_cols = attended_heads.shape[1], cotan_all.shape[1]
    chunk_shape = (n, rows // n, qkv_cols)
    out_chunks = (n, out_rows // n, out_cols)
    pieces = grads.reshape(m, grads.shape[0] // m, grads.shape[1])
    att_pieces = attended_heads.reshape(m, attended_heads.shape[0] // m, attended_heads.shape[1])
    parts = grads.shape[1] // BLK
    final = (pieces.shape[1], parts * m * BLK)
    att_final = (att_pieces.shape[1], m * att_pieces.shape[2])
    out, out_o, moved, attended = pl.pallas_call(
        functools.partial(exchange_kernel, n, m),
        out_shape=(
            jax.ShapeDtypeStruct(chunk_shape, jnp.bfloat16),
            jax.ShapeDtypeStruct(out_chunks, jnp.bfloat16),
            jax.ShapeDtypeStruct(final, pieces.dtype),
            jax.ShapeDtypeStruct(att_final, att_pieces.dtype),
        ),
        in_specs=[vmem_spec(), vmem_spec(), vmem_spec(), vmem_spec()],
        out_specs=(vmem_spec(), vmem_spec(), vmem_spec(), vmem_spec()),
        scratch_shapes=[
            pltpu.VMEM(chunk_shape, jnp.float32),
            pltpu.VMEM(chunk_shape, jnp.float32),
            pltpu.VMEM(chunk_shape, jnp.bfloat16),
            pltpu.VMEM(out_chunks, jnp.float32),
            pltpu.VMEM(out_chunks, jnp.float32),
            pltpu.VMEM(out_chunks, jnp.bfloat16),
            pltpu.VMEM(final, pieces.dtype),
            pltpu.VMEM(att_final, att_pieces.dtype),
            pltpu.SemaphoreType.DMA((8, n)),
            pltpu.SemaphoreType.DMA((2, parts + 1, m)),
        ],
        compiler_params=pltpu.CompilerParams(
            collective_id=0, has_side_effects=True, vmem_limit_bytes=VMEM_LIMIT
        ),
    )(normed_all, cotan_all, pieces, att_pieces)
    return out.reshape(rows, qkv_cols), out_o.reshape(out_rows, out_cols), moved, attended


def body(feats, gain, w_qkv, w_out, block_cols, block_counts, cotan):
    model_width = feats.shape[1]
    seq_count = lax.axis_size("seq")
    group_width = model_width // seq_count
    seq_at = lax.axis_index("seq")
    scaled, inverse, normed = layer_norm(feats, gain)
    normed_all = lax.all_gather(normed, "seq", axis=0, tiled=True)
    cotan_all = lax.all_gather(cotan, "seq", axis=0, tiled=True)
    w_heads = jnp.concatenate(
        [
            lax.dynamic_slice_in_dim(w_qkv, j * model_width + seq_at * group_width, group_width, 1)
            for j in range(3)
        ],
        axis=1,
    )
    mixed_heads = jnp.dot(normed_all, w_heads, preferred_element_type=jnp.float32).astype(
        jnp.bfloat16
    )
    query_heads = mixed_heads[:, :group_width]
    key_heads = mixed_heads[:, group_width : 2 * group_width]
    value_heads = mixed_heads[:, 2 * group_width :]
    cols = block_cols[0].reshape(-1)
    counts = block_counts[0]
    attended_heads, lse = attention_forward(query_heads, key_heads, value_heads, cols, counts)
    w_out_rows = lax.dynamic_slice_in_dim(w_out, seq_at * group_width, group_width, 0)
    grad_heads = lax.dot_general(
        cotan_all, w_out_rows, (((1,), (1,)), ((), ())), preferred_element_type=jnp.float32
    ).astype(jnp.bfloat16)
    query_grad, key_grad, value_grad = attention_backward(
        query_heads, key_heads, value_heads, attended_heads, grad_heads, lse, cols, counts
    )
    grad_heads_mixed = jnp.concatenate([query_grad, key_grad, value_grad], axis=1)
    term_qkv, grad_out, moved_grads, attended = sum_and_exchange(
        normed_all, cotan_all, grad_heads_mixed, attended_heads
    )
    result = (
        feats.astype(jnp.float32) + jnp.dot(attended, w_out, preferred_element_type=jnp.float32)
    ).astype(jnp.bfloat16)
    grad_mixed = moved_grads
    grad_normed = lax.dot_general(
        grad_mixed, w_qkv, (((1,), (1,)), ((), ())), preferred_element_type=jnp.float32
    )
    gained = grad_normed * gain[None, :]
    mean_one = jnp.mean(gained, axis=1, keepdims=True)
    mean_two = jnp.mean(gained * scaled, axis=1, keepdims=True)
    grad_feats = (
        cotan.astype(jnp.float32) + inverse * (gained - mean_one - scaled * mean_two)
    ).astype(jnp.bfloat16)
    grad_qkv = regroup_columns(
        lax.all_to_all(term_qkv, "seq", split_axis=0, concat_axis=1, tiled=True),
        seq_count,
        group_width,
    )
    return (result, grad_feats, grad_qkv, grad_out)


def solution(mesh):
    in_specs = (
        P(("dp", "seq"), None),
        P(),
        P(),
        P(),
        P("dp", None, None),
        P("dp", None),
        P(("dp", "seq"), None),
    )
    out_specs = (P(("dp", "seq"), None), P(("dp", "seq"), None), P("seq", None), P("seq", None))
    return jax.shard_map(body, mesh=mesh, in_specs=in_specs, out_specs=out_specs, check_vma=False)
```
